32 devices in a mesh: band: 4 (over y, core), seq: 8 (over z, x).
Axes of the slice: x: 2, y: 2, z: 4, core: 2. Of those that a mesh axis runs over, the one named last changes fastest.
Arguments:
- frames: bfloat16 [4, 1024, 768], P('band', 'seq'), may hold values from -6 to 6
- text: bfloat16 [4, 128, 768], P('band'), may hold values from -6 to 6
- timesteps: int32 [4], P('band'), may hold values from 0 to 999
- frame_lengths: int32 [4], P('band'), may hold values from 128 to 1024, as said below
- text_mask: int32 [4, 128], P('band'), may hold values from 0 to 1, as said below
- cotangent: bfloat16 [4, 1024, 768], P('band', 'seq'), may hold values from -6 to 6
- w_time_in: bfloat16 [256, 768], replicated, may hold values from -0.5 to 0.5
- w_time_out: bfloat16 [768, 768], replicated, may hold values from -0.3125 to 0.3125
- w_adaln: bfloat16 [768, 4608], replicated, may hold values from -0.4375 to 0.4375
- w_query: bfloat16 [768, 768], replicated, may hold values from -0.21875 to 0.21875
- w_key: bfloat16 [768, 768], replicated, may hold values from -0.21875 to 0.21875
- w_value: bfloat16 [768, 768], replicated, may hold values from -0.21875 to 0.21875
- w_attn_out: bfloat16 [768, 768], replicated, may hold values from -4 to 4
- cross_gain: bfloat16 [768], replicated, may hold values from 0.25 to 1.75
- w_cross_query: bfloat16 [768, 768], replicated, may hold values from -0.21875 to 0.21875
- w_cross_key: bfloat16 [768, 768], replicated, may hold values from -0.21875 to 0.21875
- w_cross_value: bfloat16 [768, 768], replicated, may hold values from -0.21875 to 0.21875
- w_cross_out: bfloat16 [768, 768], replicated, may hold values from -1 to 1
- w_mlp_in: bfloat16 [768, 3072], replicated, may hold values from -0.21875 to 0.21875
- w_mlp_out: bfloat16 [3072, 768], replicated, may hold values from -0.109375 to 0.109375
Outputs:
- block_out: bfloat16 [4, 1024, 768], P('band', 'seq')
- grad_frames: bfloat16 [4, 1024, 768], P('band', 'seq')
- grad_text: float32 [4, 128, 768], P('band', 'seq')
- grad_w_time_in: float32 [256, 768], P(None, 'seq')
- grad_w_time_out: float32 [768, 768], P(None, 'seq')
- grad_w_adaln: float32 [768, 4608], P(None, 'seq')
- grad_w_query: float32 [768, 768], P(None, 'seq')
- grad_w_key: float32 [768, 768], P(None, 'seq')
- grad_w_value: float32 [768, 768], P(None, 'seq')
- grad_w_attn_out: float32 [768, 768], P(None, 'seq')
- grad_cross_gain: float32 [768], P('seq')
- grad_w_cross_query: float32 [768, 768], P(None, 'seq')
- grad_w_cross_key: float32 [768, 768], P(None, 'seq')
- grad_w_cross_value: float32 [768, 768], P(None, 'seq')
- grad_w_cross_out: float32 [768, 768], P(None, 'seq')
- grad_w_mlp_in: float32 [768, 3072], P(None, 'seq')
- grad_w_mlp_out: float32 [3072, 768], P(None, 'seq')
The draws below stay inside these ranges and needn't reach their ends.
Inputs may be any that keep to these rules, and one draw needn't show every extreme that they name: `frame_lengths`: in every draw some clip has all 1024 frames valid. `text_mask`: the first text token of every clip is real.
All inputs are finite; a program needn't handle non-finite values.
Results may differ from the reference program's by a relative error of at most 0.029.
Values may be sent and summed in bfloat16 or wider, within the bound.
A program may use at most 256 MiB of HBM per device.

```python
import math
import jax
import jax.numpy as jnp
from jax import lax

D = 768
H = 12
HD = 64
FF = 3072
FREQ = 256
TXT = 128
CLIP = 1024
ITEMS = 4


def draw_frame_lengths(key, part):
    lengths = jax.random.randint(jax.random.fold_in(key, 11), (ITEMS,), CLIP // 8, CLIP + 1, dtype=jnp.int32)
    chosen = jax.random.randint(jax.random.fold_in(key, 12), (), 0, ITEMS, dtype=jnp.int32)
    return jnp.where(jnp.arange(ITEMS) == chosen, CLIP, lengths).astype(jnp.int32)


def draw_text_mask(key, part):
    levels = jax.random.randint(jax.random.fold_in(key, 13), (ITEMS, TXT), 0, 4, dtype=jnp.int32)
    marks = jnp.minimum(levels, 1)
    return jnp.where(jnp.arange(TXT)[None, :] == 0, 1, marks).astype(jnp.int32)


def plant(drawn, own_key, smallest, largest):
    shape = drawn.shape
    index_at = [jax.random.randint(jax.random.fold_in(own_key, axis), (), 0, shape[axis]) for axis in range(len(shape))]
    drawn = drawn.at[tuple(index_at)].set(smallest)
    longest = shape.index(max(shape))
    index_at[longest] = (index_at[longest] + 1) % shape[longest]
    return drawn.at[tuple(index_at)].set(largest)


def steps_of(own_key, shape, shards, smallest, high):
    gain, own = 1.0, jax.random.fold_in(own_key, 6)
    for axis_at, parts in shards:
        draws = jnp.exp(jax.random.uniform(jax.random.fold_in(own, axis_at), (parts,), jnp.float32, smallest / len(shards), high / len(shards)))
        gain = gain * jnp.repeat(draws, shape[axis_at] // parts).reshape([-1 if axis == axis_at else 1 for axis in range(len(shape))])
    return gain


def gaussian(stream_key, dims, scale, most, cuts=(), kind=jnp.bfloat16):
    level = steps_of(stream_key, dims, cuts, -0.22, 0.18) if cuts else 1.0
    values = jax.random.normal(stream_key, dims, jnp.float32) * scale * level
    return jnp.minimum(jnp.maximum(values, -most), most).astype(kind)


def setup_inputs(seed: int = 0) -> dict:
    streams_of = jax.random.split(jax.random.key(seed), 21)
    frames = gaussian(streams_of[0], (ITEMS, CLIP, D), 1.0, 6.0, ((0, 4), (1, 8)))
    text = gaussian(streams_of[1], (ITEMS, TXT, D), 1.0, 6.0, ((0, 4),))
    timesteps = plant(jax.random.randint(streams_of[2], (ITEMS,), 0, 1000), jax.random.fold_in(streams_of[2], 1), 0, 999).astype(jnp.int32)
    frame_lengths = draw_frame_lengths(jax.random.fold_in(streams_of[20], 71), 0)
    text_mask = draw_text_mask(jax.random.fold_in(streams_of[20], 71), 0)
    cotangent = gaussian(streams_of[5], (ITEMS, CLIP, D), 1.0, 6.0, ((0, 4), (1, 8)))
    w_time_in = gaussian(streams_of[6], (FREQ, D), (FREQ // 2) ** -0.5, 0.5)
    w_time_out = gaussian(streams_of[7], (D, D), (D // 2) ** -0.5, 0.3125)
    w_adaln = gaussian(streams_of[8], (D, 6 * D), (D // 4) ** -0.5, 0.4375)
    w_query = gaussian(streams_of[9], (D, D), D ** -0.5, 0.21875)
    w_key = gaussian(streams_of[10], (D, D), D ** -0.5, 0.21875)
    w_value = gaussian(streams_of[11], (D, D), D ** -0.5, 0.21875)
    w_attn_out = gaussian(streams_of[12], (D, D), 2 ** -0.5, 4.0)
    cross_gain = jnp.clip(1.0 + 0.15 * jax.random.normal(streams_of[13], (D,), jnp.float32), 0.25, 1.75).astype(jnp.bfloat16)
    w_cross_query = gaussian(streams_of[14], (D, D), D ** -0.5, 0.21875)
    w_cross_key = gaussian(streams_of[15], (D, D), D ** -0.5, 0.21875)
    w_cross_value = gaussian(streams_of[16], (D, D), D ** -0.5, 0.21875)
    w_cross_out = gaussian(streams_of[17], (D, D), 32 ** -0.5, 1.0)
    w_mlp_in = gaussian(streams_of[18], (D, FF), D ** -0.5, 0.21875)
    w_mlp_out = gaussian(streams_of[19], (FF, D), FF ** -0.5, 0.109375)
    return dict(frames=frames, text=text, timesteps=timesteps, frame_lengths=frame_lengths, text_mask=text_mask, cotangent=cotangent, w_time_in=w_time_in, w_time_out=w_time_out, w_adaln=w_adaln, w_query=w_query, w_key=w_key, w_value=w_value, w_attn_out=w_attn_out, cross_gain=cross_gain, w_cross_query=w_cross_query, w_cross_key=w_cross_key, w_cross_value=w_cross_value, w_cross_out=w_cross_out, w_mlp_in=w_mlp_in, w_mlp_out=w_mlp_out)


@jax.custom_vjp
def low(v):
    return lax.optimization_barrier(v.astype(jnp.bfloat16)).astype(jnp.float32)

@jax.custom_vjp
def low_back(v):
    return v

def low_keep(v):
    return (low(v), None)

def low_pass(kept, grad):
    return (grad,)

def back_keep(v):
    return (v, None)

def back_low(kept, grad):
    return (low(grad),)
low.defvjp(low_keep, low_pass)
low_back.defvjp(back_keep, back_low)
epsilon = 1e-06
masked_value = -1000000000.0

def product(left, right):
    return jnp.dot(left, right, precision=lax.Precision.HIGHEST)

def layer_norm(inputs):
    center = inputs - lax.optimization_barrier(jnp.mean(inputs, axis=-1, keepdims=True))
    return center * lax.rsqrt(lax.optimization_barrier(jnp.mean(center * center, axis=-1, keepdims=True)) + epsilon)

def time_embed(timestep, width):
    half_width = width // 2
    frequency = jnp.exp(-math.log(10000.0) * jnp.arange(half_width, dtype=jnp.float32) / half_width)
    angles = timestep.astype(jnp.float32) * frequency
    return jnp.concatenate([jnp.cos(angles), jnp.sin(angles)])[None, :]

def attend(queries, key_rows, value_rows, key_valid):
    scores = low_back(jnp.einsum('qhd,khd->qhk', queries, key_rows, precision=lax.Precision.HIGHEST) * 0.125)
    scores = jnp.where(key_valid[None, None, :], scores, masked_value)
    row_max = lax.optimization_barrier(jnp.max(scores, axis=-1, keepdims=True))
    log_total = row_max + jnp.log(lax.optimization_barrier(jnp.sum(jnp.exp(scores - row_max), axis=-1, keepdims=True)))
    attn_probs = low(jnp.exp(scores - log_total))
    return jnp.einsum('qhk,khd->qhd', attn_probs, value_rows, precision=lax.Precision.HIGHEST)

def forward(frames_item, text_item, weight_values, timestep, length, text_valid):
    w_time_in, w_time_out, w_adaln, w_query, w_key, w_value, w_attn_out, cross_gain, w_cross_query, w_cross_key, w_cross_value, w_cross_out, w_mlp_in, w_mlp_out = weight_values
    time_vector = low(time_embed(timestep, w_time_in.shape[0]))
    time_hidden = low(jax.nn.silu(product(time_vector, w_time_in)))
    time_out = low_back(product(time_hidden, w_time_out))
    condition = low(jax.nn.silu(time_out))
    modulation = low_back(product(condition, w_adaln))
    shift_attn, scale_attn, gate_attn, shift_mlp, scale_mlp, gate_mlp = jnp.split(modulation, 6, axis=1)
    row_count = frames_item.shape[0]
    key_valid = jnp.arange(row_count) < length
    attn_in = low(layer_norm(frames_item) * (1.0 + scale_attn) + shift_attn)
    queries = low(low_back(product(attn_in, w_query))).reshape(row_count, H, HD)
    key_rows = low(low_back(product(attn_in, w_key))).reshape(row_count, H, HD)
    value_rows = low(low_back(product(attn_in, w_value))).reshape(row_count, H, HD)
    block_size = math.gcd(row_count, 1024)

    def one_block(block_queries):
        return jax.checkpoint(attend)(block_queries, key_rows, value_rows, key_valid)
    attended = lax.map(one_block, queries.reshape(row_count // block_size, block_size, H, HD))
    attn_low = low(low_back(attended.reshape(row_count, D)))
    attn_proj = low_back(product(attn_low, w_attn_out))
    middle = frames_item + gate_attn * attn_proj
    cross_in = low(layer_norm(middle) * cross_gain)
    cross_queries = low(low_back(product(cross_in, w_cross_query))).reshape(row_count, H, HD)
    cross_keys = low(low_back(product(text_item, w_cross_key))).reshape(text_item.shape[0], H, HD)
    cross_values = low(low_back(product(text_item, w_cross_value))).reshape(text_item.shape[0], H, HD)
    cross_attended = attend(cross_queries, cross_keys, cross_values, text_valid)
    cross_low = low(low_back(cross_attended.reshape(row_count, D)))
    after_cross = middle + low_back(product(cross_low, w_cross_out))
    mlp_in = low(layer_norm(after_cross) * (1.0 + scale_mlp) + shift_mlp)
    pre_act = low_back(product(mlp_in, w_mlp_in))
    activation = low(jax.nn.gelu(pre_act, approximate=True))
    mlp_out = low_back(product(activation, w_mlp_out))
    result = after_cross + gate_mlp * mlp_out
    return jnp.where(key_valid[:, None], result, frames_item)

def reference(frames, text, timesteps, frame_lengths, text_mask, cotangent, w_time_in, w_time_out, w_adaln, w_query, w_key, w_value, w_attn_out, cross_gain, w_cross_query, w_cross_key, w_cross_value, w_cross_out, w_mlp_in, w_mlp_out):
    weights = tuple((weight.astype(jnp.float32) for weight in (w_time_in, w_time_out, w_adaln, w_query, w_key, w_value, w_attn_out, cross_gain, w_cross_query, w_cross_key, w_cross_value, w_cross_out, w_mlp_in, w_mlp_out)))

    def per_item(running, item):
        frames_item, text_item, timestep, length, mask_item, cotangent_item = item
        text_valid = mask_item != 0

        def closed(frame_values, text_values, *weight_values):
            return forward(frame_values, text_values, weight_values, timestep, length, text_valid)
        outputs, pull_back = jax.vjp(closed, frames_item.astype(jnp.float32), text_item.astype(jnp.float32), *weights)
        gradients = pull_back(cotangent_item.astype(jnp.float32))
        running = tuple((total + extra for total, extra in zip(running, gradients[2:])))
        return (running, (outputs.astype(jnp.bfloat16), gradients[0].astype(jnp.bfloat16), gradients[1]))
    initial = tuple((jnp.zeros(weight.shape, jnp.float32) for weight in weights))
    totals, (block_out, grad_frames, grad_text) = lax.scan(per_item, initial, (frames, text, timesteps, frame_lengths, text_mask, cotangent))
    return (block_out, grad_frames, grad_text) + totals
```

```python
import math

import jax
import jax.numpy as jnp
from jax import lax
from jax.experimental import pallas as pl
from jax.experimental.pallas import tpu as pltpu
from jax.sharding import PartitionSpec as P

H = 12
HD = 64


epsilon = 1e-06
masked_value = -1000000000.0
key_block = 512


def for_sending(value):
    return jax.tree.map(lambda a: a.astype(jnp.bfloat16) if a.dtype == jnp.float32 else a, value)


def narrow(values):
    return values.astype(jnp.bfloat16)


def product(left, right):
    return jnp.dot(left, right, preferred_element_type=jnp.float32)


def transposed_left(left, right):
    return lax.dot_general(
        left, right, (((0,), (0,)), ((), ())), preferred_element_type=jnp.float32
    )


def transposed_right(left, right):
    return lax.dot_general(
        left, right, (((1,), (1,)), ((), ())), preferred_element_type=jnp.float32
    )


def layer_norm(inputs):
    center = inputs - jnp.mean(inputs, axis=-1, keepdims=True)
    scaling = lax.rsqrt(jnp.mean(center * center, axis=-1, keepdims=True) + epsilon)
    return (center * scaling, scaling)


def norm_back(normed, scaling, gradient):
    mean_grad = jnp.mean(gradient, axis=-1, keepdims=True)
    mean_prod = jnp.mean(gradient * normed, axis=-1, keepdims=True)
    return scaling * (gradient - mean_grad - normed * mean_prod)


def time_embed(timesteps, width):
    half_width = width // 2
    frequency = jnp.exp(-math.log(10000.0) * jnp.arange(half_width, dtype=jnp.float32) / half_width)
    angles = timesteps.astype(jnp.float32)[:, None] * frequency[None, :]
    return jnp.concatenate([jnp.cos(angles), jnp.sin(angles)], axis=1)


def split_heads(rows_in):
    return rows_in.reshape(rows_in.shape[0], rows_in.shape[1], H, HD)


def masked_scores(queries, key_rows, key_valid):
    scores = (
        jnp.einsum("cqhd,ckhd->cqhk", queries, key_rows, preferred_element_type=jnp.float32) * 0.125
    )
    return jnp.where(key_valid[:, None, None, :], scores, masked_value)


def block_valid(anchor, start_row, block_size, lengths):
    return (anchor + start_row + jnp.arange(block_size))[None, :] < lengths[:, None]


def forward_piece(running, segment, anchor, queries, lengths):
    row_count = segment.shape[1]
    block_size = math.gcd(row_count, key_block)
    width = queries.shape[2] * queries.shape[3]

    def forward_one_block(running, counter):
        rows_in = lax.dynamic_slice_in_dim(segment, counter * block_size, block_size, 1)
        key_valid = block_valid(anchor, counter * block_size, block_size, lengths)
        scores = masked_scores(queries, split_heads(rows_in[:, :, :width]), key_valid)
        row_max, row_sum, weighted = running
        new_max = jnp.maximum(row_max, jnp.max(scores, axis=-1))
        factor = jnp.exp(row_max - new_max)
        expanded = jnp.exp(scores - new_max[..., None])
        row_sum = row_sum * factor + jnp.sum(expanded, axis=-1)
        weighted = weighted * factor[..., None] + jnp.einsum(
            "cqhk,ckhd->cqhd",
            narrow(expanded),
            split_heads(rows_in[:, :, width:]),
            preferred_element_type=jnp.float32,
        )
        return ((new_max, row_sum, weighted), None)

    running, unused = lax.scan(forward_one_block, running, jnp.arange(row_count // block_size))
    return running


def query_piece(gradient, segment, anchor, queries, grad_heads, log_total, row_delta, lengths):
    row_count = segment.shape[1]
    block_size = math.gcd(row_count, key_block)
    width = queries.shape[2] * queries.shape[3]

    def query_one_block(gradient, counter):
        rows_in = lax.dynamic_slice_in_dim(segment, counter * block_size, block_size, 1)
        key_valid = block_valid(anchor, counter * block_size, block_size, lengths)
        key_rows = split_heads(rows_in[:, :, :width])
        scores = masked_scores(queries, key_rows, key_valid)
        attn_probs = jnp.exp(scores - log_total[..., None])
        grad_probs = jnp.einsum(
            "cqhd,ckhd->cqhk",
            grad_heads,
            split_heads(rows_in[:, :, width:]),
            preferred_element_type=jnp.float32,
        )
        grad_scores = narrow(attn_probs * (grad_probs - row_delta[..., None]))
        gradient = (
            gradient
            + jnp.einsum(
                "cqhk,ckhd->cqhd", grad_scores, key_rows, preferred_element_type=jnp.float32
            )
            * 0.125
        )
        return (gradient, None)

    gradient, unused = lax.scan(query_one_block, gradient, jnp.arange(row_count // block_size))
    return gradient


def own_columns(values, place, count):
    share = values.shape[1] // count
    return lax.dynamic_slice_in_dim(values, place * share, share, 1)


MESH = pl.DeviceIdType.MESH
D = 768
PART = 48

PRODUCTS = (
    [(0, j) for j in range(4)]
    + [(1 + j, 4) for j in range(4)]
    + [(5, 5), (6, 6), (7, 7), (8, 8), (8, 9)]
    + [(9, 10), (9, 11), (9, 12)]
)
LEFTS = 10
RIGHTS = 13
TEXT_UNIT = 8


def places():
    band, seq = lax.axis_index("band"), lax.axis_index("seq")
    return lax.div(band, 2), lax.rem(band, 2), lax.div(seq, 2), lax.rem(seq, 2)


def device(y, core, z, x):
    return (y * 2 + core, z * 2 + x)


def remote(src, dst, send, recv, target):
    return pltpu.make_async_remote_copy(
        src_ref=src, dst_ref=dst, send_sem=send, recv_sem=recv, device_id=target, device_id_type=MESH
    )


def weight_kernel(
    left_ref,
    right_ref,
    small_ref,
    mlp_in_ref,
    mlp_out_ref,
    gt,
    grecv,
    lrecv,
    psend,
    pown,
    precv,
    qsend,
    qown,
    qrecv,
    rsend,
    rown,
    rrecv,
    final,
    ls,
    lr,
    gs,
    gr,
    ps,
    pr,
    qs,
    qr,
    rs,
    rr,
    fs,
    fr,
):
    y, core, z, x = places()
    other_x, other_core, other_y = 1 - x, 1 - core, 1 - y
    partners = [
        device(y, core, z, other_x),
        device(y, other_core, z, x),
        device(other_y, core, z, x),
        device(other_y, other_core, z, x),
    ] + [device(y, core, lax.rem(z + k, 4), x) for k in (1, 2, 3)]
    barrier = pltpu.get_barrier_semaphore()
    for partner in partners:
        pl.semaphore_signal(barrier, inc=1, device_id=partner, device_id_type=MESH)
    pl.semaphore_wait(barrier, len(partners))

    def left_copy(u):
        return remote(left_ref.at[u], lrecv.at[u], ls.at[u], lr.at[u], partners[0])

    def right_copy(u):
        return remote(gt.at[u, other_x], grecv.at[u], gs.at[u], gr.at[u], partners[0])

    def core_copy(i):
        return remote(psend.at[i], precv.at[i], ps.at[i], pr.at[i], partners[1])

    def y_copy(i):
        return remote(qsend.at[i], qrecv.at[i], qs.at[i], qr.at[i], partners[2])

    def z_copy(i, k):
        return remote(
            rsend.at[i, lax.rem(z + k, 4)],
            rrecv.at[i, k],
            rs.at[i, k],
            rr.at[i, k],
            partners[3 + k],
        )

    def last_copy(i, j):
        return remote(
            final.at[i, core, y], final.at[i, core, y], fs.at[i, j], fr.at[i, j], partners[j]
        )

    for u in range(RIGHTS):
        turned = jnp.transpose(right_ref[u].astype(jnp.float32)).astype(jnp.bfloat16)
        for s in range(8):
            for c in range(2):
                at = s * 96 + c * PART
                gt[u, s % 2, c, pl.ds((s // 2) * PART, PART), :] = turned[at : at + PART]
        right_copy(u).start()
        if u < LEFTS and u != TEXT_UNIT:
            left_copy(u).start()

    def stage_product(i):
        left, right = PRODUCTS[i]
        if i == 0 or PRODUCTS[i - 1][0] != left:
            if left != TEXT_UNIT:
                left_copy(left).wait_recv()
        if i == 0 or PRODUCTS[i - 1][1] != right:
            right_copy(right).wait_recv()
        for c, keep in ((other_core, False), (core, True)):
            mine, theirs = gt[right, x, c], grecv[right, c]
            if left == TEXT_UNIT:
                both = (mine.astype(jnp.float32) + theirs.astype(jnp.float32)).astype(jnp.bfloat16)
                part = jnp.dot(both, left_ref[left], preferred_element_type=jnp.float32)
            else:
                part = jnp.dot(
                    jnp.concatenate([mine, theirs], axis=1),
                    jnp.concatenate([left_ref[left], lrecv[left]], axis=0),
                    preferred_element_type=jnp.float32,
                )
            if keep:
                pown[i % 2] = part
            else:
                psend[i] = part.astype(jnp.bfloat16)
                core_copy(i).start()

    def stage_core(i):
        core_copy(i).wait_recv()
        total = pown[i % 2] + precv[i].astype(jnp.float32)
        for h in range(2):
            half = total[:, h * 384 : (h + 1) * 384]

            @pl.when(h == y)
            def _():
                qown[i % 2] = half

            @pl.when(h != y)
            def _():
                qsend[i] = half.astype(jnp.bfloat16)

        y_copy(i).start()

    def stage_y(i):
        y_copy(i).wait_recv()
        total = qown[i % 2] + qrecv[i].astype(jnp.float32)
        for k in range(4):
            rsend[i, k] = total[k * PART : (k + 1) * PART].astype(jnp.bfloat16)
            rown[i % 2, k] = total[k * PART : (k + 1) * PART]
        for k in (1, 2, 3):
            z_copy(i, k).start()

    def stage_z(i):
        for k in (1, 2, 3):
            z_copy(i, k).wait_recv()
        total = rown[i % 2, z]
        for k in (1, 2, 3):
            total = total + rrecv[i, k].astype(jnp.float32)
        final[i, core, y] = total.astype(jnp.bfloat16)
        for j in (1, 2, 3):
            last_copy(i, j).start()

    n = len(PRODUCTS)
    stages = (stage_product, stage_core, stage_y, stage_z)
    for step in range(n + 3):
        for at, stage in reversed(list(enumerate(stages))):
            if 0 <= step - at < n:
                stage(step - at)

    for i in range(n):
        for j in (1, 2, 3):
            last_copy(i, j).wait_recv()
        whole = jnp.concatenate(
            [jnp.concatenate([final[i, c, h] for h in range(2)], axis=1) for c in range(2)], axis=0
        ).astype(jnp.float32)
        turned = jnp.transpose(whole)
        if i < 4:
            mlp_in_ref[i] = turned
        elif i < 8:
            mlp_out_ref[pl.ds((i - 4) * D, D), :] = turned
        else:
            small_ref[i - 8] = turned
    for u in range(LEFTS):
        if u != TEXT_UNIT:
            left_copy(u).wait_send()
    for u in range(RIGHTS):
        right_copy(u).wait_send()
    for i in range(n):
        core_copy(i).wait_send()
        y_copy(i).wait_send()
        for k in (1, 2, 3):
            z_copy(i, k).wait_send()
            last_copy(i, k).wait_send()


def weight_sums(lefts, rights):
    n = len(PRODUCTS)
    dma = pltpu.SemaphoreType.DMA
    return pl.pallas_call(
        weight_kernel,
        out_shape=(
            jax.ShapeDtypeStruct((8, D, 96), jnp.float32),
            jax.ShapeDtypeStruct((4, D, 96), jnp.float32),
            jax.ShapeDtypeStruct((4 * D, 96), jnp.float32),
        ),
        in_specs=[pl.BlockSpec(memory_space=pltpu.VMEM)] * 2,
        out_specs=(pl.BlockSpec(memory_space=pltpu.VMEM),) * 3,
        scratch_shapes=[
            pltpu.VMEM((RIGHTS, 2, 2, 192, 128), jnp.bfloat16),
            pltpu.VMEM((RIGHTS, 2, 192, 128), jnp.bfloat16),
            pltpu.VMEM((LEFTS, 128, D), jnp.bfloat16),
            pltpu.VMEM((n, 192, D), jnp.bfloat16),
            pltpu.VMEM((2, 192, D), jnp.float32),
            pltpu.VMEM((n, 192, D), jnp.bfloat16),
            pltpu.VMEM((n, 192, 384), jnp.bfloat16),
            pltpu.VMEM((2, 192, 384), jnp.float32),
            pltpu.VMEM((n, 192, 384), jnp.bfloat16),
            pltpu.VMEM((n, 4, PART, 384), jnp.bfloat16),
            pltpu.VMEM((2, 4, PART, 384), jnp.float32),
            pltpu.VMEM((n, 4, PART, 384), jnp.bfloat16),
            pltpu.VMEM((n, 2, 2, PART, 384), jnp.bfloat16),
            dma((LEFTS,)),
            dma((LEFTS,)),
            dma((RIGHTS,)),
            dma((RIGHTS,)),
            dma((n,)),
            dma((n,)),
            dma((n,)),
            dma((n,)),
            dma((n, 4)),
            dma((n, 4)),
            dma((n, 4)),
            dma((n, 4)),
        ],
        compiler_params=pltpu.CompilerParams(
            collective_id=0, has_side_effects=True, vmem_limit_bytes=60 * 1024 * 1024
        ),
    )(lefts, rights)


def on_device(
    frames,
    text,
    timesteps,
    frame_lengths,
    text_mask,
    cotangent,
    w_time_in,
    w_time_out,
    w_adaln,
    w_query,
    w_key,
    w_value,
    w_attn_out,
    cross_gain,
    w_cross_query,
    w_cross_key,
    w_cross_value,
    w_cross_out,
    w_mlp_in,
    w_mlp_out,
):
    clips = frames.shape[0]
    rows = frames.shape[1]
    width = frames.shape[2]
    tokens = clips * rows
    text_count = text.shape[1]
    seq_place = lax.axis_index("seq")
    seq_count = lax.axis_size("seq")
    offset = seq_place * rows
    inputs = frames.astype(jnp.float32)
    own_valid = (offset + jnp.arange(rows))[None, :] < frame_lengths[:, None]
    row_valid = own_valid[:, :, None]
    text_valid = text_mask != 0

    def flatten(values):
        return values.reshape(tokens, values.shape[-1])

    def unflatten(values):
        return values.reshape(clips, rows, values.shape[-1])

    time_vector = narrow(time_embed(timesteps, w_time_in.shape[0]))
    time_first = product(time_vector, w_time_in)
    time_hidden = narrow(jax.nn.silu(time_first))
    time_out = product(time_hidden, w_time_out)
    condition = narrow(jax.nn.silu(time_out))
    modulation = product(condition, w_adaln)
    shift_attn, scale_attn, gate_attn, shift_mlp, scale_mlp, gate_mlp = [
        piece[:, None, :] for piece in jnp.split(modulation, 6, axis=1)
    ]
    normed_attn, scaling_attn = layer_norm(inputs)
    attn_in = narrow(normed_attn * (1.0 + scale_attn) + shift_attn)
    attn_flat = flatten(attn_in)
    query_flat = narrow(product(attn_flat, w_query))
    queries = split_heads(unflatten(query_flat))
    kv_local = unflatten(
        jnp.concatenate(
            [narrow(product(attn_flat, w_key)), narrow(product(attn_flat, w_value))], axis=1
        )
    )
    start_state = (
        jnp.full((clips, rows, H), -1e30, jnp.float32),
        jnp.zeros((clips, rows, H), jnp.float32),
        jnp.zeros((clips, rows, H, HD), jnp.float32),
    )
    row_max, row_sum, weighted = forward_piece(
        start_state,
        lax.all_gather(kv_local, "seq", axis=1, tiled=True),
        jnp.int32(0),
        queries,
        frame_lengths,
    )
    attended = weighted / row_sum[..., None]
    log_total = row_max + jnp.log(row_sum)
    attn_low = narrow(attended.reshape(clips, rows, width))
    attn_proj = unflatten(product(flatten(attn_low), w_attn_out))
    middle = inputs + gate_attn * attn_proj
    normed_cross, scaling_cross = layer_norm(middle)
    gain_values = cross_gain.astype(jnp.float32)
    cross_in = narrow(normed_cross * gain_values)
    cross_queries = split_heads(unflatten(narrow(product(flatten(cross_in), w_cross_query))))
    text_flat = text.reshape(clips * text_count, width)
    cross_keys = split_heads(
        narrow(product(text_flat, w_cross_key)).reshape(clips, text_count, width)
    )
    cross_values = split_heads(
        narrow(product(text_flat, w_cross_value)).reshape(clips, text_count, width)
    )
    cross_scores = masked_scores(cross_queries, cross_keys, text_valid)
    cross_max = jnp.max(cross_scores, axis=-1, keepdims=True)
    cross_total = cross_max + jnp.log(
        jnp.sum(jnp.exp(cross_scores - cross_max), axis=-1, keepdims=True)
    )
    cross_probs = jnp.exp(cross_scores - cross_total)
    cross_probs_low = narrow(cross_probs)
    cross_attended = jnp.einsum(
        "cqhk,ckhd->cqhd", cross_probs_low, cross_values, preferred_element_type=jnp.float32
    )
    cross_low = narrow(cross_attended.reshape(clips, rows, width))
    after_cross = middle + unflatten(product(flatten(cross_low), w_cross_out))
    normed_mlp, scaling_mlp = layer_norm(after_cross)
    mlp_in = narrow(normed_mlp * (1.0 + scale_mlp) + shift_mlp)
    pre_act = product(flatten(mlp_in), w_mlp_in)
    activation = narrow(jax.nn.gelu(pre_act, approximate=True))
    mlp_out = unflatten(product(activation, w_mlp_out))
    result = after_cross + gate_mlp * mlp_out
    block_out = jnp.where(row_valid, result, inputs).astype(jnp.bfloat16)
    grad_out = cotangent.astype(jnp.float32)
    grad_res = jnp.where(row_valid, grad_out, 0.0)
    grad_mlp = flatten(narrow(gate_mlp * grad_res))
    grad_w_mlp_out = transposed_left(activation, grad_mlp)
    grad_act = transposed_right(grad_mlp, w_mlp_out)
    gelu_pull = jax.vjp(lambda values: jax.nn.gelu(values, approximate=True), pre_act)[1]
    grad_pre = narrow(gelu_pull(grad_act)[0])
    grad_w_mlp_in = transposed_left(flatten(mlp_in), grad_pre)
    grad_mlp_in = unflatten(transposed_right(grad_pre, w_mlp_in))
    grad_after = grad_res + norm_back(normed_mlp, scaling_mlp, grad_mlp_in * (1.0 + scale_mlp))
    grad_cross_out = flatten(narrow(grad_after))
    grad_w_cross_out = transposed_left(flatten(cross_low), grad_cross_out)
    grad_cross_attn = split_heads(unflatten(narrow(transposed_right(grad_cross_out, w_cross_out))))
    cross_delta = jnp.sum(grad_cross_attn.astype(jnp.float32) * cross_attended, axis=-1)
    cross_grad_probs = jnp.einsum(
        "cqhd,ckhd->cqhk", grad_cross_attn, cross_values, preferred_element_type=jnp.float32
    )
    cross_grad_scores = narrow(cross_probs * (cross_grad_probs - cross_delta[..., None]))
    grad_cross_query = narrow(
        jnp.einsum(
            "cqhk,ckhd->cqhd", cross_grad_scores, cross_keys, preferred_element_type=jnp.float32
        )
        * 0.125
    ).reshape(tokens, width)
    cross_key_part = (
        jnp.einsum(
            "cqhk,cqhd->ckhd", cross_grad_scores, cross_queries, preferred_element_type=jnp.float32
        )
        * 0.125
    )
    cross_value_part = jnp.einsum(
        "cqhk,cqhd->ckhd", cross_probs_low, grad_cross_attn, preferred_element_type=jnp.float32
    )
    cross_kv_part = jnp.concatenate(
        [
            cross_key_part.reshape(clips, text_count, width),
            cross_value_part.reshape(clips, text_count, width),
        ],
        axis=2,
    )
    text_total = lax.psum_scatter(cross_kv_part, "seq", scatter_dimension=1, tiled=True)
    text_share = text_total.shape[1]
    grad_cross_key = narrow(text_total[:, :, :width]).reshape(clips * text_share, width)
    grad_cross_value = narrow(text_total[:, :, width:]).reshape(clips * text_share, width)
    text_own = lax.dynamic_slice_in_dim(text, seq_place * text_share, text_share, 1).reshape(
        clips * text_share, width
    )
    grad_text = (
        transposed_right(grad_cross_key, w_cross_key)
        + transposed_right(grad_cross_value, w_cross_value)
    ).reshape(clips, text_share, width)
    grad_w_cross_key = transposed_left(text_own, grad_cross_key)
    grad_w_cross_value = transposed_left(text_own, grad_cross_value)
    grad_w_cross_query = transposed_left(flatten(cross_in), grad_cross_query)
    grad_cross_in = unflatten(transposed_right(grad_cross_query, w_cross_query))
    grad_gain_part = jnp.sum(grad_cross_in * normed_cross, axis=(0, 1))
    grad_mid = grad_after + norm_back(normed_cross, scaling_cross, grad_cross_in * gain_values)
    grad_attn_proj = flatten(narrow(gate_attn * grad_mid))
    grad_w_attn_out = transposed_left(flatten(attn_low), grad_attn_proj)
    grad_attn_flat = narrow(transposed_right(grad_attn_proj, w_attn_out))
    grad_heads = split_heads(unflatten(grad_attn_flat))
    row_delta = jnp.sum(grad_heads.astype(jnp.float32) * attended, axis=-1)
    zero_heads = jnp.zeros((clips, rows, H, HD), jnp.float32)
    gathered = lax.all_gather(kv_local, "seq", axis=1, tiled=True)
    query_grad = query_piece(
        zero_heads, gathered, 0, queries, grad_heads, log_total, row_delta, frame_lengths
    )
    anchor = jnp.int32(0)
    block_size = math.gcd(rows * lax.axis_size("seq"), key_block)

    def key_one_block(counter):
        rows_in = lax.dynamic_slice_in_dim(gathered, counter * block_size, block_size, 1)
        key_valid = block_valid(anchor, counter * block_size, block_size, frame_lengths)
        scores = masked_scores(queries, split_heads(rows_in[:, :, :width]), key_valid)
        attn_probs = jnp.exp(scores - log_total[..., None])
        grad_probs = jnp.einsum(
            "cqhd,ckhd->cqhk",
            grad_heads,
            split_heads(rows_in[:, :, width:]),
            preferred_element_type=jnp.float32,
        )
        grad_scores = narrow(attn_probs * (grad_probs - row_delta[..., None]))
        grad_keys = (
            jnp.einsum("cqhk,cqhd->ckhd", grad_scores, queries, preferred_element_type=jnp.float32)
            * 0.125
        )
        grad_values = jnp.einsum(
            "cqhk,cqhd->ckhd", narrow(attn_probs), grad_heads, preferred_element_type=jnp.float32
        )
        joined = jnp.concatenate(
            [
                grad_keys.reshape(clips, block_size, width),
                grad_values.reshape(clips, block_size, width),
            ],
            axis=2,
        )
        return jnp.transpose(joined, (1, 0, 2))

    blocks = lax.map(key_one_block, jnp.arange(rows * lax.axis_size("seq") // block_size))
    kv_term = lax.psum_scatter(
        blocks.reshape(rows * lax.axis_size("seq"), clips, 2 * width),
        "seq",
        scatter_dimension=0,
        tiled=True,
    )
    kv_grad = jnp.transpose(kv_term, (1, 0, 2))
    grad_query = narrow(query_grad.reshape(tokens, width))
    grad_key = flatten(narrow(kv_grad[:, :, :width]))
    grad_value = flatten(narrow(kv_grad[:, :, width:]))
    grad_w_query = transposed_left(attn_flat, grad_query)
    grad_w_key = transposed_left(attn_flat, grad_key)
    grad_w_value = transposed_left(attn_flat, grad_value)
    grad_attn_in = unflatten(
        transposed_right(grad_query, w_query)
        + transposed_right(grad_key, w_key)
        + transposed_right(grad_value, w_value)
    )
    grad_inputs = grad_mid + norm_back(normed_attn, scaling_attn, grad_attn_in * (1.0 + scale_attn))
    grad_frames = jnp.where(row_valid, grad_inputs, grad_out).astype(jnp.bfloat16)
    modulation_part = jnp.concatenate(
        [
            jnp.sum(grad_attn_in, axis=1),
            jnp.sum(grad_attn_in * normed_attn, axis=1),
            jnp.sum(grad_mid * attn_proj, axis=1),
            jnp.sum(grad_mlp_in, axis=1),
            jnp.sum(grad_mlp_in * normed_mlp, axis=1),
            jnp.sum(grad_res * mlp_out, axis=1),
        ],
        axis=1,
    )
    modulation_total = lax.psum(modulation_part, "seq")
    grad_modulation = narrow(modulation_total)
    grad_w_adaln = transposed_left(condition, grad_modulation)
    grad_condition = transposed_right(grad_modulation, w_adaln)
    grad_time_out = narrow(jax.vjp(jax.nn.silu, time_out)[1](grad_condition)[0])
    grad_w_time_out = transposed_left(time_hidden, grad_time_out)
    grad_time_hidden = transposed_right(grad_time_out, w_time_out)
    grad_time_first = jax.vjp(jax.nn.silu, time_first)[1](grad_time_hidden)[0]
    grad_w_time_in = lax.dot_general(
        time_vector.astype(jnp.float32),
        grad_time_first,
        (((0,), (0,)), ((), ())),
        precision=lax.Precision.HIGHEST,
    )
    by_block = lambda values: jnp.transpose(
        values.reshape(tokens, 8, 4, 96), (2, 0, 1, 3)
    ).reshape(4, tokens, width)
    lefts = jnp.concatenate(
        [
            flatten(mlp_in)[None],
            jnp.transpose(activation.reshape(tokens, 4, width), (1, 0, 2)),
            jnp.stack(
                [flatten(cross_low), flatten(cross_in), flatten(attn_low), text_flat, attn_flat]
            ),
        ],
        axis=0,
    )
    text_keys, text_values = [
        narrow(values.reshape(clips * text_count, width))
        for values in (cross_key_part, cross_value_part)
    ]
    rights = jnp.concatenate(
        [
            by_block(grad_pre),
            jnp.stack(
                [
                    grad_mlp,
                    grad_cross_out,
                    grad_cross_query,
                    grad_attn_proj,
                    text_keys,
                    text_values,
                    grad_query,
                    grad_key,
                    grad_value,
                ]
            ),
        ],
        axis=0,
    )
    small, mlp_in_parts, sum_mlp_out = weight_sums(lefts, rights)
    sum_mlp_in = jnp.transpose(mlp_in_parts, (1, 0, 2)).reshape(width, 4 * 96)
    (
        sum_cross_out,
        sum_cross_query,
        sum_attn_out,
        sum_cross_key,
        sum_cross_value,
        sum_query,
        sum_key,
        sum_value,
    ) = [small[i] for i in range(8)]
    gain_share = width // seq_count
    sum_gain = lax.dynamic_slice_in_dim(
        lax.psum(grad_gain_part, ("band", "seq")), seq_place * gain_share, gain_share, 0
    )
    replicated = (
        own_columns(grad_w_time_in, seq_place, seq_count),
        own_columns(grad_w_time_out, seq_place, seq_count),
        own_columns(grad_w_adaln, seq_place, seq_count),
    )
    sum_time_in, sum_time_out, sum_adaln = jax.tree.map(
        lambda part: part.astype(jnp.float32), lax.psum(for_sending(replicated), "band")
    )
    return (
        block_out,
        grad_frames,
        grad_text,
        sum_time_in,
        sum_time_out,
        sum_adaln,
        sum_query,
        sum_key,
        sum_value,
        sum_attn_out,
        sum_gain,
        sum_cross_query,
        sum_cross_key,
        sum_cross_value,
        sum_cross_out,
        sum_mlp_in,
        sum_mlp_out,
    )


def on_device_general(
    frames,
    text,
    timesteps,
    frame_lengths,
    text_mask,
    cotangent,
    w_time_in,
    w_time_out,
    w_adaln,
    w_query,
    w_key,
    w_value,
    w_attn_out,
    cross_gain,
    w_cross_query,
    w_cross_key,
    w_cross_value,
    w_cross_out,
    w_mlp_in,
    w_mlp_out,
):
    clips = frames.shape[0]
    rows = frames.shape[1]
    width = frames.shape[2]
    tokens = clips * rows
    text_count = text.shape[1]
    seq_place = lax.axis_index("seq")
    seq_count = lax.axis_size("seq")
    offset = seq_place * rows
    inputs = frames.astype(jnp.float32)
    own_valid = (offset + jnp.arange(rows))[None, :] < frame_lengths[:, None]
    row_valid = own_valid[:, :, None]
    text_valid = text_mask != 0

    def flatten(values):
        return values.reshape(tokens, values.shape[-1])

    def unflatten(values):
        return values.reshape(clips, rows, values.shape[-1])

    time_vector = narrow(time_embed(timesteps, w_time_in.shape[0]))
    time_first = product(time_vector, w_time_in)
    time_hidden = narrow(jax.nn.silu(time_first))
    time_out = product(time_hidden, w_time_out)
    condition = narrow(jax.nn.silu(time_out))
    modulation = product(condition, w_adaln)
    shift_attn, scale_attn, gate_attn, shift_mlp, scale_mlp, gate_mlp = [
        piece[:, None, :] for piece in jnp.split(modulation, 6, axis=1)
    ]
    normed_attn, scaling_attn = layer_norm(inputs)
    attn_in = narrow(normed_attn * (1.0 + scale_attn) + shift_attn)
    attn_flat = flatten(attn_in)
    query_flat = narrow(product(attn_flat, w_query))
    queries = split_heads(unflatten(query_flat))
    kv_local = unflatten(
        jnp.concatenate(
            [narrow(product(attn_flat, w_key)), narrow(product(attn_flat, w_value))], axis=1
        )
    )
    start_state = (
        jnp.full((clips, rows, H), -1e30, jnp.float32),
        jnp.zeros((clips, rows, H), jnp.float32),
        jnp.zeros((clips, rows, H, HD), jnp.float32),
    )
    row_max, row_sum, weighted = forward_piece(
        start_state,
        lax.all_gather(kv_local, "seq", axis=1, tiled=True),
        jnp.int32(0),
        queries,
        frame_lengths,
    )
    attended = weighted / row_sum[..., None]
    log_total = row_max + jnp.log(row_sum)
    attn_low = narrow(attended.reshape(clips, rows, width))
    attn_proj = unflatten(product(flatten(attn_low), w_attn_out))
    middle = inputs + gate_attn * attn_proj
    normed_cross, scaling_cross = layer_norm(middle)
    gain_values = cross_gain.astype(jnp.float32)
    cross_in = narrow(normed_cross * gain_values)
    cross_queries = split_heads(unflatten(narrow(product(flatten(cross_in), w_cross_query))))
    text_flat = text.reshape(clips * text_count, width)
    cross_keys = split_heads(
        narrow(product(text_flat, w_cross_key)).reshape(clips, text_count, width)
    )
    cross_values = split_heads(
        narrow(product(text_flat, w_cross_value)).reshape(clips, text_count, width)
    )
    cross_scores = masked_scores(cross_queries, cross_keys, text_valid)
    cross_max = jnp.max(cross_scores, axis=-1, keepdims=True)
    cross_total = cross_max + jnp.log(
        jnp.sum(jnp.exp(cross_scores - cross_max), axis=-1, keepdims=True)
    )
    cross_probs = jnp.exp(cross_scores - cross_total)
    cross_probs_low = narrow(cross_probs)
    cross_attended = jnp.einsum(
        "cqhk,ckhd->cqhd", cross_probs_low, cross_values, preferred_element_type=jnp.float32
    )
    cross_low = narrow(cross_attended.reshape(clips, rows, width))
    after_cross = middle + unflatten(product(flatten(cross_low), w_cross_out))
    normed_mlp, scaling_mlp = layer_norm(after_cross)
    mlp_in = narrow(normed_mlp * (1.0 + scale_mlp) + shift_mlp)
    pre_act = product(flatten(mlp_in), w_mlp_in)
    activation = narrow(jax.nn.gelu(pre_act, approximate=True))
    mlp_out = unflatten(product(activation, w_mlp_out))
    result = after_cross + gate_mlp * mlp_out
    block_out = jnp.where(row_valid, result, inputs).astype(jnp.bfloat16)
    grad_out = cotangent.astype(jnp.float32)
    grad_res = jnp.where(row_valid, grad_out, 0.0)
    grad_mlp = flatten(narrow(gate_mlp * grad_res))
    grad_w_mlp_out = transposed_left(activation, grad_mlp)
    grad_act = transposed_right(grad_mlp, w_mlp_out)
    gelu_pull = jax.vjp(lambda values: jax.nn.gelu(values, approximate=True), pre_act)[1]
    grad_pre = narrow(gelu_pull(grad_act)[0])
    grad_w_mlp_in = transposed_left(flatten(mlp_in), grad_pre)
    grad_mlp_in = unflatten(transposed_right(grad_pre, w_mlp_in))
    grad_after = grad_res + norm_back(normed_mlp, scaling_mlp, grad_mlp_in * (1.0 + scale_mlp))
    grad_cross_out = flatten(narrow(grad_after))
    grad_w_cross_out = transposed_left(flatten(cross_low), grad_cross_out)
    grad_cross_attn = split_heads(unflatten(narrow(transposed_right(grad_cross_out, w_cross_out))))
    cross_delta = jnp.sum(grad_cross_attn.astype(jnp.float32) * cross_attended, axis=-1)
    cross_grad_probs = jnp.einsum(
        "cqhd,ckhd->cqhk", grad_cross_attn, cross_values, preferred_element_type=jnp.float32
    )
    cross_grad_scores = narrow(cross_probs * (cross_grad_probs - cross_delta[..., None]))
    grad_cross_query = narrow(
        jnp.einsum(
            "cqhk,ckhd->cqhd", cross_grad_scores, cross_keys, preferred_element_type=jnp.float32
        )
        * 0.125
    ).reshape(tokens, width)
    cross_key_part = (
        jnp.einsum(
            "cqhk,cqhd->ckhd", cross_grad_scores, cross_queries, preferred_element_type=jnp.float32
        )
        * 0.125
    )
    cross_value_part = jnp.einsum(
        "cqhk,cqhd->ckhd", cross_probs_low, grad_cross_attn, preferred_element_type=jnp.float32
    )
    cross_kv_part = jnp.concatenate(
        [
            cross_key_part.reshape(clips, text_count, width),
            cross_value_part.reshape(clips, text_count, width),
        ],
        axis=2,
    )
    text_total = lax.psum_scatter(cross_kv_part, "seq", scatter_dimension=1, tiled=True)
    text_share = text_total.shape[1]
    grad_cross_key = narrow(text_total[:, :, :width]).reshape(clips * text_share, width)
    grad_cross_value = narrow(text_total[:, :, width:]).reshape(clips * text_share, width)
    text_own = lax.dynamic_slice_in_dim(text, seq_place * text_share, text_share, 1).reshape(
        clips * text_share, width
    )
    grad_text = (
        transposed_right(grad_cross_key, w_cross_key)
        + transposed_right(grad_cross_value, w_cross_value)
    ).reshape(clips, text_share, width)
    grad_w_cross_key = transposed_left(text_own, grad_cross_key)
    grad_w_cross_value = transposed_left(text_own, grad_cross_value)
    grad_w_cross_query = transposed_left(flatten(cross_in), grad_cross_query)
    grad_cross_in = unflatten(transposed_right(grad_cross_query, w_cross_query))
    grad_gain_part = jnp.sum(grad_cross_in * normed_cross, axis=(0, 1))
    grad_mid = grad_after + norm_back(normed_cross, scaling_cross, grad_cross_in * gain_values)
    grad_attn_proj = flatten(narrow(gate_attn * grad_mid))
    grad_w_attn_out = transposed_left(flatten(attn_low), grad_attn_proj)
    grad_attn_flat = narrow(transposed_right(grad_attn_proj, w_attn_out))
    grad_heads = split_heads(unflatten(grad_attn_flat))
    row_delta = jnp.sum(grad_heads.astype(jnp.float32) * attended, axis=-1)
    zero_heads = jnp.zeros((clips, rows, H, HD), jnp.float32)
    gathered = lax.all_gather(kv_local, "seq", axis=1, tiled=True)
    query_grad = query_piece(
        zero_heads, gathered, 0, queries, grad_heads, log_total, row_delta, frame_lengths
    )
    anchor = jnp.int32(0)
    block_size = math.gcd(rows * lax.axis_size("seq"), key_block)

    def key_one_block(counter):
        rows_in = lax.dynamic_slice_in_dim(gathered, counter * block_size, block_size, 1)
        key_valid = block_valid(anchor, counter * block_size, block_size, frame_lengths)
        scores = masked_scores(queries, split_heads(rows_in[:, :, :width]), key_valid)
        attn_probs = jnp.exp(scores - log_total[..., None])
        grad_probs = jnp.einsum(
            "cqhd,ckhd->cqhk",
            grad_heads,
            split_heads(rows_in[:, :, width:]),
            preferred_element_type=jnp.float32,
        )
        grad_scores = narrow(attn_probs * (grad_probs - row_delta[..., None]))
        grad_keys = (
            jnp.einsum("cqhk,cqhd->ckhd", grad_scores, queries, preferred_element_type=jnp.float32)
            * 0.125
        )
        grad_values = jnp.einsum(
            "cqhk,cqhd->ckhd", narrow(attn_probs), grad_heads, preferred_element_type=jnp.float32
        )
        joined = jnp.concatenate(
            [
                grad_keys.reshape(clips, block_size, width),
                grad_values.reshape(clips, block_size, width),
            ],
            axis=2,
        )
        return jnp.transpose(joined, (1, 0, 2))

    blocks = lax.map(key_one_block, jnp.arange(rows * lax.axis_size("seq") // block_size))
    kv_term = lax.psum_scatter(
        blocks.reshape(rows * lax.axis_size("seq"), clips, 2 * width),
        "seq",
        scatter_dimension=0,
        tiled=True,
    )
    kv_grad = jnp.transpose(kv_term, (1, 0, 2))
    grad_query = narrow(query_grad.reshape(tokens, width))
    grad_key = flatten(narrow(kv_grad[:, :, :width]))
    grad_value = flatten(narrow(kv_grad[:, :, width:]))
    grad_w_query = transposed_left(attn_flat, grad_query)
    grad_w_key = transposed_left(attn_flat, grad_key)
    grad_w_value = transposed_left(attn_flat, grad_value)
    grad_attn_in = unflatten(
        transposed_right(grad_query, w_query)
        + transposed_right(grad_key, w_key)
        + transposed_right(grad_value, w_value)
    )
    grad_inputs = grad_mid + norm_back(normed_attn, scaling_attn, grad_attn_in * (1.0 + scale_attn))
    grad_frames = jnp.where(row_valid, grad_inputs, grad_out).astype(jnp.bfloat16)
    modulation_part = jnp.concatenate(
        [
            jnp.sum(grad_attn_in, axis=1),
            jnp.sum(grad_attn_in * normed_attn, axis=1),
            jnp.sum(grad_mid * attn_proj, axis=1),
            jnp.sum(grad_mlp_in, axis=1),
            jnp.sum(grad_mlp_in * normed_mlp, axis=1),
            jnp.sum(grad_res * mlp_out, axis=1),
        ],
        axis=1,
    )
    modulation_total = lax.psum(modulation_part, "seq")
    grad_modulation = narrow(modulation_total)
    grad_w_adaln = transposed_left(condition, grad_modulation)
    grad_condition = transposed_right(grad_modulation, w_adaln)
    grad_time_out = narrow(jax.vjp(jax.nn.silu, time_out)[1](grad_condition)[0])
    grad_w_time_out = transposed_left(time_hidden, grad_time_out)
    grad_time_hidden = transposed_right(grad_time_out, w_time_out)
    grad_time_first = jax.vjp(jax.nn.silu, time_first)[1](grad_time_hidden)[0]
    grad_w_time_in = lax.dot_general(
        time_vector.astype(jnp.float32),
        grad_time_first,
        (((0,), (0,)), ((), ())),
        precision=lax.Precision.HIGHEST,
    )
    shared = (
        lax.psum_scatter(grad_w_query, "seq", scatter_dimension=1, tiled=True),
        lax.psum_scatter(grad_w_key, "seq", scatter_dimension=1, tiled=True),
        lax.psum_scatter(grad_w_value, "seq", scatter_dimension=1, tiled=True),
        lax.psum_scatter(grad_w_attn_out, "seq", scatter_dimension=1, tiled=True),
        lax.psum_scatter(grad_gain_part, "seq", scatter_dimension=0, tiled=True),
        lax.psum_scatter(grad_w_cross_query, "seq", scatter_dimension=1, tiled=True),
        lax.psum_scatter(grad_w_cross_key, "seq", scatter_dimension=1, tiled=True),
        lax.psum_scatter(grad_w_cross_value, "seq", scatter_dimension=1, tiled=True),
        lax.psum_scatter(grad_w_cross_out, "seq", scatter_dimension=1, tiled=True),
        lax.psum_scatter(grad_w_mlp_in, "seq", scatter_dimension=1, tiled=True),
        lax.psum_scatter(grad_w_mlp_out, "seq", scatter_dimension=1, tiled=True),
    )
    replicated = (
        own_columns(grad_w_time_in, seq_place, seq_count),
        own_columns(grad_w_time_out, seq_place, seq_count),
        own_columns(grad_w_adaln, seq_place, seq_count),
    )
    summed = jax.tree.map(
        lambda part: part.astype(jnp.float32), lax.psum(for_sending(shared + replicated), "band")
    )
    (
        sum_query,
        sum_key,
        sum_value,
        sum_attn_out,
        sum_gain,
        sum_cross_query,
        sum_cross_key,
        sum_cross_value,
        sum_cross_out,
        sum_mlp_in,
        sum_mlp_out,
        sum_time_in,
        sum_time_out,
        sum_adaln,
    ) = summed
    return (
        block_out,
        grad_frames,
        grad_text,
        sum_time_in,
        sum_time_out,
        sum_adaln,
        sum_query,
        sum_key,
        sum_value,
        sum_attn_out,
        sum_gain,
        sum_cross_query,
        sum_cross_key,
        sum_cross_value,
        sum_cross_out,
        sum_mlp_in,
        sum_mlp_out,
    )


def solution(mesh):
    placed = (
        P("band", "seq", None),
        P("band", None, None),
        P("band"),
        P("band"),
        P("band", None),
        P("band", "seq", None),
        P(),
        P(),
        P(),
        P(),
        P(),
        P(),
        P(),
        P(),
        P(),
        P(),
        P(),
        P(),
        P(),
        P(),
    )
    paired = mesh.shape["band"] == 4 and mesh.shape["seq"] == 8
    return jax.shard_map(
        on_device if paired else on_device_general,
        mesh=mesh,
        in_specs=placed,
        out_specs=(
            P("band", "seq", None),
            P("band", "seq", None),
            P("band", "seq", None),
            P(None, "seq"),
            P(None, "seq"),
            P(None, "seq"),
            P(None, "seq"),
            P(None, "seq"),
            P(None, "seq"),
            P(None, "seq"),
            P("seq"),
            P(None, "seq"),
            P(None, "seq"),
            P(None, "seq"),
            P(None, "seq"),
            P(None, "seq"),
            P(None, "seq"),
        ),
        check_vma=False,
    )
```

```python
import math
import types

import jax
import jax.numpy as jnp
from jax import lax
from jax.experimental import pallas as pl
from jax.experimental.pallas import tpu as pltpu
from jax.sharding import PartitionSpec as P

H = 12
HD = 64


epsilon = 1e-06
masked_value = -1000000000.0
key_block = 512


def for_sending(value):
    return jax.tree.map(lambda a: a.astype(jnp.bfloat16) if a.dtype == jnp.float32 else a, value)


def narrow(values):
    return values.astype(jnp.bfloat16)


def product(left, right):
    return jnp.dot(left, right, preferred_element_type=jnp.float32)


def transposed_left(left, right):
    return lax.dot_general(
        left, right, (((0,), (0,)), ((), ())), preferred_element_type=jnp.float32
    )


def transposed_right(left, right):
    return lax.dot_general(
        left, right, (((1,), (1,)), ((), ())), preferred_element_type=jnp.float32
    )


def layer_norm(inputs):
    center = inputs - jnp.mean(inputs, axis=-1, keepdims=True)
    scaling = lax.rsqrt(jnp.mean(center * center, axis=-1, keepdims=True) + epsilon)
    return (center * scaling, scaling)


def norm_back(normed, scaling, gradient):
    mean_grad = jnp.mean(gradient, axis=-1, keepdims=True)
    mean_prod = jnp.mean(gradient * normed, axis=-1, keepdims=True)
    return scaling * (gradient - mean_grad - normed * mean_prod)


def time_embed(timesteps, width):
    half_width = width // 2
    frequency = jnp.exp(-math.log(10000.0) * jnp.arange(half_width, dtype=jnp.float32) / half_width)
    angles = timesteps.astype(jnp.float32)[:, None] * frequency[None, :]
    return jnp.concatenate([jnp.cos(angles), jnp.sin(angles)], axis=1)


def split_heads(rows_in):
    return rows_in.reshape(rows_in.shape[0], rows_in.shape[1], H, HD)


def masked_scores(queries, key_rows, key_valid):
    scores = (
        jnp.einsum("cqhd,ckhd->cqhk", queries, key_rows, preferred_element_type=jnp.float32) * 0.125
    )
    return jnp.where(key_valid[:, None, None, :], scores, masked_value)


def block_valid(anchor, start_row, block_size, lengths):
    return (anchor + start_row + jnp.arange(block_size))[None, :] < lengths[:, None]


def forward_piece(running, segment, anchor, queries, lengths):
    row_count = segment.shape[1]
    block_size = math.gcd(row_count, key_block)
    width = queries.shape[2] * queries.shape[3]

    def forward_one_block(running, counter):
        rows_in = lax.dynamic_slice_in_dim(segment, counter * block_size, block_size, 1)
        key_valid = block_valid(anchor, counter * block_size, block_size, lengths)
        scores = masked_scores(queries, split_heads(rows_in[:, :, :width]), key_valid)
        row_max, row_sum, weighted = running
        new_max = jnp.maximum(row_max, jnp.max(scores, axis=-1))
        factor = jnp.exp(row_max - new_max)
        expanded = jnp.exp(scores - new_max[..., None])
        row_sum = row_sum * factor + jnp.sum(expanded, axis=-1)
        weighted = weighted * factor[..., None] + jnp.einsum(
            "cqhk,ckhd->cqhd",
            narrow(expanded),
            split_heads(rows_in[:, :, width:]),
            preferred_element_type=jnp.float32,
        )
        return ((new_max, row_sum, weighted), None)

    running, unused = lax.scan(forward_one_block, running, jnp.arange(row_count // block_size))
    return running


def query_piece(gradient, segment, anchor, queries, grad_heads, log_total, row_delta, lengths):
    row_count = segment.shape[1]
    block_size = math.gcd(row_count, key_block)
    width = queries.shape[2] * queries.shape[3]

    def query_one_block(gradient, counter):
        rows_in = lax.dynamic_slice_in_dim(segment, counter * block_size, block_size, 1)
        key_valid = block_valid(anchor, counter * block_size, block_size, lengths)
        key_rows = split_heads(rows_in[:, :, :width])
        scores = masked_scores(queries, key_rows, key_valid)
        attn_probs = jnp.exp(scores - log_total[..., None])
        grad_probs = jnp.einsum(
            "cqhd,ckhd->cqhk",
            grad_heads,
            split_heads(rows_in[:, :, width:]),
            preferred_element_type=jnp.float32,
        )
        grad_scores = narrow(attn_probs * (grad_probs - row_delta[..., None]))
        gradient = (
            gradient
            + jnp.einsum(
                "cqhk,ckhd->cqhd", grad_scores, key_rows, preferred_element_type=jnp.float32
            )
            * 0.125
        )
        return (gradient, None)

    gradient, unused = lax.scan(query_one_block, gradient, jnp.arange(row_count // block_size))
    return gradient


def own_columns(values, place, count):
    share = values.shape[1] // count
    return lax.dynamic_slice_in_dim(values, place * share, share, 1)


MESH = pl.DeviceIdType.MESH
D = 768
PART = 48
VMEM_BYTES = 66500 * 1000


def places():
    band, seq = lax.axis_index("band"), lax.axis_index("seq")
    return lax.div(band, 2), lax.rem(band, 2), lax.div(seq, 2), lax.rem(seq, 2)


def device(y, core, z, x):
    return (y * 2 + core, z * 2 + x)


def remote(src, dst, send, recv, target):
    return pltpu.make_async_remote_copy(
        src_ref=src, dst_ref=dst, send_sem=send, recv_sem=recv, device_id=target, device_id_type=MESH
    )


def greet(partners):
    barrier = pltpu.get_barrier_semaphore()
    for partner in partners:
        pl.semaphore_signal(barrier, inc=1, device_id=partner, device_id_type=MESH)
    pl.semaphore_wait(barrier, len(partners))


class Spread:
    def __init__(self, buffers, recv, up, down, across):
        self.buffers, self.recv, self.up, self.down, self.across = buffers, recv, up, down, across
        self.y, self.core, self.z, self.x = places()

    def copies(self, slot, sems, at, target):
        return [
            remote(buf.at[slot], buf.at[slot], sems.at[i, at], self.recv.at[i, slot], target)
            for i, buf in enumerate(self.buffers)
        ]

    def to_up(self, k):
        return self.copies(
            (self.z - k) * 2 + self.x, self.up, k, device(self.y, self.core, self.z + 1, self.x)
        )

    def to_down(self, k):
        return self.copies(
            (self.z + k) * 2 + self.x, self.down, k, device(self.y, self.core, self.z - 1, self.x)
        )

    def to_across(self, row):
        return self.copies(
            row * 2 + self.x, self.across, row, device(self.y, self.core, self.z, 1 - self.x)
        )

    def arrived(self, slot):
        for copy in self.copies(slot, self.across, 0, device(self.y, self.core, self.z, 1 - self.x)):
            copy.wait_recv()

    def start(self):
        z = self.z

        @pl.when(z < 3)
        def _():
            for copy in self.to_up(0):
                copy.start()

        @pl.when(z > 0)
        def _():
            for copy in self.to_down(0):
                copy.start()

        for copy in self.to_across(z):
            copy.start()

    def relay(self, k):
        z = self.z

        @pl.when(z >= k)
        def _():
            self.arrived((z - k) * 2 + self.x)

            @pl.when(z < 3)
            def _():
                for copy in self.to_up(k):
                    copy.start()

            for copy in self.to_across(z - k):
                copy.start()

        @pl.when(z + k <= 3)
        def _():
            self.arrived((z + k) * 2 + self.x)

            @pl.when(z > 0)
            def _():
                for copy in self.to_down(k):
                    copy.start()

            for copy in self.to_across(z + k):
                copy.start()

    def finish(self):
        z = self.z
        for k in range(4):

            @pl.when((z >= k) & (z < 3))
            def _():
                for copy in self.to_up(k):
                    copy.wait_send()

            @pl.when((z + k <= 3) & (z > 0))
            def _():
                for copy in self.to_down(k):
                    copy.wait_send()

            for copy in self.to_across(k):
                copy.wait_send()


def silu(values):
    return values / (1.0 + jnp.exp(-values))


def head_mask(half):
    lane = lax.broadcasted_iota(jnp.int32, (1, 128), 1)
    return (lane < 64) if half == 0 else (lane >= 64)


def keep_head(tile, half):
    return jnp.where(head_mask(half), tile, jnp.zeros_like(tile))


def attend_kernel(
    length_ref,
    vector_ref,
    frames_ref,
    w_time_in_ref,
    w_time_out_ref,
    w_adaln_ref,
    w_query_ref,
    w_key_ref,
    w_value_ref,
    mod_ref,
    time_ref,
    qkv_ref,
    attended_ref,
    stats_ref,
    gathered,
    time_in,
    time_out,
    adaln,
    projections,
    load_sems,
    recv,
    up,
    down,
    across,
):
    y, core, z, x = places()
    me = z * 2 + x
    own = pltpu.make_async_copy(frames_ref, gathered.at[me], load_sems.at[0])
    own.start()
    loads = [
        pltpu.make_async_copy(w_time_in_ref, time_in, load_sems.at[1]),
        pltpu.make_async_copy(w_time_out_ref, time_out, load_sems.at[2]),
    ]
    loads += [
        pltpu.make_async_copy(
            w_adaln_ref.at[:, pl.ds(i * 1536, 1536)], adaln.at[i], load_sems.at[3 + i]
        )
        for i in range(3)
    ]
    loads += [
        pltpu.make_async_copy(ref, projections.at[i], load_sems.at[6 + i])
        for i, ref in enumerate((w_query_ref, w_key_ref, w_value_ref))
    ]
    for load in loads:
        load.start()
    neighbours = Spread([gathered], recv, up, down, across)
    barrier = pltpu.get_barrier_semaphore()
    pl.semaphore_signal(
        barrier, inc=1, device_id=device(y, core, z, 1 - x), device_id_type=MESH
    )

    @pl.when(z < 3)
    def _():
        pl.semaphore_signal(barrier, inc=1, device_id=device(y, core, z + 1, x), device_id_type=MESH)

    @pl.when(z > 0)
    def _():
        pl.semaphore_signal(barrier, inc=1, device_id=device(y, core, z - 1, x), device_id_type=MESH)

    pl.semaphore_wait(barrier, 2 + lax.rem(lax.div(z + 1, 2), 2))
    own.wait()
    neighbours.start()
    loads[0].wait()
    first = product(vector_ref[...], time_in[...])
    hidden = narrow(silu(first))
    loads[1].wait()
    second = product(hidden, time_out[...])
    condition = narrow(silu(second))
    time_ref[:, 0:D] = first[0:8]
    time_ref[:, D : 2 * D] = second[0:8]
    loads[2].wait()
    mod_ref[:, 0:1536] = product(condition, adaln[0])[0:8]
    neighbours.relay(1)
    loads[3].wait()
    mod_ref[:, 1536:3072] = product(condition, adaln[1])[0:8]
    neighbours.relay(2)
    loads[4].wait()
    mod_ref[:, 3072:4608] = product(condition, adaln[2])[0:8]
    neighbours.relay(3)
    for load in loads[5:]:
        load.wait()

    def project(slot):
        normed, unused = layer_norm(gathered[slot].astype(jnp.float32))
        low = narrow(normed * (1.0 + mod_ref[0:1, D : 2 * D]) + mod_ref[0:1, 0:D])
        for i in range(3):
            qkv_ref[i, slot] = narrow(product(low, projections[i]))

    def own_column(row, unused):
        project(row * 2 + x)
        return unused

    def other_column(row, unused):
        neighbours.arrived(row * 2 + 1 - x)
        project(row * 2 + 1 - x)
        return unused

    lax.fori_loop(0, 4, own_column, 0)
    lax.fori_loop(0, 4, other_column, 0)
    length = length_ref[0]
    key_valid = lax.broadcasted_iota(jnp.int32, (1, 1024), 1) < length
    lane = lax.broadcasted_iota(jnp.int32, (1, 128), 1)

    def pair(tile, stats):
        at = pl.ds(pl.multiple_of(tile * 128, 128), 128)
        query = qkv_ref[0, me, :, at]
        keys = qkv_ref[1, :, :, at].reshape(1024, 128)
        values = qkv_ref[2, :, :, at].reshape(1024, 128)
        outs = []
        for half in range(2):
            scores = transposed_right(keep_head(query, half), keys) * 0.125
            scores = jnp.where(key_valid, scores, masked_value)
            row_max = jnp.max(scores, axis=1, keepdims=True)
            expanded = jnp.exp(scores - row_max)
            row_sum = jnp.sum(expanded, axis=1, keepdims=True)
            outs.append(product(narrow(expanded), values) / row_sum)
            stats = jnp.where(lane == tile * 2 + half, row_max + jnp.log(row_sum), stats)
        attended_ref[:, at] = jnp.where(head_mask(0), outs[0], outs[1])
        return stats

    stats_ref[...] = lax.fori_loop(0, 6, pair, jnp.zeros((128, 128), jnp.float32))
    neighbours.finish()


def vmem(*shape, dtype=jnp.bfloat16):
    return pltpu.VMEM(shape, dtype)


def attend(length, vector, frames, weights):
    dma = pltpu.SemaphoreType.DMA
    in_vmem = pl.BlockSpec(memory_space=pltpu.VMEM)
    in_place = pl.BlockSpec(memory_space=pl.ANY)
    return pl.pallas_call(
        attend_kernel,
        out_shape=(
            jax.ShapeDtypeStruct((8, 6 * D), jnp.float32),
            jax.ShapeDtypeStruct((8, 2 * D), jnp.float32),
            jax.ShapeDtypeStruct((3, 8, 128, D), jnp.bfloat16),
            jax.ShapeDtypeStruct((128, D), jnp.float32),
            jax.ShapeDtypeStruct((128, 128), jnp.float32),
        ),
        in_specs=[pl.BlockSpec(memory_space=pltpu.SMEM), in_vmem] + [in_place] * 7,
        out_specs=(in_vmem,) * 5,
        scratch_shapes=[
            vmem(8, 128, D),
            vmem(256, D),
            vmem(D, D),
            vmem(3, D, 1536),
            vmem(3, D, D),
            dma((9,)),
            dma((1, 8)),
            dma((1, 4)),
            dma((1, 4)),
            dma((1, 4)),
        ],
        compiler_params=pltpu.CompilerParams(
            collective_id=1, has_side_effects=True, vmem_limit_bytes=VMEM_BYTES
        ),
    )(length, vector, frames, *weights)


PRODUCTS = (
    [(1 + j, 4) for j in range(4)]
    + [(0, j) for j in range(4)]
    + [(5, 5), (6, 6), (9, 8), (9, 9), (7, 7)]
    + [(8, 10), (8, 11), (8, 12)]
)
LEFTS = 9
RIGHTS = 13
TEXT_UNIT = 9
SLOTS = 4
LATER = (0, 1, 3, 5, 7, 8)
IN_VMEM = [
    "mask",
    "frames",
    "cotangent",
    "text",
    "gain",
    "mod",
    "time",
    "vector",
    "qkv",
    "attended",
    "stats",
]
IN_PLACE = [
    "hbm_out",
    "hbm_cross_query",
    "hbm_cross_key",
    "hbm_cross_value",
    "hbm_cross_out",
    "hbm_mlp_in",
    "hbm_mlp_out",
    "hbm_query",
    "hbm_key",
    "hbm_value",
    "hbm_adaln",
    "hbm_time_out",
]
OUT_VMEM = [
    "block_out",
    "grad_frames",
    "grad_text",
    "gain_sum",
    "conditions",
    "hiddens",
    "vectors",
    "grad_mods",
    "grad_time_outs",
    "grad_time_firsts",
]
OUT_PLACE = ["pieces"]


def block_scratch():
    n = len(PRODUCTS)
    sem = lambda *shape: pltpu.SemaphoreType.DMA(shape)
    f32 = jnp.float32
    return dict(
        square=vmem(9, D, D),
        mlp_in=vmem(D, 4 * D),
        mlp_out=vmem(4 * D, D),
        adaln_high=vmem(D, 2 * D),
        load_sems=sem(16),
        lefts=vmem(LEFTS, 128, D),
        gt=vmem(RIGHTS, 2, 2, 192, 128),
        grecv=vmem(RIGHTS, 2, 192, 128),
        lrecv=vmem(LEFTS, 128, D),
        pbuf=vmem(SLOTS, 2, 192, D),
        precv=vmem(n, 192, D),
        qbuf=vmem(SLOTS, 2, 192, 384),
        qrecv=vmem(n, 192, 384),
        rbuf=vmem(SLOTS, 4, PART, 384),
        rrecv=vmem(n, 4, PART, 384),
        final=vmem(n, 2, 2, PART, 384),
        ls=sem(LEFTS),
        lr=sem(LEFTS),
        gs=sem(RIGHTS),
        gr=sem(RIGHTS),
        ps=sem(n),
        pr=sem(n),
        qs=sem(n),
        qr=sem(n),
        rs=sem(n, 4),
        rr=sem(n, 4),
        fs=sem(n, 2),
        fr=sem(n, 2),
        out_sems=sem(n),
        heads=vmem(8, 128, D),
        rowstats=vmem(8, 32, 128, dtype=f32),
        sp_recv=sem(2, 8),
        sp_up=sem(2, 4),
        sp_down=sem(2, 4),
        sp_across=sem(2, 4),
        times=vmem(4, 8, 2 * D, dtype=f32),
        vecs=vmem(4, 16, 256),
        ts=sem(2, 4),
        tr=sem(2, 4),
        text_part=vmem(8, 16, D, dtype=f32),
        text_send=vmem(8, 16, D),
        text_recv=vmem(8, 16, D),
        xs=sem(8),
        xr=sem(8),
        sums=vmem(8, D, dtype=f32),
        sums_recv=vmem(8, 8, D, dtype=f32),
        ss=sem(8),
        sr=sem(8),
        clip_sums=vmem(4, 8, D, dtype=f32),
        cs=sem(4),
        cr=sem(4),
        proj=vmem(128, D, dtype=f32),
        middle=vmem(128, D, dtype=f32),
        normed_cross=vmem(128, D, dtype=f32),
        normed_mlp=vmem(128, D, dtype=f32),
        after=vmem(128, D, dtype=f32),
        pre=vmem(4, 128, D, dtype=f32),
        acc=vmem(128, D, dtype=f32),
        grad_pre=vmem(4, 128, D),
        grad_mlp=vmem(128, D),
        cross_q=vmem(128, D),
        cross_k=vmem(128, D),
        cross_v=vmem(128, D),
        cross_probs=vmem(12, 128, 128, dtype=f32),
        grad_heads=vmem(128, D),
        grad_q=vmem(128, D),
        grad_k=vmem(128, D),
        grad_v=vmem(128, D),
    )


def gelu(v):
    inner = jnp.tanh(0.7978845608028654 * (v + 0.044715 * v * v * v))
    return 0.5 * v * (1.0 + inner)


def gelu_slope(v):
    inner = jnp.tanh(0.7978845608028654 * (v + 0.044715 * v * v * v))
    return 0.5 * (1.0 + inner) + 0.5 * v * (1.0 - inner * inner) * 0.7978845608028654 * (
        1.0 + 3 * 0.044715 * v * v
    )


def silu_slope(v):
    gate = 1.0 / (1.0 + jnp.exp(-v))
    return gate * (1.0 + v * (1.0 - gate))


class Sums:
    def __init__(self, r):
        self.r = r
        self.y, self.core, self.z, self.x = y, core, z, x = places()
        self.across = device(y, core, z, 1 - x)
        self.clips = [
            None,
            device(y, 1 - core, z, x),
            device(1 - y, core, z, x),
            device(1 - y, 1 - core, z, x),
        ]
        self.done = 0

    def left_copy(self, u):
        r = self.r
        return remote(r.lefts.at[u], r.lrecv.at[u], r.ls.at[u], r.lr.at[u], self.across)

    def right_copy(self, u):
        r = self.r
        return remote(r.gt.at[u, 1 - self.x], r.grecv.at[u], r.gs.at[u], r.gr.at[u], self.across)

    def core_copy(self, i):
        r = self.r
        mine = r.pbuf.at[i % SLOTS, 1 - self.core]
        return remote(mine, r.precv.at[i], r.ps.at[i], r.pr.at[i], self.clips[1])

    def y_copy(self, i):
        r = self.r
        mine = r.qbuf.at[i % SLOTS, 1 - self.y]
        return remote(mine, r.qrecv.at[i], r.qs.at[i], r.qr.at[i], self.clips[2])

    def z_copy(self, i, k):
        r = self.r
        to = lax.rem(self.z + k, 4)
        return remote(
            r.rbuf.at[i % SLOTS, to],
            r.rrecv.at[i, k],
            r.rs.at[i, k],
            r.rr.at[i, k],
            device(self.y, self.core, to, self.x),
        )

    def last_y_copy(self, i):
        r = self.r
        piece = r.final.at[i, self.core, self.y]
        return remote(piece, piece, r.fs.at[i, 0], r.fr.at[i, 0], self.clips[2])

    def last_core_copy(self, i):
        r = self.r
        piece = r.final.at[i, self.core]
        return remote(piece, piece, r.fs.at[i, 1], r.fr.at[i, 1], self.clips[1])

    def out_copy(self, i):
        r = self.r
        return pltpu.make_async_copy(r.final.at[i], r.pieces.at[i], r.out_sems.at[i])

    def post_left(self, u, values):
        self.r.lefts[u] = values
        self.left_copy(u).start()

    def post_right(self, u, values):
        turned = narrow(jnp.transpose(values.astype(jnp.float32)))
        for s in range(8):
            for c in range(2):
                at = s * 96 + c * PART
                self.r.gt[u, s % 2, c, pl.ds((s // 2) * PART, PART), :] = turned[at : at + PART]
        self.right_copy(u).start()

    def multiply(self, i):
        r, x = self.r, self.x
        left, right = PRODUCTS[i]
        if left != TEXT_UNIT and (i == 0 or PRODUCTS[i - 1][0] != left):
            self.left_copy(left).wait_recv()
        if i == 0 or PRODUCTS[i - 1][1] != right:
            self.right_copy(right).wait_recv()
        if i >= SLOTS:
            self.core_copy(i - SLOTS).wait_send()
        for c in range(2):
            mine, theirs = r.gt[right, x, c], r.grecv[right, c]
            if left == TEXT_UNIT:
                both = narrow(mine.astype(jnp.float32) + theirs.astype(jnp.float32))
                part = product(both, r.text[...])
            else:
                part = product(
                    jnp.concatenate([mine, theirs], axis=1),
                    jnp.concatenate([r.lefts[left], r.lrecv[left]], axis=0),
                )
            r.pbuf[i % SLOTS, c] = narrow(part)
        self.core_copy(i).start()

    def add_core(self, i):
        r = self.r
        self.core_copy(i).wait_recv()
        if i >= SLOTS:
            self.y_copy(i - SLOTS).wait_send()
        total = narrow(
            r.pbuf[i % SLOTS, self.core].astype(jnp.float32) + r.precv[i].astype(jnp.float32)
        )
        r.qbuf[i % SLOTS, 0] = total[:, :384]
        r.qbuf[i % SLOTS, 1] = total[:, 384:]
        self.y_copy(i).start()

    def add_y(self, i):
        r = self.r
        self.y_copy(i).wait_recv()
        if i >= SLOTS:
            for k in (1, 2, 3):
                self.z_copy(i - SLOTS, k).wait_send()
        total = narrow(
            r.qbuf[i % SLOTS, self.y].astype(jnp.float32) + r.qrecv[i].astype(jnp.float32)
        )
        for k in range(4):
            r.rbuf[i % SLOTS, k] = total[k * PART : (k + 1) * PART]
        for k in (1, 2, 3):
            self.z_copy(i, k).start()

    def add_z(self, i):
        r = self.r
        for k in (1, 2, 3):
            self.z_copy(i, k).wait_recv()
        total = r.rbuf[i % SLOTS, self.z].astype(jnp.float32)
        for k in (1, 2, 3):
            total = total + r.rrecv[i, k].astype(jnp.float32)
        r.final[i, self.core, self.y] = narrow(total)
        self.last_y_copy(i).start()

    def pass_on(self, i):
        self.last_y_copy(i).wait_recv()
        self.last_core_copy(i).start()

    def output(self, i):
        self.last_core_copy(i).wait_recv()
        self.out_copy(i).start()

    def step(self, times=1):
        n = len(PRODUCTS)
        stages = (
            self.multiply,
            self.add_core,
            self.add_y,
            self.add_z,
            self.pass_on,
            self.output,
        )
        for unused in range(times):
            for later, stage in reversed(list(zip(LATER, stages))):
                if 0 <= self.done - later < n:
                    stage(self.done - later)
            self.done += 1

    def finish(self):
        n = len(PRODUCTS)
        while self.done < n + LATER[-1]:
            self.step()
        for u in range(LEFTS):
            self.left_copy(u).wait_send()
        for u in range(RIGHTS):
            self.right_copy(u).wait_send()
        for i in range(n):
            if i >= n - SLOTS:
                self.core_copy(i).wait_send()
                self.y_copy(i).wait_send()
                for k in (1, 2, 3):
                    self.z_copy(i, k).wait_send()
            self.last_y_copy(i).wait_send()
            self.last_core_copy(i).wait_send()
            self.out_copy(i).wait()


def block_kernel(length_ref, *refs):
    names = IN_VMEM + IN_PLACE + OUT_VMEM + OUT_PLACE + list(block_scratch())
    r = types.SimpleNamespace(**dict(zip(names, refs, strict=True)))
    y, core, z, x = places()
    me, band = z * 2 + x, y * 2 + core
    peers = [device(y, core, lax.div(s, 2), lax.rem(s, 2)) for s in [lax.rem(me + k, 8) for k in range(8)]]
    sums = Sums(r)

    def load(i, src, dst):
        return pltpu.make_async_copy(src, dst, r.load_sems.at[i])

    squares = (
        r.hbm_out,
        r.hbm_cross_query,
        r.hbm_cross_key,
        r.hbm_cross_value,
        r.hbm_cross_out,
        r.hbm_query,
        r.hbm_key,
        r.hbm_value,
        r.hbm_time_out,
    )
    OUT, CQ, CK, CV, CO, WQ, WK, WV, TIME = range(9)
    loads = [load(i, ref, r.square.at[i]) for i, ref in enumerate(squares)]
    loads.append(load(9, r.hbm_mlp_in, r.mlp_in))
    loads.append(load(10, r.hbm_mlp_out, r.mlp_out))
    loads.append(load(11, r.hbm_adaln.at[:, pl.ds(3072, 1536)], r.adaln_high))
    adaln_low = load(12, r.hbm_adaln.at[:, pl.ds(0, 3072)], r.mlp_in)
    for i in (0, 2, 3, 1, 4, 9, 10, 5, 6, 7, 8, 11):
        loads[i].start()
    greet(peers[1:] + sums.clips[1:])

    def clip_copy(refs, sems, recvs, j):
        return [
            remote(ref.at[band], ref.at[band], sems.at[i, j], recvs.at[i, j], sums.clips[j])
            for i, ref in enumerate(refs)
        ]

    r.times[band] = r.time[...]
    r.vecs[band] = r.vector[...]
    for j in (1, 2, 3):
        for copy in clip_copy((r.times, r.vecs), r.ts, r.tr, j):
            copy.start()

    length = length_ref[0]

    def row_valid():
        return lax.broadcasted_iota(jnp.int32, (128, 1), 0) + me * 128 < length

    def modulation(i):
        return r.mod[0:1, i * D : (i + 1) * D]

    def over_rows(values):
        return jnp.sum(values, axis=0, keepdims=True)

    lane = lax.broadcasted_iota(jnp.int32, (1, 128), 1)
    text_valid = r.mask[...] != 0
    gain = r.gain[...].astype(jnp.float32)

    def tile_at(tile):
        return pl.ds(pl.multiple_of(tile * 128, 128), 128)

    normed, unused = layer_norm(r.frames[...].astype(jnp.float32))
    sums.post_left(8, narrow(normed * (1.0 + modulation(1)) + modulation(0)))
    sums.post_left(7, narrow(r.attended[...]))
    r.grad_mlp[...] = narrow(
        modulation(5) * jnp.where(row_valid(), r.cotangent[...].astype(jnp.float32), 0.0)
    )
    sums.post_right(4, r.grad_mlp[...])
    loads[OUT].wait()
    r.proj[...] = product(r.lefts[7], r.square[OUT])
    r.middle[...] = r.frames[...].astype(jnp.float32) + modulation(2) * r.proj[...]
    normed, scaling_cross = layer_norm(r.middle[...])
    r.normed_cross[...] = normed
    sums.post_left(6, narrow(normed * gain))
    loads[CK].wait()
    r.cross_k[...] = narrow(product(r.text[...], r.square[CK]))
    loads[CV].wait()
    r.cross_v[...] = narrow(product(r.text[...], r.square[CV]))
    loads[CQ].wait()
    r.cross_q[...] = narrow(product(r.lefts[6], r.square[CQ]))

    def cross_pair(tile, unused):
        at = tile_at(tile)
        query, keys, values = r.cross_q[:, at], r.cross_k[:, at], r.cross_v[:, at]
        outs = []
        for half in range(2):
            scores = transposed_right(keep_head(query, half), keys) * 0.125
            scores = jnp.where(text_valid, scores, masked_value)
            row_max = jnp.max(scores, axis=1, keepdims=True)
            total = row_max + jnp.log(jnp.sum(jnp.exp(scores - row_max), axis=1, keepdims=True))
            probs = jnp.exp(scores - total)
            r.cross_probs[tile * 2 + half] = probs
            outs.append(product(narrow(probs), values))
        r.lefts[5, :, at] = narrow(jnp.where(head_mask(0), outs[0], outs[1]))
        return unused

    lax.fori_loop(0, 6, cross_pair, 0)
    sums.left_copy(5).start()
    loads[CO].wait()
    r.after[...] = r.middle[...] + product(r.lefts[5], r.square[CO])
    normed, scaling_mlp = layer_norm(r.after[...])
    r.normed_mlp[...] = normed
    sums.post_left(0, narrow(normed * (1.0 + modulation(4)) + modulation(3)))
    loads[9].wait()
    loads[10].wait()
    for j in range(4):
        pre = product(r.lefts[0], r.mlp_in[:, j * D : (j + 1) * D])
        r.pre[j] = pre
        sums.post_left(1 + j, narrow(gelu(pre)))
        part = product(r.lefts[1 + j], r.mlp_out[j * D : (j + 1) * D, :])
        r.acc[...] = part if j == 0 else r.acc[...] + part
    frames = r.frames[...].astype(jnp.float32)
    r.block_out[...] = narrow(
        jnp.where(row_valid(), r.after[...] + modulation(5) * r.acc[...], frames)
    )
    grad_res = jnp.where(row_valid(), r.cotangent[...].astype(jnp.float32), 0.0)
    r.sums[5:6, :] = over_rows(grad_res * r.acc[...])
    for j in range(4):
        slope = gelu_slope(r.pre[j])
        grad = narrow(slope * transposed_right(r.grad_mlp[...], r.mlp_out[j * D : (j + 1) * D, :]))
        r.grad_pre[j] = grad
        for part in range(2):
            s = j * 2 + part
            turned = narrow(
                jnp.transpose(grad[:, part * 384 : (part + 1) * 384].astype(jnp.float32))
            )
            for u in range(4):
                for c in range(2):
                    at = u * 96 + c * PART
                    r.gt[u, s % 2, c, pl.ds((s // 2) * PART, PART), :] = turned[at : at + PART]
    for u in range(4):
        sums.right_copy(u).start()
    for j in range(4):
        part = transposed_right(r.grad_pre[j], r.mlp_in[:, j * D : (j + 1) * D])
        r.acc[...] = part if j == 0 else r.acc[...] + part
    adaln_low.start()
    r.sums[3:4, :] = over_rows(r.acc[...])
    r.sums[4:5, :] = over_rows(r.acc[...] * r.normed_mlp[...])
    grad_res = jnp.where(row_valid(), r.cotangent[...].astype(jnp.float32), 0.0)
    r.after[...] = grad_res + norm_back(
        r.normed_mlp[...], scaling_mlp, r.acc[...] * (1.0 + modulation(4))
    )
    low = narrow(r.after[...])
    sums.post_right(5, low)
    r.grad_heads[...] = narrow(transposed_right(low, r.square[CO]))

    def cross_pair_back(tile, unused):
        at = tile_at(tile)
        query, keys, values = r.cross_q[:, at], r.cross_k[:, at], r.cross_v[:, at]
        grad = r.grad_heads[:, at]
        outs = []
        for half in range(2):
            probs = r.cross_probs[tile * 2 + half]
            grad_probs = transposed_right(keep_head(grad, half), values)
            inner = jnp.sum(probs * grad_probs, axis=1, keepdims=True)
            scores = narrow(probs * (grad_probs - inner)).astype(jnp.float32)
            outs.append(
                (
                    product(narrow(scores), keys),
                    product(narrow(jnp.transpose(scores)), query),
                    product(narrow(jnp.transpose(probs)), grad),
                )
            )
        grad_q, grad_k, grad_v = [jnp.where(head_mask(0), a, b) for a, b in zip(*outs)]
        r.grad_q[:, at] = narrow(grad_q * 0.125)
        r.grad_k[:, at] = narrow(grad_k * 0.125)
        r.grad_v[:, at] = narrow(grad_v)
        return unused

    lax.fori_loop(0, 6, cross_pair_back, 0)
    sums.post_right(6, r.grad_q[...])
    grad_cross_in = transposed_right(r.grad_q[...], r.square[CQ])
    r.sums[6:7, :] = over_rows(grad_cross_in * r.normed_cross[...])
    r.sums[7:8, :] = jnp.zeros((1, D), jnp.float32)
    r.middle[...] = r.after[...] + norm_back(
        r.normed_cross[...], scaling_cross, grad_cross_in * gain
    )
    low = narrow(modulation(2) * r.middle[...])
    grad_heads = narrow(transposed_right(low, r.square[OUT]))
    r.heads[me] = grad_heads
    products = grad_heads.astype(jnp.float32) * r.attended[...]
    delta = jnp.zeros((128, 128), jnp.float32)
    for h in range(12):
        tile = products[:, (h // 2) * 128 : (h // 2 + 1) * 128]
        inner = jnp.sum(jnp.where(head_mask(h % 2), tile, 0.0), axis=1, keepdims=True)
        delta = jnp.where(lane == h, inner, delta)
    r.rowstats[me] = jnp.concatenate(
        [jnp.transpose(r.stats[...])[:16], jnp.transpose(delta)[:16]], axis=0
    )
    spread = Spread([r.heads, r.rowstats], r.sp_recv, r.sp_up, r.sp_down, r.sp_across)
    spread.start()
    sums.post_right(7, low)
    r.sums[2:3, :] = over_rows(r.middle[...] * r.proj[...])
    sums.post_right(8, r.grad_k[...])
    sums.post_right(9, r.grad_v[...])
    text_grad = transposed_right(r.grad_k[...], r.square[CK]) + transposed_right(
        r.grad_v[...], r.square[CV]
    )
    for s in range(8):
        r.text_part[s] = text_grad[s * 16 : (s + 1) * 16]
        r.text_send[s] = narrow(text_grad[s * 16 : (s + 1) * 16])

    def text_copy(k):
        return remote(
            r.text_send.at[lax.rem(me + k, 8)], r.text_recv.at[k], r.xs.at[k], r.xr.at[k], peers[k]
        )

    for k in range(1, 8):
        text_copy(k).start()
    spread.relay(1)
    key_valid = lax.broadcasted_iota(jnp.int32, (1, 1024), 1) < length

    def query_pair(tile, unused):
        at = tile_at(tile)
        query, grad = r.qkv[0, me, :, at], r.heads[me, :, at]
        keys = r.qkv[1, :, :, at].reshape(1024, 128)
        values = r.qkv[2, :, :, at].reshape(1024, 128)
        tile_product = grad.astype(jnp.float32) * r.attended[:, at]
        outs = []
        for half in range(2):
            scores = transposed_right(keep_head(query, half), keys) * 0.125
            scores = jnp.where(key_valid, scores, masked_value)
            total = jnp.sum(
                jnp.where(lane == tile * 2 + half, r.stats[...], 0.0), axis=1, keepdims=True
            )
            inner = jnp.sum(jnp.where(head_mask(half), tile_product, 0.0), axis=1, keepdims=True)
            grad_probs = transposed_right(keep_head(grad, half), values)
            outs.append(product(narrow(jnp.exp(scores - total) * (grad_probs - inner)), keys))
        r.grad_q[:, at] = narrow(jnp.where(head_mask(0), outs[0], outs[1]) * 0.125)
        return unused

    lax.fori_loop(0, 2, query_pair, 0)
    spread.relay(2)
    lax.fori_loop(2, 4, query_pair, 0)
    spread.relay(3)
    lax.fori_loop(4, 6, query_pair, 0)
    sums.post_right(10, r.grad_q[...])
    sums.step(6)
    for row in range(4):
        spread.arrived(row * 2 + 1 - x)

    def key_pair(tile, unused):
        at = tile_at(tile)
        key, value = r.qkv[1, me, :, at], r.qkv[2, me, :, at]
        queries = r.qkv[0, :, :, at].reshape(1024, 128)
        grads = r.heads[:, :, at].reshape(1024, 128)
        outs = []
        for half in range(2):
            h = tile * 2 + half
            total = jnp.concatenate([r.rowstats[s, pl.ds(h, 1), :] for s in range(8)], axis=1)
            inner = jnp.concatenate([r.rowstats[s, pl.ds(16 + h, 1), :] for s in range(8)], axis=1)
            scores = transposed_right(keep_head(key, half), queries) * 0.125
            scores = jnp.where(row_valid(), scores, masked_value)
            probs = jnp.exp(scores - total)
            grad_probs = transposed_right(keep_head(value, half), grads)
            grad_scores = narrow(probs * (grad_probs - inner))
            outs.append((product(grad_scores, queries), product(narrow(probs), grads)))
        grad_k, grad_v = [jnp.where(head_mask(0), a, b) for a, b in zip(*outs)]
        r.grad_k[:, at] = narrow(grad_k * 0.125)
        r.grad_v[:, at] = narrow(grad_v)
        return unused

    lax.fori_loop(0, 6, key_pair, 0)
    sums.post_right(11, r.grad_k[...])
    sums.post_right(12, r.grad_v[...])
    for i in (WQ, WK, WV):
        loads[i].wait()
    grad_in = (
        transposed_right(r.grad_q[...], r.square[WQ])
        + transposed_right(r.grad_k[...], r.square[WK])
        + transposed_right(r.grad_v[...], r.square[WV])
    )
    r.acc[...] = grad_in
    normed, scaling = layer_norm(r.frames[...].astype(jnp.float32))
    r.sums[0:1, :] = over_rows(r.acc[...])
    r.sums[1:2, :] = over_rows(r.acc[...] * normed)

    def sums_copy(k):
        return remote(r.sums, r.sums_recv.at[k], r.ss.at[k], r.sr.at[k], peers[k])

    for k in range(1, 8):
        sums_copy(k).start()
    grads = r.middle[...] + norm_back(normed, scaling, r.acc[...] * (1.0 + modulation(1)))
    r.grad_frames[...] = narrow(
        jnp.where(row_valid(), grads, r.cotangent[...].astype(jnp.float32))
    )
    sums.step(4)
    total = r.sums[...]
    for k in range(1, 8):
        sums_copy(k).wait_recv()
        total = total + r.sums_recv[k]
    r.clip_sums[band] = total

    def total_copy(j):
        return remote(
            r.clip_sums.at[band], r.clip_sums.at[band], r.cs.at[j], r.cr.at[j], sums.clips[j]
        )

    for j in (1, 2, 3):
        total_copy(j).start()
    sums.step(3)
    for j in (1, 2, 3):
        total_copy(j).wait_recv()
        for copy in clip_copy((r.times, r.vecs), r.ts, r.tr, j):
            copy.wait_recv()
    r.gain_sum[0:1, :] = (r.clip_sums[0, 6:7] + r.clip_sums[1, 6:7]) + (
        r.clip_sums[2, 6:7] + r.clip_sums[3, 6:7]
    )
    r.gain_sum[1:8, :] = jnp.zeros((7, D), jnp.float32)

    def by_clip(pieces):
        return jnp.concatenate(pieces + [jnp.zeros((12, pieces[0].shape[1]), jnp.float32)], axis=0)

    for i in range(6):
        r.grad_mods[:, i * D : (i + 1) * D] = narrow(
            by_clip([r.clip_sums[b, i : i + 1] for b in range(4)])
        )
    firsts = by_clip([r.times[b, 0:1, 0:D] for b in range(4)])
    seconds = by_clip([r.times[b, 0:1, D : 2 * D] for b in range(4)])
    r.hiddens[...] = narrow(silu(firsts))
    r.conditions[...] = narrow(silu(seconds))
    for b in range(4):
        r.vectors[b] = r.vecs[b]
    adaln_low.wait()
    loads[11].wait()
    loads[TIME].wait()
    grad_condition = transposed_right(r.grad_mods[:, :3072], r.mlp_in[...]) + transposed_right(
        r.grad_mods[:, 3072:], r.adaln_high[...]
    )
    low = narrow(silu_slope(seconds) * grad_condition)
    r.grad_time_outs[...] = low
    r.grad_time_firsts[...] = silu_slope(firsts) * transposed_right(low, r.square[TIME])
    total = r.text_part[me]
    for k in range(1, 8):
        text_copy(k).wait_recv()
        total = total + r.text_recv[k].astype(jnp.float32)
    r.grad_text[...] = total
    sums.finish()
    spread.finish()
    for k in range(1, 8):
        text_copy(k).wait_send()
        sums_copy(k).wait_send()
    for j in (1, 2, 3):
        total_copy(j).wait_send()
        for copy in clip_copy((r.times, r.vecs), r.ts, r.tr, j):
            copy.wait_send()


def block(length, vmem_args, place_args):
    in_vmem = pl.BlockSpec(memory_space=pltpu.VMEM)
    in_place = pl.BlockSpec(memory_space=pl.ANY)
    shape = jax.ShapeDtypeStruct
    f32, bf16 = jnp.float32, jnp.bfloat16
    return pl.pallas_call(
        block_kernel,
        out_shape=(
            shape((128, D), bf16),
            shape((128, D), bf16),
            shape((16, D), f32),
            shape((8, D), f32),
            shape((16, D), bf16),
            shape((16, D), bf16),
            shape((4, 16, 256), bf16),
            shape((16, 6 * D), bf16),
            shape((16, D), bf16),
            shape((16, D), f32),
            shape((len(PRODUCTS), 2, 2, PART, 384), bf16),
        ),
        in_specs=[pl.BlockSpec(memory_space=pltpu.SMEM)]
        + [in_vmem] * len(IN_VMEM)
        + [in_place] * len(IN_PLACE),
        out_specs=(in_vmem,) * len(OUT_VMEM) + (in_place,) * len(OUT_PLACE),
        scratch_shapes=list(block_scratch().values()),
        compiler_params=pltpu.CompilerParams(
            collective_id=0, has_side_effects=True, vmem_limit_bytes=VMEM_BYTES
        ),
    )(length, *vmem_args, *place_args)


SQUARES = (8, 9, 12, 10, 11, 13, 14, 15)
FINAL_IN = [
    "pieces",
    "block_out",
    "grad_frames",
    "grad_text",
    "gain_sum",
    "conditions",
    "hiddens",
    "vectors",
    "grad_mods",
    "grad_time_outs",
    "grad_time_firsts",
]
FINAL_SHAPES = (
    [((128, D), jnp.bfloat16), ((128, D), jnp.bfloat16), ((16, D), jnp.float32)]
    + [((96, 256), jnp.float32), ((96, D), jnp.float32), ((576, D), jnp.float32)]
    + [((1, 96), jnp.float32), ((D, 384), jnp.float32), ((96, 4 * D), jnp.float32)]
    + [((96, D), jnp.float32)] * 8
)


def final_kernel(*refs):
    r = types.SimpleNamespace(**dict(zip(FINAL_IN, refs)))
    count = len(FINAL_SHAPES)
    rest = refs[len(FINAL_IN) :]
    outs, staged, (turned_mods, turned_small, sems) = rest[:count], rest[count : 2 * count], rest[2 * count :]
    seq = lax.axis_index("seq")

    def put(i, values):
        staged[i][...] = values
        copy(i).start()

    def copy(i):
        return pltpu.make_async_copy(staged[i], outs[i], sems.at[i])

    def whole(p):
        return jnp.concatenate(
            [jnp.concatenate([r.pieces[p, c, h] for h in range(2)], axis=1) for c in range(2)],
            axis=0,
        ).astype(jnp.float32)

    put(7, jnp.transpose(jnp.concatenate([whole(4 + j) for j in range(4)], axis=0)))
    for j in range(4):
        staged[8][:, j * D : (j + 1) * D] = whole(j)
    copy(8).start()
    for j, p in enumerate(SQUARES):
        put(9 + j, whole(p))
    put(0, r.block_out[...])
    put(1, r.grad_frames[...])
    put(2, r.grad_text[...])
    turned_mods[...] = jnp.transpose(r.grad_mods[...].astype(jnp.float32))
    put(
        5,
        product(
            narrow(turned_mods[pl.ds(pl.multiple_of(seq * 576, 64), 576), :]), r.conditions[...]
        ),
    )
    own = pl.ds(pl.multiple_of(seq * 96, 32), 96)
    turned_small[0] = jnp.transpose(r.grad_time_outs[...].astype(jnp.float32))
    put(4, product(narrow(turned_small[0, own, :]), r.hiddens[...]))
    turned_small[1] = jnp.transpose(r.grad_time_firsts[...])
    rows = [r.vectors[b, 0:1].astype(jnp.float32) for b in range(4)]
    vectors = jnp.concatenate(rows + [jnp.zeros((12, 256), jnp.float32)], axis=0)
    put(
        3,
        jnp.dot(
            turned_small[1, own, :],
            vectors,
            precision=lax.Precision.HIGHEST,
            preferred_element_type=jnp.float32,
        ),
    )
    gains = jnp.concatenate([r.gain_sum[...], jnp.zeros((8, D), jnp.float32)], axis=0)
    turned_small[2] = jnp.transpose(gains)
    put(6, jnp.transpose(turned_small[2, own, :])[0:1])
    for i in range(count):
        copy(i).wait()


def finish(values):
    in_vmem = pl.BlockSpec(memory_space=pltpu.VMEM)
    in_place = pl.BlockSpec(memory_space=pl.ANY)
    return pl.pallas_call(
        final_kernel,
        out_shape=tuple(jax.ShapeDtypeStruct(*shape) for shape in FINAL_SHAPES),
        in_specs=[in_vmem] * len(FINAL_IN),
        out_specs=(in_place,) * len(FINAL_SHAPES),
        scratch_shapes=[pltpu.VMEM(*shape) for shape in FINAL_SHAPES]
        + [
            vmem(6 * D, 16, dtype=jnp.float32),
            vmem(3, D, 16, dtype=jnp.float32),
            pltpu.SemaphoreType.DMA((len(FINAL_SHAPES),)),
        ],
        compiler_params=pltpu.CompilerParams(vmem_limit_bytes=VMEM_BYTES),
    )(*values)


def on_device(
    frames,
    text,
    timesteps,
    frame_lengths,
    text_mask,
    cotangent,
    w_time_in,
    w_time_out,
    w_adaln,
    w_query,
    w_key,
    w_value,
    w_attn_out,
    cross_gain,
    w_cross_query,
    w_cross_key,
    w_cross_value,
    w_cross_out,
    w_mlp_in,
    w_mlp_out,
):
    vector = jnp.broadcast_to(narrow(time_embed(timesteps, w_time_in.shape[0])), (16, 256))
    mod, time, qkv, attended, stats = attend(
        frame_lengths,
        vector,
        frames[0],
        (w_time_in, w_time_out, w_adaln, w_query, w_key, w_value),
    )
    (
        block_out,
        grad_frames,
        grad_text,
        gain_sum,
        conditions,
        hiddens,
        vectors,
        grad_mods,
        grad_time_outs,
        grad_time_firsts,
        pieces,
    ) = block(
        frame_lengths,
        (
            text_mask,
            frames[0],
            cotangent[0],
            text[0],
            cross_gain[None],
            mod,
            time,
            vector,
            qkv,
            attended,
            stats,
        ),
        (
            w_attn_out,
            w_cross_query,
            w_cross_key,
            w_cross_value,
            w_cross_out,
            w_mlp_in,
            w_mlp_out,
            w_query,
            w_key,
            w_value,
            w_adaln,
            w_time_out,
        ),
    )
    (
        block_out,
        grad_frames,
        grad_text,
        sum_time_in,
        sum_time_out,
        sum_adaln,
        sum_gain,
        sum_mlp_in,
        sum_mlp_out,
        sum_cross_out,
        sum_cross_query,
        sum_attn_out,
        sum_cross_key,
        sum_cross_value,
        sum_query,
        sum_key,
        sum_value,
    ) = finish(
        (
            pieces,
            block_out,
            grad_frames,
            grad_text,
            gain_sum,
            conditions,
            hiddens,
            vectors,
            grad_mods,
            grad_time_outs,
            grad_time_firsts,
        )
    )
    return (
        block_out[None],
        grad_frames[None],
        grad_text[None],
        sum_time_in.T,
        sum_time_out.T,
        sum_adaln.T,
        sum_query.T,
        sum_key.T,
        sum_value.T,
        sum_attn_out.T,
        sum_gain[0],
        sum_cross_query.T,
        sum_cross_key.T,
        sum_cross_value.T,
        sum_cross_out.T,
        sum_mlp_in,
        sum_mlp_out.T,
    )


def on_device_general(
    frames,
    text,
    timesteps,
    frame_lengths,
    text_mask,
    cotangent,
    w_time_in,
    w_time_out,
    w_adaln,
    w_query,
    w_key,
    w_value,
    w_attn_out,
    cross_gain,
    w_cross_query,
    w_cross_key,
    w_cross_value,
    w_cross_out,
    w_mlp_in,
    w_mlp_out,
):
    clips = frames.shape[0]
    rows = frames.shape[1]
    width = frames.shape[2]
    tokens = clips * rows
    text_count = text.shape[1]
    seq_place = lax.axis_index("seq")
    seq_count = lax.axis_size("seq")
    offset = seq_place * rows
    inputs = frames.astype(jnp.float32)
    own_valid = (offset + jnp.arange(rows))[None, :] < frame_lengths[:, None]
    row_valid = own_valid[:, :, None]
    text_valid = text_mask != 0

    def flatten(values):
        return values.reshape(tokens, values.shape[-1])

    def unflatten(values):
        return values.reshape(clips, rows, values.shape[-1])

    time_vector = narrow(time_embed(timesteps, w_time_in.shape[0]))
    time_first = product(time_vector, w_time_in)
    time_hidden = narrow(jax.nn.silu(time_first))
    time_out = product(time_hidden, w_time_out)
    condition = narrow(jax.nn.silu(time_out))
    modulation = product(condition, w_adaln)
    shift_attn, scale_attn, gate_attn, shift_mlp, scale_mlp, gate_mlp = [
        piece[:, None, :] for piece in jnp.split(modulation, 6, axis=1)
    ]
    normed_attn, scaling_attn = layer_norm(inputs)
    attn_in = narrow(normed_attn * (1.0 + scale_attn) + shift_attn)
    attn_flat = flatten(attn_in)
    query_flat = narrow(product(attn_flat, w_query))
    queries = split_heads(unflatten(query_flat))
    kv_local = unflatten(
        jnp.concatenate(
            [narrow(product(attn_flat, w_key)), narrow(product(attn_flat, w_value))], axis=1
        )
    )
    start_state = (
        jnp.full((clips, rows, H), -1e30, jnp.float32),
        jnp.zeros((clips, rows, H), jnp.float32),
        jnp.zeros((clips, rows, H, HD), jnp.float32),
    )
    row_max, row_sum, weighted = forward_piece(
        start_state,
        lax.all_gather(kv_local, "seq", axis=1, tiled=True),
        jnp.int32(0),
        queries,
        frame_lengths,
    )
    attended = weighted / row_sum[..., None]
    log_total = row_max + jnp.log(row_sum)
    attn_low = narrow(attended.reshape(clips, rows, width))
    attn_proj = unflatten(product(flatten(attn_low), w_attn_out))
    middle = inputs + gate_attn * attn_proj
    normed_cross, scaling_cross = layer_norm(middle)
    gain_values = cross_gain.astype(jnp.float32)
    cross_in = narrow(normed_cross * gain_values)
    cross_queries = split_heads(unflatten(narrow(product(flatten(cross_in), w_cross_query))))
    text_flat = text.reshape(clips * text_count, width)
    cross_keys = split_heads(
        narrow(product(text_flat, w_cross_key)).reshape(clips, text_count, width)
    )
    cross_values = split_heads(
        narrow(product(text_flat, w_cross_value)).reshape(clips, text_count, width)
    )
    cross_scores = masked_scores(cross_queries, cross_keys, text_valid)
    cross_max = jnp.max(cross_scores, axis=-1, keepdims=True)
    cross_total = cross_max + jnp.log(
        jnp.sum(jnp.exp(cross_scores - cross_max), axis=-1, keepdims=True)
    )
    cross_probs = jnp.exp(cross_scores - cross_total)
    cross_probs_low = narrow(cross_probs)
    cross_attended = jnp.einsum(
        "cqhk,ckhd->cqhd", cross_probs_low, cross_values, preferred_element_type=jnp.float32
    )
    cross_low = narrow(cross_attended.reshape(clips, rows, width))
    after_cross = middle + unflatten(product(flatten(cross_low), w_cross_out))
    normed_mlp, scaling_mlp = layer_norm(after_cross)
    mlp_in = narrow(normed_mlp * (1.0 + scale_mlp) + shift_mlp)
    pre_act = product(flatten(mlp_in), w_mlp_in)
    activation = narrow(jax.nn.gelu(pre_act, approximate=True))
    mlp_out = unflatten(product(activation, w_mlp_out))
    result = after_cross + gate_mlp * mlp_out
    block_out = jnp.where(row_valid, result, inputs).astype(jnp.bfloat16)
    grad_out = cotangent.astype(jnp.float32)
    grad_res = jnp.where(row_valid, grad_out, 0.0)
    grad_mlp = flatten(narrow(gate_mlp * grad_res))
    grad_w_mlp_out = transposed_left(activation, grad_mlp)
    grad_act = transposed_right(grad_mlp, w_mlp_out)
    gelu_pull = jax.vjp(lambda values: jax.nn.gelu(values, approximate=True), pre_act)[1]
    grad_pre = narrow(gelu_pull(grad_act)[0])
    grad_w_mlp_in = transposed_left(flatten(mlp_in), grad_pre)
    grad_mlp_in = unflatten(transposed_right(grad_pre, w_mlp_in))
    grad_after = grad_res + norm_back(normed_mlp, scaling_mlp, grad_mlp_in * (1.0 + scale_mlp))
    grad_cross_out = flatten(narrow(grad_after))
    grad_w_cross_out = transposed_left(flatten(cross_low), grad_cross_out)
    grad_cross_attn = split_heads(unflatten(narrow(transposed_right(grad_cross_out, w_cross_out))))
    cross_delta = jnp.sum(grad_cross_attn.astype(jnp.float32) * cross_attended, axis=-1)
    cross_grad_probs = jnp.einsum(
        "cqhd,ckhd->cqhk", grad_cross_attn, cross_values, preferred_element_type=jnp.float32
    )
    cross_grad_scores = narrow(cross_probs * (cross_grad_probs - cross_delta[..., None]))
    grad_cross_query = narrow(
        jnp.einsum(
            "cqhk,ckhd->cqhd", cross_grad_scores, cross_keys, preferred_element_type=jnp.float32
        )
        * 0.125
    ).reshape(tokens, width)
    cross_key_part = (
        jnp.einsum(
            "cqhk,cqhd->ckhd", cross_grad_scores, cross_queries, preferred_element_type=jnp.float32
        )
        * 0.125
    )
    cross_value_part = jnp.einsum(
        "cqhk,cqhd->ckhd", cross_probs_low, grad_cross_attn, preferred_element_type=jnp.float32
    )
    cross_kv_part = jnp.concatenate(
        [
            cross_key_part.reshape(clips, text_count, width),
            cross_value_part.reshape(clips, text_count, width),
        ],
        axis=2,
    )
    text_total = lax.psum_scatter(cross_kv_part, "seq", scatter_dimension=1, tiled=True)
    text_share = text_total.shape[1]
    grad_cross_key = narrow(text_total[:, :, :width]).reshape(clips * text_share, width)
    grad_cross_value = narrow(text_total[:, :, width:]).reshape(clips * text_share, width)
    text_own = lax.dynamic_slice_in_dim(text, seq_place * text_share, text_share, 1).reshape(
        clips * text_share, width
    )
    grad_text = (
        transposed_right(grad_cross_key, w_cross_key)
        + transposed_right(grad_cross_value, w_cross_value)
    ).reshape(clips, text_share, width)
    grad_w_cross_key = transposed_left(text_own, grad_cross_key)
    grad_w_cross_value = transposed_left(text_own, grad_cross_value)
    grad_w_cross_query = transposed_left(flatten(cross_in), grad_cross_query)
    grad_cross_in = unflatten(transposed_right(grad_cross_query, w_cross_query))
    grad_gain_part = jnp.sum(grad_cross_in * normed_cross, axis=(0, 1))
    grad_mid = grad_after + norm_back(normed_cross, scaling_cross, grad_cross_in * gain_values)
    grad_attn_proj = flatten(narrow(gate_attn * grad_mid))
    grad_w_attn_out = transposed_left(flatten(attn_low), grad_attn_proj)
    grad_attn_flat = narrow(transposed_right(grad_attn_proj, w_attn_out))
    grad_heads = split_heads(unflatten(grad_attn_flat))
    row_delta = jnp.sum(grad_heads.astype(jnp.float32) * attended, axis=-1)
    zero_heads = jnp.zeros((clips, rows, H, HD), jnp.float32)
    gathered = lax.all_gather(kv_local, "seq", axis=1, tiled=True)
    query_grad = query_piece(
        zero_heads, gathered, 0, queries, grad_heads, log_total, row_delta, frame_lengths
    )
    anchor = jnp.int32(0)
    block_size = math.gcd(rows * lax.axis_size("seq"), key_block)

    def key_one_block(counter):
        rows_in = lax.dynamic_slice_in_dim(gathered, counter * block_size, block_size, 1)
        key_valid = block_valid(anchor, counter * block_size, block_size, frame_lengths)
        scores = masked_scores(queries, split_heads(rows_in[:, :, :width]), key_valid)
        attn_probs = jnp.exp(scores - log_total[..., None])
        grad_probs = jnp.einsum(
            "cqhd,ckhd->cqhk",
            grad_heads,
            split_heads(rows_in[:, :, width:]),
            preferred_element_type=jnp.float32,
        )
        grad_scores = narrow(attn_probs * (grad_probs - row_delta[..., None]))
        grad_keys = (
            jnp.einsum("cqhk,cqhd->ckhd", grad_scores, queries, preferred_element_type=jnp.float32)
            * 0.125
        )
        grad_values = jnp.einsum(
            "cqhk,cqhd->ckhd", narrow(attn_probs), grad_heads, preferred_element_type=jnp.float32
        )
        joined = jnp.concatenate(
            [
                grad_keys.reshape(clips, block_size, width),
                grad_values.reshape(clips, block_size, width),
            ],
            axis=2,
        )
        return jnp.transpose(joined, (1, 0, 2))

    blocks = lax.map(key_one_block, jnp.arange(rows * lax.axis_size("seq") // block_size))
    kv_term = lax.psum_scatter(
        blocks.reshape(rows * lax.axis_size("seq"), clips, 2 * width),
        "seq",
        scatter_dimension=0,
        tiled=True,
    )
    kv_grad = jnp.transpose(kv_term, (1, 0, 2))
    grad_query = narrow(query_grad.reshape(tokens, width))
    grad_key = flatten(narrow(kv_grad[:, :, :width]))
    grad_value = flatten(narrow(kv_grad[:, :, width:]))
    grad_w_query = transposed_left(attn_flat, grad_query)
    grad_w_key = transposed_left(attn_flat, grad_key)
    grad_w_value = transposed_left(attn_flat, grad_value)
    grad_attn_in = unflatten(
        transposed_right(grad_query, w_query)
        + transposed_right(grad_key, w_key)
        + transposed_right(grad_value, w_value)
    )
    grad_inputs = grad_mid + norm_back(normed_attn, scaling_attn, grad_attn_in * (1.0 + scale_attn))
    grad_frames = jnp.where(row_valid, grad_inputs, grad_out).astype(jnp.bfloat16)
    modulation_part = jnp.concatenate(
        [
            jnp.sum(grad_attn_in, axis=1),
            jnp.sum(grad_attn_in * normed_attn, axis=1),
            jnp.sum(grad_mid * attn_proj, axis=1),
            jnp.sum(grad_mlp_in, axis=1),
            jnp.sum(grad_mlp_in * normed_mlp, axis=1),
            jnp.sum(grad_res * mlp_out, axis=1),
        ],
        axis=1,
    )
    modulation_total = lax.psum(modulation_part, "seq")
    grad_modulation = narrow(modulation_total)
    grad_w_adaln = transposed_left(condition, grad_modulation)
    grad_condition = transposed_right(grad_modulation, w_adaln)
    grad_time_out = narrow(jax.vjp(jax.nn.silu, time_out)[1](grad_condition)[0])
    grad_w_time_out = transposed_left(time_hidden, grad_time_out)
    grad_time_hidden = transposed_right(grad_time_out, w_time_out)
    grad_time_first = jax.vjp(jax.nn.silu, time_first)[1](grad_time_hidden)[0]
    grad_w_time_in = lax.dot_general(
        time_vector.astype(jnp.float32),
        grad_time_first,
        (((0,), (0,)), ((), ())),
        precision=lax.Precision.HIGHEST,
    )
    shared = (
        lax.psum_scatter(grad_w_query, "seq", scatter_dimension=1, tiled=True),
        lax.psum_scatter(grad_w_key, "seq", scatter_dimension=1, tiled=True),
        lax.psum_scatter(grad_w_value, "seq", scatter_dimension=1, tiled=True),
        lax.psum_scatter(grad_w_attn_out, "seq", scatter_dimension=1, tiled=True),
        lax.psum_scatter(grad_gain_part, "seq", scatter_dimension=0, tiled=True),
        lax.psum_scatter(grad_w_cross_query, "seq", scatter_dimension=1, tiled=True),
        lax.psum_scatter(grad_w_cross_key, "seq", scatter_dimension=1, tiled=True),
        lax.psum_scatter(grad_w_cross_value, "seq", scatter_dimension=1, tiled=True),
        lax.psum_scatter(grad_w_cross_out, "seq", scatter_dimension=1, tiled=True),
        lax.psum_scatter(grad_w_mlp_in, "seq", scatter_dimension=1, tiled=True),
        lax.psum_scatter(grad_w_mlp_out, "seq", scatter_dimension=1, tiled=True),
    )
    replicated = (
        own_columns(grad_w_time_in, seq_place, seq_count),
        own_columns(grad_w_time_out, seq_place, seq_count),
        own_columns(grad_w_adaln, seq_place, seq_count),
    )
    summed = jax.tree.map(
        lambda part: part.astype(jnp.float32), lax.psum(for_sending(shared + replicated), "band")
    )
    (
        sum_query,
        sum_key,
        sum_value,
        sum_attn_out,
        sum_gain,
        sum_cross_query,
        sum_cross_key,
        sum_cross_value,
        sum_cross_out,
        sum_mlp_in,
        sum_mlp_out,
        sum_time_in,
        sum_time_out,
        sum_adaln,
    ) = summed
    return (
        block_out,
        grad_frames,
        grad_text,
        sum_time_in,
        sum_time_out,
        sum_adaln,
        sum_query,
        sum_key,
        sum_value,
        sum_attn_out,
        sum_gain,
        sum_cross_query,
        sum_cross_key,
        sum_cross_value,
        sum_cross_out,
        sum_mlp_in,
        sum_mlp_out,
    )


def solution(mesh):
    placed = (
        P("band", "seq", None),
        P("band", None, None),
        P("band"),
        P("band"),
        P("band", None),
        P("band", "seq", None),
        P(),
        P(),
        P(),
        P(),
        P(),
        P(),
        P(),
        P(),
        P(),
        P(),
        P(),
        P(),
        P(),
        P(),
    )
    paired = mesh.shape["band"] == 4 and mesh.shape["seq"] == 8
    return jax.shard_map(
        on_device if paired else on_device_general,
        mesh=mesh,
        in_specs=placed,
        out_specs=(
            P("band", "seq", None),
            P("band", "seq", None),
            P("band", "seq", None),
            P(None, "seq"),
            P(None, "seq"),
            P(None, "seq"),
            P(None, "seq"),
            P(None, "seq"),
            P(None, "seq"),
            P(None, "seq"),
            P("seq"),
            P(None, "seq"),
            P(None, "seq"),
            P(None, "seq"),
            P(None, "seq"),
            P(None, "seq"),
            P(None, "seq"),
        ),
        check_vma=False,
    )
```

```python
import math
import types

import jax
import jax.numpy as jnp
from jax import lax
from jax.experimental import pallas as pl
from jax.experimental.pallas import tpu as pltpu
from jax.sharding import PartitionSpec as P

H = 12
HD = 64


epsilon = 1e-06
masked_value = -1000000000.0
key_block = 512


def for_sending(value):
    return jax.tree.map(lambda a: a.astype(jnp.bfloat16) if a.dtype == jnp.float32 else a, value)


def narrow(values):
    return values.astype(jnp.bfloat16)


def product(left, right):
    return jnp.dot(left, right, preferred_element_type=jnp.float32)


def transposed_left(left, right):
    return lax.dot_general(
        left, right, (((0,), (0,)), ((), ())), preferred_element_type=jnp.float32
    )


def transposed_right(left, right):
    return lax.dot_general(
        left, right, (((1,), (1,)), ((), ())), preferred_element_type=jnp.float32
    )


def layer_norm(inputs):
    center = inputs - jnp.mean(inputs, axis=-1, keepdims=True)
    scaling = lax.rsqrt(jnp.mean(center * center, axis=-1, keepdims=True) + epsilon)
    return (center * scaling, scaling)


def norm_back(normed, scaling, gradient):
    mean_grad = jnp.mean(gradient, axis=-1, keepdims=True)
    mean_prod = jnp.mean(gradient * normed, axis=-1, keepdims=True)
    return scaling * (gradient - mean_grad - normed * mean_prod)


def time_embed(timesteps, width):
    half_width = width // 2
    frequency = jnp.exp(-math.log(10000.0) * jnp.arange(half_width, dtype=jnp.float32) / half_width)
    angles = timesteps.astype(jnp.float32)[:, None] * frequency[None, :]
    return jnp.concatenate([jnp.cos(angles), jnp.sin(angles)], axis=1)


def split_heads(rows_in):
    return rows_in.reshape(rows_in.shape[0], rows_in.shape[1], H, HD)


def masked_scores(queries, key_rows, key_valid):
    scores = (
        jnp.einsum("cqhd,ckhd->cqhk", queries, key_rows, preferred_element_type=jnp.float32) * 0.125
    )
    return jnp.where(key_valid[:, None, None, :], scores, masked_value)


def block_valid(anchor, start_row, block_size, lengths):
    return (anchor + start_row + jnp.arange(block_size))[None, :] < lengths[:, None]


def forward_piece(running, segment, anchor, queries, lengths):
    row_count = segment.shape[1]
    block_size = math.gcd(row_count, key_block)
    width = queries.shape[2] * queries.shape[3]

    def forward_one_block(running, counter):
        rows_in = lax.dynamic_slice_in_dim(segment, counter * block_size, block_size, 1)
        key_valid = block_valid(anchor, counter * block_size, block_size, lengths)
        scores = masked_scores(queries, split_heads(rows_in[:, :, :width]), key_valid)
        row_max, row_sum, weighted = running
        new_max = jnp.maximum(row_max, jnp.max(scores, axis=-1))
        factor = jnp.exp(row_max - new_max)
        expanded = jnp.exp(scores - new_max[..., None])
        row_sum = row_sum * factor + jnp.sum(expanded, axis=-1)
        weighted = weighted * factor[..., None] + jnp.einsum(
            "cqhk,ckhd->cqhd",
            narrow(expanded),
            split_heads(rows_in[:, :, width:]),
            preferred_element_type=jnp.float32,
        )
        return ((new_max, row_sum, weighted), None)

    running, unused = lax.scan(forward_one_block, running, jnp.arange(row_count // block_size))
    return running


def query_piece(gradient, segment, anchor, queries, grad_heads, log_total, row_delta, lengths):
    row_count = segment.shape[1]
    block_size = math.gcd(row_count, key_block)
    width = queries.shape[2] * queries.shape[3]

    def query_one_block(gradient, counter):
        rows_in = lax.dynamic_slice_in_dim(segment, counter * block_size, block_size, 1)
        key_valid = block_valid(anchor, counter * block_size, block_size, lengths)
        key_rows = split_heads(rows_in[:, :, :width])
        scores = masked_scores(queries, key_rows, key_valid)
        attn_probs = jnp.exp(scores - log_total[..., None])
        grad_probs = jnp.einsum(
            "cqhd,ckhd->cqhk",
            grad_heads,
            split_heads(rows_in[:, :, width:]),
            preferred_element_type=jnp.float32,
        )
        grad_scores = narrow(attn_probs * (grad_probs - row_delta[..., None]))
        gradient = (
            gradient
            + jnp.einsum(
                "cqhk,ckhd->cqhd", grad_scores, key_rows, preferred_element_type=jnp.float32
            )
            * 0.125
        )
        return (gradient, None)

    gradient, unused = lax.scan(query_one_block, gradient, jnp.arange(row_count // block_size))
    return gradient


def own_columns(values, place, count):
    share = values.shape[1] // count
    return lax.dynamic_slice_in_dim(values, place * share, share, 1)


MESH = pl.DeviceIdType.MESH
D = 768
PART = 48
VMEM_BYTES = 66500 * 1000


def places():
    band, seq = lax.axis_index("band"), lax.axis_index("seq")
    return lax.div(band, 2), lax.rem(band, 2), lax.div(seq, 2), lax.rem(seq, 2)


def device(y, core, z, x):
    return (y * 2 + core, z * 2 + x)


def remote(src, dst, send, recv, target):
    return pltpu.make_async_remote_copy(
        src_ref=src, dst_ref=dst, send_sem=send, recv_sem=recv, device_id=target, device_id_type=MESH
    )


def greet(partners):
    barrier = pltpu.get_barrier_semaphore()
    for partner in partners:
        pl.semaphore_signal(barrier, inc=1, device_id=partner, device_id_type=MESH)
    pl.semaphore_wait(barrier, len(partners))


class Spread:
    def __init__(self, buffers, recv, up, down, across):
        self.buffers, self.recv, self.up, self.down, self.across = buffers, recv, up, down, across
        self.y, self.core, self.z, self.x = places()

    def copies(self, slot, sems, at, target):
        return [
            remote(buf.at[slot], buf.at[slot], sems.at[i, at], self.recv.at[i, slot], target)
            for i, buf in enumerate(self.buffers)
        ]

    def to_up(self, k):
        return self.copies(
            (self.z - k) * 2 + self.x, self.up, k, device(self.y, self.core, self.z + 1, self.x)
        )

    def to_down(self, k):
        return self.copies(
            (self.z + k) * 2 + self.x, self.down, k, device(self.y, self.core, self.z - 1, self.x)
        )

    def to_across(self, row):
        return self.copies(
            row * 2 + self.x, self.across, row, device(self.y, self.core, self.z, 1 - self.x)
        )

    def arrived(self, slot):
        for copy in self.copies(slot, self.across, 0, device(self.y, self.core, self.z, 1 - self.x)):
            copy.wait_recv()

    def start(self):
        z = self.z

        @pl.when(z < 3)
        def _():
            for copy in self.to_up(0):
                copy.start()

        @pl.when(z > 0)
        def _():
            for copy in self.to_down(0):
                copy.start()

        for copy in self.to_across(z):
            copy.start()

    def relay(self, k):
        z = self.z

        @pl.when(z >= k)
        def _():
            self.arrived((z - k) * 2 + self.x)

            @pl.when(z < 3)
            def _():
                for copy in self.to_up(k):
                    copy.start()

            for copy in self.to_across(z - k):
                copy.start()

        @pl.when(z + k <= 3)
        def _():
            self.arrived((z + k) * 2 + self.x)

            @pl.when(z > 0)
            def _():
                for copy in self.to_down(k):
                    copy.start()

            for copy in self.to_across(z + k):
                copy.start()

    def finish(self):
        z = self.z
        for k in range(4):

            @pl.when((z >= k) & (z < 3))
            def _():
                for copy in self.to_up(k):
                    copy.wait_send()

            @pl.when((z + k <= 3) & (z > 0))
            def _():
                for copy in self.to_down(k):
                    copy.wait_send()

            for copy in self.to_across(k):
                copy.wait_send()


def silu(values):
    return values / (1.0 + jnp.exp(-values))


def head_mask(half):
    lane = lax.broadcasted_iota(jnp.int32, (1, 128), 1)
    return (lane < 64) if half == 0 else (lane >= 64)


def keep_head(tile, half):
    return jnp.where(head_mask(half), tile, jnp.zeros_like(tile))


def vmem(*shape, dtype=jnp.bfloat16):
    return pltpu.VMEM(shape, dtype)

PRODUCTS = (
    [(1 + j, 4) for j in range(4)]
    + [(0, j) for j in range(4)]
    + [(5, 5), (6, 6), (9, 8), (9, 9), (7, 7)]
    + [(8, 10), (8, 11), (8, 12)]
)
LEFTS = 8
RIGHTS = 13
TEXT_UNIT = 9
SLOTS = 4
LATER = (0, 1, 3, 5, 7, 8)
IN_VMEM = [
    "mask",
    "frames",
    "cotangent",
    "text",
    "gain",
    "vector",
]
IN_PLACE = [
    "hbm_out",
    "hbm_cross_query",
    "hbm_cross_key",
    "hbm_cross_value",
    "hbm_cross_out",
    "hbm_mlp_in",
    "hbm_mlp_out",
    "hbm_query",
    "hbm_key",
    "hbm_value",
    "hbm_adaln",
    "hbm_time_out",
    "hbm_time_in",
]
OUT_VMEM = [
    "block_out",
    "grad_frames",
    "grad_text",
    "gain_sum",
    "conditions",
    "hiddens",
    "vectors",
    "grad_mods",
    "grad_time_outs",
    "grad_time_firsts",
]
OUT_PLACE = ["pieces"]


def block_scratch():
    n = len(PRODUCTS)
    sem = lambda *shape: pltpu.SemaphoreType.DMA(shape)
    f32 = jnp.float32
    return dict(
        mod=vmem(8, 6 * D, dtype=f32),
        time=vmem(8, 2 * D, dtype=f32),
        qkv=vmem(3, 8, 128, D),
        attended=vmem(128, D, dtype=f32),
        pair=vmem(2, 128, D),
        stats=vmem(128, 128, dtype=f32),
        gathered=vmem(8, 128, D),
        time_in=vmem(256, D),
        fr_recv=sem(1, 8),
        fr_up=sem(1, 4),
        fr_down=sem(1, 4),
        fr_across=sem(1, 4),
        square=vmem(9, D, D),
        mlp_in=vmem(D, 4 * D),
        mlp_out=vmem(4 * D, D),
        adaln_high=vmem(D, 2 * D),
        load_sems=sem(16),
        lefts=vmem(LEFTS, 128, D),
        gt=vmem(RIGHTS, 2, 2, 192, 128),
        grecv=vmem(RIGHTS, 2, 192, 128),
        lrecv=vmem(LEFTS, 128, D),
        pbuf=vmem(SLOTS, 2, 192, D),
        precv=vmem(n, 192, D),
        qbuf=vmem(SLOTS, 2, 192, 384),
        qrecv=vmem(n, 192, 384),
        rbuf=vmem(SLOTS, 4, PART, 384),
        rrecv=vmem(n, 4, PART, 384),
        final=vmem(n, 2, 2, PART, 384),
        ls=sem(LEFTS),
        lr=sem(LEFTS),
        gs=sem(RIGHTS),
        gr=sem(RIGHTS),
        ps=sem(n),
        pr=sem(n),
        qs=sem(n),
        qr=sem(n),
        rs=sem(n, 4),
        rr=sem(n, 4),
        fs=sem(n, 2),
        fr=sem(n, 2),
        out_sems=sem(n),
        heads=vmem(8, 128, D),
        rowstats=vmem(8, 32, 128, dtype=f32),
        sp_recv=sem(2, 8),
        sp_up=sem(2, 4),
        sp_down=sem(2, 4),
        sp_across=sem(2, 4),
        times=vmem(4, 8, 2 * D, dtype=f32),
        vecs=vmem(4, 16, 256),
        ts=sem(2, 4),
        tr=sem(2, 4),
        text_part=vmem(8, 16, D, dtype=f32),
        text_send=vmem(8, 16, D),
        text_recv=vmem(8, 16, D),
        xs=sem(8),
        xr=sem(8),
        sums=vmem(8, D, dtype=f32),
        sums_recv=vmem(8, 8, D, dtype=f32),
        ss=sem(8),
        sr=sem(8),
        clip_sums=vmem(4, 8, D, dtype=f32),
        cs=sem(4),
        cr=sem(4),
        proj=vmem(128, D, dtype=f32),
        middle=vmem(128, D, dtype=f32),
        normed_cross=vmem(128, D, dtype=f32),
        normed_mlp=vmem(128, D, dtype=f32),
        after=vmem(128, D, dtype=f32),
        pre=vmem(4, 128, D, dtype=f32),
        acc=vmem(128, D, dtype=f32),
        grad_mlp=vmem(128, D),
        cross_probs=vmem(12, 128, 128, dtype=f32),
        grad_q=vmem(128, D),
        grad_k=vmem(128, D),
        grad_v=vmem(128, D),
    )


def gelu(v):
    inner = jnp.tanh(0.7978845608028654 * (v + 0.044715 * v * v * v))
    return 0.5 * v * (1.0 + inner)


def gelu_slope(v):
    inner = jnp.tanh(0.7978845608028654 * (v + 0.044715 * v * v * v))
    return 0.5 * (1.0 + inner) + 0.5 * v * (1.0 - inner * inner) * 0.7978845608028654 * (
        1.0 + 3 * 0.044715 * v * v
    )


def silu_slope(v):
    gate = 1.0 / (1.0 + jnp.exp(-v))
    return gate * (1.0 + v * (1.0 - gate))


class Sums:
    def __init__(self, r):
        self.r = r
        self.y, self.core, self.z, self.x = y, core, z, x = places()
        self.across = device(y, core, z, 1 - x)
        self.high, self.low = lax.div(z, 2), lax.rem(z, 2)
        self.along = device(y, core, 2 * self.high + 1 - self.low, x)
        self.clips = [
            None,
            device(y, 1 - core, z, x),
            device(1 - y, core, z, x),
            device(1 - y, 1 - core, z, x),
        ]
        self.done = 0

    def left_copy(self, u):
        r = self.r
        to = self.along if 1 <= u <= 4 else self.across
        return remote(r.lefts.at[u], r.lrecv.at[u], r.ls.at[u], r.lr.at[u], to)

    def right_copy(self, u):
        r = self.r
        if u == 4:
            half, to = 1 - self.low, self.along
        else:
            half, to = 1 - self.x, self.across
        return remote(r.gt.at[u, half], r.grecv.at[u], r.gs.at[u], r.gr.at[u], to)

    def core_copy(self, i):
        r = self.r
        mine = r.pbuf.at[i % SLOTS, 1 - self.core]
        return remote(mine, r.precv.at[i], r.ps.at[i], r.pr.at[i], self.clips[1])

    def y_copy(self, i):
        r = self.r
        mine = r.qbuf.at[i % SLOTS, 1 - self.y]
        return remote(mine, r.qrecv.at[i], r.qs.at[i], r.qr.at[i], self.clips[2])

    def spot(self, i):
        return self.high * 2 + self.x if 1 <= PRODUCTS[i][0] <= 4 else self.z

    def z_copy(self, i, k):
        r = self.r
        to = lax.rem(self.spot(i) + k, 4)
        if 1 <= PRODUCTS[i][0] <= 4:
            target = device(self.y, self.core, 2 * lax.div(to, 2) + self.low, lax.rem(to, 2))
        else:
            target = device(self.y, self.core, to, self.x)
        return remote(
            r.rbuf.at[i % SLOTS, to], r.rrecv.at[i, k], r.rs.at[i, k], r.rr.at[i, k], target
        )

    def last_y_copy(self, i):
        r = self.r
        piece = r.final.at[i, self.core, self.y]
        return remote(piece, piece, r.fs.at[i, 0], r.fr.at[i, 0], self.clips[2])

    def last_core_copy(self, i):
        r = self.r
        piece = r.final.at[i, self.core]
        return remote(piece, piece, r.fs.at[i, 1], r.fr.at[i, 1], self.clips[1])

    def out_copy(self, i):
        r = self.r
        return pltpu.make_async_copy(r.final.at[i], r.pieces.at[i], r.out_sems.at[i])

    def post_left(self, u, values):
        self.r.lefts[u] = values
        self.left_copy(u).start()

    def post_right(self, u, values):
        turned = narrow(jnp.transpose(values.astype(jnp.float32)))
        for s in range(8):
            for c in range(2):
                at = s * 96 + c * PART
                half, block = (s // 2 % 2, s // 4 * 2 + s % 2) if u == 4 else (s % 2, s // 2)
                self.r.gt[u, half, c, pl.ds(block * PART, PART), :] = turned[at : at + PART]
        self.right_copy(u).start()

    def multiply(self, i):
        r = self.r
        left, right = PRODUCTS[i]
        if left < LEFTS and (i == 0 or PRODUCTS[i - 1][0] != left):
            self.left_copy(left).wait_recv()
        if i == 0 or PRODUCTS[i - 1][1] != right:
            self.right_copy(right).wait_recv()
        if i >= SLOTS:
            self.core_copy(i - SLOTS).wait_send()
        for c in range(2):
            mine, theirs = r.gt[right, self.low if right == 4 else self.x, c], r.grecv[right, c]
            if left == TEXT_UNIT:
                both = narrow(mine.astype(jnp.float32) + theirs.astype(jnp.float32))
                part = product(both, r.text[...])
            else:
                both = (r.pair[0], r.pair[1]) if left == 8 else (r.lefts[left], r.lrecv[left])
                part = product(
                    jnp.concatenate([mine, theirs], axis=1), jnp.concatenate(both, axis=0)
                )
            r.pbuf[i % SLOTS, c] = narrow(part)
        self.core_copy(i).start()

    def add_core(self, i):
        r = self.r
        self.core_copy(i).wait_recv()
        if i >= SLOTS:
            self.y_copy(i - SLOTS).wait_send()
        total = narrow(
            r.pbuf[i % SLOTS, self.core].astype(jnp.float32) + r.precv[i].astype(jnp.float32)
        )
        r.qbuf[i % SLOTS, 0] = total[:, :384]
        r.qbuf[i % SLOTS, 1] = total[:, 384:]
        self.y_copy(i).start()

    def add_y(self, i):
        r = self.r
        self.y_copy(i).wait_recv()
        if i >= SLOTS:
            for k in (1, 2, 3):
                self.z_copy(i - SLOTS, k).wait_send()
        total = narrow(
            r.qbuf[i % SLOTS, self.y].astype(jnp.float32) + r.qrecv[i].astype(jnp.float32)
        )
        for k in range(4):
            r.rbuf[i % SLOTS, k] = total[k * PART : (k + 1) * PART]
        for k in (1, 2, 3):
            self.z_copy(i, k).start()

    def add_z(self, i):
        r = self.r
        for k in (1, 2, 3):
            self.z_copy(i, k).wait_recv()
        total = r.rbuf[i % SLOTS, self.spot(i)].astype(jnp.float32)
        for k in (1, 2, 3):
            total = total + r.rrecv[i, k].astype(jnp.float32)
        r.final[i, self.core, self.y] = narrow(total)
        self.last_y_copy(i).start()

    def pass_on(self, i):
        self.last_y_copy(i).wait_recv()
        self.last_core_copy(i).start()

    def output(self, i):
        self.last_core_copy(i).wait_recv()
        self.out_copy(i).start()

    def step(self, times=1):
        n = len(PRODUCTS)
        stages = (
            self.multiply,
            self.add_core,
            self.add_y,
            self.add_z,
            self.pass_on,
            self.output,
        )
        for unused in range(times):
            for later, stage in reversed(list(zip(LATER, stages))):
                if 0 <= self.done - later < n:
                    stage(self.done - later)
            self.done += 1

    def finish(self):
        n = len(PRODUCTS)
        while self.done < n + LATER[-1]:
            self.step()
        for u in range(LEFTS):
            self.left_copy(u).wait_send()
        for u in range(RIGHTS):
            self.right_copy(u).wait_send()
        for i in range(n):
            if i >= n - SLOTS:
                self.core_copy(i).wait_send()
                self.y_copy(i).wait_send()
                for k in (1, 2, 3):
                    self.z_copy(i, k).wait_send()
            self.last_y_copy(i).wait_send()
            self.last_core_copy(i).wait_send()
            self.out_copy(i).wait()


def block_kernel(length_ref, *refs):
    names = IN_VMEM + IN_PLACE + OUT_VMEM + OUT_PLACE + list(block_scratch())
    r = types.SimpleNamespace(**dict(zip(names, refs, strict=True)))
    y, core, z, x = places()
    me, band = z * 2 + x, y * 2 + core
    peers = [device(y, core, lax.div(s, 2), lax.rem(s, 2)) for s in [lax.rem(me + k, 8) for k in range(8)]]
    r.cross_q, r.cross_k, r.cross_v, r.grad_heads = [r.gathered.at[i] for i in range(4, 8)]
    sums = Sums(r)

    def load(i, src, dst):
        return pltpu.make_async_copy(src, dst, r.load_sems.at[i])

    squares = (
        r.hbm_out,
        r.hbm_cross_query,
        r.hbm_cross_key,
        r.hbm_cross_value,
        r.hbm_cross_out,
        r.hbm_query,
        r.hbm_key,
        r.hbm_value,
        r.hbm_time_out,
    )
    OUT, CQ, CK, CV, CO, WQ, WK, WV, TIME = range(9)
    loads = [load(i, ref, r.square.at[i]) for i, ref in enumerate(squares)]
    loads.append(load(9, r.hbm_mlp_in, r.mlp_in))
    loads.append(load(10, r.hbm_mlp_out, r.mlp_out))
    loads.append(load(11, r.hbm_adaln.at[:, pl.ds(3072, 1536)], r.adaln_high))
    adaln_low = load(12, r.hbm_adaln.at[:, pl.ds(0, 3072)], r.mlp_in)
    load_time_in = load(13, r.hbm_time_in, r.time_in)
    own_frames = load(14, r.frames, r.gathered.at[me])
    own_frames.start()
    load_time_in.start()
    loads[TIME].start()
    adaln_low.start()
    for i in (11, WQ, WK, WV, OUT, CK, CV, CQ, CO, 10):
        loads[i].start()
    greet(peers[1:] + sums.clips[1:])
    own_frames.wait()
    neighbours = Spread([r.gathered], r.fr_recv, r.fr_up, r.fr_down, r.fr_across)
    neighbours.start()

    def clip_copy(refs, sems, recvs, j):
        return [
            remote(ref.at[band], ref.at[band], sems.at[i, j], recvs.at[i, j], sums.clips[j])
            for i, ref in enumerate(refs)
        ]

    length = length_ref[0]

    def row_valid():
        return lax.broadcasted_iota(jnp.int32, (128, 1), 0) + me * 128 < length

    def modulation(i):
        return r.mod[0:1, i * D : (i + 1) * D]

    def over_rows(values):
        return jnp.sum(values, axis=0, keepdims=True)

    lane = lax.broadcasted_iota(jnp.int32, (1, 128), 1)
    text_valid = r.mask[...] != 0
    gain = r.gain[...].astype(jnp.float32)

    def tile_at(tile):
        return pl.ds(pl.multiple_of(tile * 128, 128), 128)

    load_time_in.wait()
    first = product(r.vector[...], r.time_in[...])
    hidden = narrow(silu(first))
    loads[TIME].wait()
    second = product(hidden, r.square[TIME])
    condition = narrow(silu(second))
    r.time[:, 0:D] = first[0:8]
    r.time[:, D : 2 * D] = second[0:8]
    r.times[band] = r.time[...]
    r.vecs[band] = r.vector[...]
    for j in (1, 2, 3):
        for copy in clip_copy((r.times, r.vecs), r.ts, r.tr, j):
            copy.start()

    adaln_low.wait()
    r.mod[:, 0:1536] = product(condition, r.mlp_in[:, 0:1536])[0:8]
    neighbours.relay(1)
    r.mod[:, 1536:3072] = product(condition, r.mlp_in[:, 1536:3072])[0:8]
    loads[9].start()
    loads[11].wait()
    r.mod[:, 3072:4608] = product(condition, r.adaln_high[...])[0:8]
    for i in (WQ, WK, WV):
        loads[i].wait()
    def project(row, column):
        normed, unused = layer_norm(r.gathered[row * 2 + column].astype(jnp.float32))
        low = narrow(normed * (1.0 + modulation(1)) + modulation(0))
        for i in range(3):
            r.qkv[i, row * 2 + column] = narrow(product(low, r.square[WQ + i]))
        return low

    def own_column(row, unused):
        low = project(row, x)

        @pl.when(row == z)
        def _():
            r.pair[0] = low

        return unused

    def other_column(row, unused):
        neighbours.arrived(row * 2 + 1 - x)
        low = project(row, 1 - x)

        @pl.when(row == z)
        def _():
            r.pair[1] = low

        return unused

    neighbours.relay(2)
    neighbours.relay(3)
    lax.fori_loop(0, 4, own_column, 0)
    lax.fori_loop(0, 4, other_column, 0)
    key_valid = lax.broadcasted_iota(jnp.int32, (1, 1024), 1) < length

    def attend_pair(tile, stats):
        at = tile_at(tile)
        query = r.qkv[0, me, :, at]
        keys = r.qkv[1, :, :, at].reshape(1024, 128)
        values = r.qkv[2, :, :, at].reshape(1024, 128)
        outs = []
        for half in range(2):
            scores = transposed_right(keep_head(query, half), keys) * 0.125
            scores = jnp.where(key_valid, scores, masked_value)
            row_max = jnp.max(scores, axis=1, keepdims=True)
            expanded = jnp.exp(scores - row_max)
            row_sum = jnp.sum(expanded, axis=1, keepdims=True)
            outs.append(product(narrow(expanded), values) / row_sum)
            stats = jnp.where(lane == tile * 2 + half, row_max + jnp.log(row_sum), stats)
        r.attended[:, at] = jnp.where(head_mask(0), outs[0], outs[1])
        return stats

    r.stats[...] = lax.fori_loop(0, 6, attend_pair, jnp.zeros((128, 128), jnp.float32))
    neighbours.finish()
    sums.post_left(7, narrow(r.attended[...]))
    r.grad_mlp[...] = narrow(
        modulation(5) * jnp.where(row_valid(), r.cotangent[...].astype(jnp.float32), 0.0)
    )
    sums.post_right(4, r.grad_mlp[...])
    loads[OUT].wait()
    r.proj[...] = product(r.lefts[7], r.square[OUT])
    r.middle[...] = r.frames[...].astype(jnp.float32) + modulation(2) * r.proj[...]
    normed, scaling_cross = layer_norm(r.middle[...])
    r.normed_cross[...] = normed
    sums.post_left(6, narrow(normed * gain))
    loads[CK].wait()
    r.cross_k[...] = narrow(product(r.text[...], r.square[CK]))
    loads[CV].wait()
    r.cross_v[...] = narrow(product(r.text[...], r.square[CV]))
    loads[CQ].wait()
    r.cross_q[...] = narrow(product(r.lefts[6], r.square[CQ]))

    def cross_pair(tile, unused):
        at = tile_at(tile)
        query, keys, values = r.cross_q[:, at], r.cross_k[:, at], r.cross_v[:, at]
        outs = []
        for half in range(2):
            scores = transposed_right(keep_head(query, half), keys) * 0.125
            scores = jnp.where(text_valid, scores, masked_value)
            row_max = jnp.max(scores, axis=1, keepdims=True)
            total = row_max + jnp.log(jnp.sum(jnp.exp(scores - row_max), axis=1, keepdims=True))
            probs = jnp.exp(scores - total)
            r.cross_probs[tile * 2 + half] = probs
            outs.append(product(narrow(probs), values))
        r.lefts[5, :, at] = narrow(jnp.where(head_mask(0), outs[0], outs[1]))
        return unused

    lax.fori_loop(0, 6, cross_pair, 0)
    sums.left_copy(5).start()
    loads[CO].wait()
    r.after[...] = r.middle[...] + product(r.lefts[5], r.square[CO])
    normed, scaling_mlp = layer_norm(r.after[...])
    r.normed_mlp[...] = normed
    sums.post_left(0, narrow(normed * (1.0 + modulation(4)) + modulation(3)))
    loads[9].wait()
    loads[10].wait()
    for j in range(4):
        pre = product(r.lefts[0], r.mlp_in[:, j * D : (j + 1) * D])
        r.pre[j] = pre
        sums.post_left(1 + j, narrow(gelu(pre)))
        part = product(r.lefts[1 + j], r.mlp_out[j * D : (j + 1) * D, :])
        r.acc[...] = part if j == 0 else r.acc[...] + part
    frames = r.frames[...].astype(jnp.float32)
    r.block_out[...] = narrow(
        jnp.where(row_valid(), r.after[...] + modulation(5) * r.acc[...], frames)
    )
    grad_res = jnp.where(row_valid(), r.cotangent[...].astype(jnp.float32), 0.0)
    r.sums[5:6, :] = over_rows(grad_res * r.acc[...])
    for j in range(4):
        slope = gelu_slope(r.pre[j])
        grad = narrow(slope * transposed_right(r.grad_mlp[...], r.mlp_out[j * D : (j + 1) * D, :]))
        r.gathered[j] = grad
        for part in range(2):
            s = j * 2 + part
            turned = narrow(
                jnp.transpose(grad[:, part * 384 : (part + 1) * 384].astype(jnp.float32))
            )
            for u in range(4):
                for c in range(2):
                    at = u * 96 + c * PART
                    r.gt[u, s % 2, c, pl.ds((s // 2) * PART, PART), :] = turned[at : at + PART]
    for u in range(4):
        sums.right_copy(u).start()
    sums.step(1)
    for j in range(4):
        part = transposed_right(r.gathered[j], r.mlp_in[:, j * D : (j + 1) * D])
        r.acc[...] = part if j == 0 else r.acc[...] + part
    adaln_low.start()
    sums.step(2)
    r.sums[3:4, :] = over_rows(r.acc[...])
    r.sums[4:5, :] = over_rows(r.acc[...] * r.normed_mlp[...])
    grad_res = jnp.where(row_valid(), r.cotangent[...].astype(jnp.float32), 0.0)
    r.after[...] = grad_res + norm_back(
        r.normed_mlp[...], scaling_mlp, r.acc[...] * (1.0 + modulation(4))
    )
    low = narrow(r.after[...])
    sums.post_right(5, low)
    r.grad_heads[...] = narrow(transposed_right(low, r.square[CO]))

    def cross_pair_back(tile, unused):
        at = tile_at(tile)
        query, keys, values = r.cross_q[:, at], r.cross_k[:, at], r.cross_v[:, at]
        grad = r.grad_heads[:, at]
        outs = []
        for half in range(2):
            probs = r.cross_probs[tile * 2 + half]
            grad_probs = transposed_right(keep_head(grad, half), values)
            inner = jnp.sum(probs * grad_probs, axis=1, keepdims=True)
            scores = narrow(probs * (grad_probs - inner)).astype(jnp.float32)
            outs.append(
                (
                    product(narrow(scores), keys),
                    product(narrow(jnp.transpose(scores)), query),
                    product(narrow(jnp.transpose(probs)), grad),
                )
            )
        grad_q, grad_k, grad_v = [jnp.where(head_mask(0), a, b) for a, b in zip(*outs)]
        r.grad_q[:, at] = narrow(grad_q * 0.125)
        r.grad_k[:, at] = narrow(grad_k * 0.125)
        r.grad_v[:, at] = narrow(grad_v)
        return unused

    lax.fori_loop(0, 6, cross_pair_back, 0)
    sums.post_right(6, r.grad_q[...])
    sums.step(2)
    grad_cross_in = transposed_right(r.grad_q[...], r.square[CQ])
    r.sums[6:7, :] = over_rows(grad_cross_in * r.normed_cross[...])
    r.sums[7:8, :] = jnp.zeros((1, D), jnp.float32)
    r.middle[...] = r.after[...] + norm_back(
        r.normed_cross[...], scaling_cross, grad_cross_in * gain
    )
    low = narrow(modulation(2) * r.middle[...])
    grad_heads = narrow(transposed_right(low, r.square[OUT]))
    r.heads[me] = grad_heads
    products = grad_heads.astype(jnp.float32) * r.attended[...]
    delta = jnp.zeros((128, 128), jnp.float32)
    for h in range(12):
        tile = products[:, (h // 2) * 128 : (h // 2 + 1) * 128]
        inner = jnp.sum(jnp.where(head_mask(h % 2), tile, 0.0), axis=1, keepdims=True)
        delta = jnp.where(lane == h, inner, delta)
    r.rowstats[me] = jnp.concatenate(
        [jnp.transpose(r.stats[...])[:16], jnp.transpose(delta)[:16]], axis=0
    )
    spread = Spread([r.heads, r.rowstats], r.sp_recv, r.sp_up, r.sp_down, r.sp_across)
    spread.start()
    sums.post_right(7, low)
    sums.step(1)
    r.sums[2:3, :] = over_rows(r.middle[...] * r.proj[...])
    sums.post_right(8, r.grad_k[...])
    sums.post_right(9, r.grad_v[...])
    text_grad = transposed_right(r.grad_k[...], r.square[CK]) + transposed_right(
        r.grad_v[...], r.square[CV]
    )
    for s in range(8):
        r.text_part[s] = text_grad[s * 16 : (s + 1) * 16]
        r.text_send[s] = narrow(text_grad[s * 16 : (s + 1) * 16])

    def text_copy(k):
        return remote(
            r.text_send.at[lax.rem(me + k, 8)], r.text_recv.at[k], r.xs.at[k], r.xr.at[k], peers[k]
        )

    for k in range(1, 8):
        text_copy(k).start()
    spread.relay(1)
    sums.step(1)
    key_valid = lax.broadcasted_iota(jnp.int32, (1, 1024), 1) < length

    def query_pair(tile, unused):
        at = tile_at(tile)
        query, grad = r.qkv[0, me, :, at], r.heads[me, :, at]
        keys = r.qkv[1, :, :, at].reshape(1024, 128)
        values = r.qkv[2, :, :, at].reshape(1024, 128)
        tile_product = grad.astype(jnp.float32) * r.attended[:, at]
        outs = []
        for half in range(2):
            scores = transposed_right(keep_head(query, half), keys) * 0.125
            scores = jnp.where(key_valid, scores, masked_value)
            total = jnp.sum(
                jnp.where(lane == tile * 2 + half, r.stats[...], 0.0), axis=1, keepdims=True
            )
            inner = jnp.sum(jnp.where(head_mask(half), tile_product, 0.0), axis=1, keepdims=True)
            grad_probs = transposed_right(keep_head(grad, half), values)
            outs.append(product(narrow(jnp.exp(scores - total) * (grad_probs - inner)), keys))
        r.grad_q[:, at] = narrow(jnp.where(head_mask(0), outs[0], outs[1]) * 0.125)
        return unused

    lax.fori_loop(0, 2, query_pair, 0)
    spread.relay(2)
    sums.step(1)
    lax.fori_loop(2, 4, query_pair, 0)
    spread.relay(3)
    sums.step(1)
    lax.fori_loop(4, 6, query_pair, 0)
    sums.post_right(10, r.grad_q[...])
    sums.step(3)
    for row in range(4):
        spread.arrived(row * 2 + 1 - x)

    def key_pair(tile, unused):
        at = tile_at(tile)
        key, value = r.qkv[1, me, :, at], r.qkv[2, me, :, at]
        queries = r.qkv[0, :, :, at].reshape(1024, 128)
        grads = r.heads[:, :, at].reshape(1024, 128)
        outs = []
        for half in range(2):
            h = tile * 2 + half
            total = jnp.concatenate([r.rowstats[s, pl.ds(h, 1), :] for s in range(8)], axis=1)
            inner = jnp.concatenate([r.rowstats[s, pl.ds(16 + h, 1), :] for s in range(8)], axis=1)
            scores = transposed_right(keep_head(key, half), queries) * 0.125
            scores = jnp.where(row_valid(), scores, masked_value)
            probs = jnp.exp(scores - total)
            grad_probs = transposed_right(keep_head(value, half), grads)
            grad_scores = narrow(probs * (grad_probs - inner))
            outs.append((product(grad_scores, queries), product(narrow(probs), grads)))
        grad_k, grad_v = [jnp.where(head_mask(0), a, b) for a, b in zip(*outs)]
        r.grad_k[:, at] = narrow(grad_k * 0.125)
        r.grad_v[:, at] = narrow(grad_v)
        return unused

    lax.fori_loop(0, 6, key_pair, 0)
    sums.post_right(11, r.grad_k[...])
    sums.post_right(12, r.grad_v[...])
    sums.step(1)
    grad_in = (
        transposed_right(r.grad_q[...], r.square[WQ])
        + transposed_right(r.grad_k[...], r.square[WK])
        + transposed_right(r.grad_v[...], r.square[WV])
    )
    r.acc[...] = grad_in
    normed, scaling = layer_norm(r.frames[...].astype(jnp.float32))
    r.sums[0:1, :] = over_rows(r.acc[...])
    r.sums[1:2, :] = over_rows(r.acc[...] * normed)

    def sums_copy(k):
        return remote(r.sums, r.sums_recv.at[k], r.ss.at[k], r.sr.at[k], peers[k])

    for k in range(1, 8):
        sums_copy(k).start()
    sums.step(3)
    grads = r.middle[...] + norm_back(normed, scaling, r.acc[...] * (1.0 + modulation(1)))
    r.grad_frames[...] = narrow(
        jnp.where(row_valid(), grads, r.cotangent[...].astype(jnp.float32))
    )
    total = r.sums[...]
    for k in range(1, 8):
        sums_copy(k).wait_recv()
        total = total + r.sums_recv[k]
    r.clip_sums[band] = total

    def total_copy(j):
        return remote(
            r.clip_sums.at[band], r.clip_sums.at[band], r.cs.at[j], r.cr.at[j], sums.clips[j]
        )

    for j in (1, 2, 3):
        total_copy(j).start()
    sums.step(2)
    for j in (1, 2, 3):
        total_copy(j).wait_recv()
        for copy in clip_copy((r.times, r.vecs), r.ts, r.tr, j):
            copy.wait_recv()
    r.gain_sum[0:1, :] = (r.clip_sums[0, 6:7] + r.clip_sums[1, 6:7]) + (
        r.clip_sums[2, 6:7] + r.clip_sums[3, 6:7]
    )
    r.gain_sum[1:8, :] = jnp.zeros((7, D), jnp.float32)

    def by_clip(pieces):
        return jnp.concatenate(pieces + [jnp.zeros((12, pieces[0].shape[1]), jnp.float32)], axis=0)

    for i in range(6):
        r.grad_mods[:, i * D : (i + 1) * D] = narrow(
            by_clip([r.clip_sums[b, i : i + 1] for b in range(4)])
        )
    firsts = by_clip([r.times[b, 0:1, 0:D] for b in range(4)])
    seconds = by_clip([r.times[b, 0:1, D : 2 * D] for b in range(4)])
    r.hiddens[...] = narrow(silu(firsts))
    r.conditions[...] = narrow(silu(seconds))
    for b in range(4):
        r.vectors[b] = r.vecs[b]
    adaln_low.wait()
    grad_condition = transposed_right(r.grad_mods[:, :3072], r.mlp_in[...]) + transposed_right(
        r.grad_mods[:, 3072:], r.adaln_high[...]
    )
    low = narrow(silu_slope(seconds) * grad_condition)
    r.grad_time_outs[...] = low
    r.grad_time_firsts[...] = silu_slope(firsts) * transposed_right(low, r.square[TIME])
    total = r.text_part[me]
    for k in range(1, 8):
        text_copy(k).wait_recv()
        total = total + r.text_recv[k].astype(jnp.float32)
    r.grad_text[...] = total
    sums.finish()
    spread.finish()
    for k in range(1, 8):
        text_copy(k).wait_send()
        sums_copy(k).wait_send()
    for j in (1, 2, 3):
        total_copy(j).wait_send()
        for copy in clip_copy((r.times, r.vecs), r.ts, r.tr, j):
            copy.wait_send()


def block(length, vmem_args, place_args):
    in_vmem = pl.BlockSpec(memory_space=pltpu.VMEM)
    in_place = pl.BlockSpec(memory_space=pl.ANY)
    shape = jax.ShapeDtypeStruct
    f32, bf16 = jnp.float32, jnp.bfloat16
    return pl.pallas_call(
        block_kernel,
        out_shape=(
            shape((128, D), bf16),
            shape((128, D), bf16),
            shape((16, D), f32),
            shape((8, D), f32),
            shape((16, D), bf16),
            shape((16, D), bf16),
            shape((4, 16, 256), bf16),
            shape((16, 6 * D), bf16),
            shape((16, D), bf16),
            shape((16, D), f32),
            shape((len(PRODUCTS), 2, 2, PART, 384), bf16),
        ),
        in_specs=[pl.BlockSpec(memory_space=pltpu.SMEM)]
        + [in_vmem] * len(IN_VMEM)
        + [in_place] * len(IN_PLACE),
        out_specs=(in_vmem,) * len(OUT_VMEM) + (in_place,) * len(OUT_PLACE),
        scratch_shapes=list(block_scratch().values()),
        compiler_params=pltpu.CompilerParams(
            collective_id=0, has_side_effects=True, vmem_limit_bytes=VMEM_BYTES
        ),
    )(length, *vmem_args, *place_args)


SQUARES = (8, 9, 12, 10, 11, 13, 14, 15)
FINAL_IN = [
    "pieces",
    "block_out",
    "grad_frames",
    "grad_text",
    "gain_sum",
    "conditions",
    "hiddens",
    "vectors",
    "grad_mods",
    "grad_time_outs",
    "grad_time_firsts",
]
FINAL_SHAPES = (
    [((128, D), jnp.bfloat16), ((128, D), jnp.bfloat16), ((16, D), jnp.float32)]
    + [((96, 256), jnp.float32), ((96, D), jnp.float32), ((576, D), jnp.float32)]
    + [((1, 96), jnp.float32), ((D, 384), jnp.float32), ((96, 4 * D), jnp.float32)]
    + [((96, D), jnp.float32)] * 8
)


def final_kernel(*refs):
    r = types.SimpleNamespace(**dict(zip(FINAL_IN, refs)))
    count = len(FINAL_SHAPES)
    rest = refs[len(FINAL_IN) :]
    outs, staged, (turned_mods, turned_small, sems) = rest[:count], rest[count : 2 * count], rest[2 * count :]
    seq = lax.axis_index("seq")

    def put(i, values):
        staged[i][...] = values
        copy(i).start()

    def copy(i):
        return pltpu.make_async_copy(staged[i], outs[i], sems.at[i])

    def whole(p):
        return jnp.concatenate(
            [jnp.concatenate([r.pieces[p, c, h] for h in range(2)], axis=1) for c in range(2)],
            axis=0,
        ).astype(jnp.float32)

    put(7, jnp.transpose(jnp.concatenate([whole(4 + j) for j in range(4)], axis=0)))
    for j in range(4):
        staged[8][:, j * D : (j + 1) * D] = whole(j)
    copy(8).start()
    for j, p in enumerate(SQUARES):
        put(9 + j, whole(p))
    put(0, r.block_out[...])
    put(1, r.grad_frames[...])
    put(2, r.grad_text[...])
    turned_mods[...] = jnp.transpose(r.grad_mods[...].astype(jnp.float32))
    put(
        5,
        product(
            narrow(turned_mods[pl.ds(pl.multiple_of(seq * 576, 64), 576), :]), r.conditions[...]
        ),
    )
    own = pl.ds(pl.multiple_of(seq * 96, 32), 96)
    turned_small[0] = jnp.transpose(r.grad_time_outs[...].astype(jnp.float32))
    put(4, product(narrow(turned_small[0, own, :]), r.hiddens[...]))
    turned_small[1] = jnp.transpose(r.grad_time_firsts[...])
    rows = [r.vectors[b, 0:1].astype(jnp.float32) for b in range(4)]
    vectors = jnp.concatenate(rows + [jnp.zeros((12, 256), jnp.float32)], axis=0)
    put(
        3,
        jnp.dot(
            turned_small[1, own, :],
            vectors,
            precision=lax.Precision.HIGHEST,
            preferred_element_type=jnp.float32,
        ),
    )
    gains = jnp.concatenate([r.gain_sum[...], jnp.zeros((8, D), jnp.float32)], axis=0)
    turned_small[2] = jnp.transpose(gains)
    put(6, jnp.transpose(turned_small[2, own, :])[0:1])
    for i in range(count):
        copy(i).wait()


def finish(values):
    in_vmem = pl.BlockSpec(memory_space=pltpu.VMEM)
    in_place = pl.BlockSpec(memory_space=pl.ANY)
    return pl.pallas_call(
        final_kernel,
        out_shape=tuple(jax.ShapeDtypeStruct(*shape) for shape in FINAL_SHAPES),
        in_specs=[in_vmem] * len(FINAL_IN),
        out_specs=(in_place,) * len(FINAL_SHAPES),
        scratch_shapes=[pltpu.VMEM(*shape) for shape in FINAL_SHAPES]
        + [
            vmem(6 * D, 16, dtype=jnp.float32),
            vmem(3, D, 16, dtype=jnp.float32),
            pltpu.SemaphoreType.DMA((len(FINAL_SHAPES),)),
        ],
        compiler_params=pltpu.CompilerParams(vmem_limit_bytes=VMEM_BYTES),
    )(*values)


def on_device(
    frames,
    text,
    timesteps,
    frame_lengths,
    text_mask,
    cotangent,
    w_time_in,
    w_time_out,
    w_adaln,
    w_query,
    w_key,
    w_value,
    w_attn_out,
    cross_gain,
    w_cross_query,
    w_cross_key,
    w_cross_value,
    w_cross_out,
    w_mlp_in,
    w_mlp_out,
):
    vector = jnp.broadcast_to(narrow(time_embed(timesteps, w_time_in.shape[0])), (16, 256))
    (
        block_out,
        grad_frames,
        grad_text,
        gain_sum,
        conditions,
        hiddens,
        vectors,
        grad_mods,
        grad_time_outs,
        grad_time_firsts,
        pieces,
    ) = block(
        frame_lengths,
        (
            text_mask,
            frames[0],
            cotangent[0],
            text[0],
            cross_gain[None],
            vector,
        ),
        (
            w_attn_out,
            w_cross_query,
            w_cross_key,
            w_cross_value,
            w_cross_out,
            w_mlp_in,
            w_mlp_out,
            w_query,
            w_key,
            w_value,
            w_adaln,
            w_time_out,
            w_time_in,
        ),
    )
    (
        block_out,
        grad_frames,
        grad_text,
        sum_time_in,
        sum_time_out,
        sum_adaln,
        sum_gain,
        sum_mlp_in,
        sum_mlp_out,
        sum_cross_out,
        sum_cross_query,
        sum_attn_out,
        sum_cross_key,
        sum_cross_value,
        sum_query,
        sum_key,
        sum_value,
    ) = finish(
        (
            pieces,
            block_out,
            grad_frames,
            grad_text,
            gain_sum,
            conditions,
            hiddens,
            vectors,
            grad_mods,
            grad_time_outs,
            grad_time_firsts,
        )
    )
    return (
        block_out[None],
        grad_frames[None],
        grad_text[None],
        sum_time_in.T,
        sum_time_out.T,
        sum_adaln.T,
        sum_query.T,
        sum_key.T,
        sum_value.T,
        sum_attn_out.T,
        sum_gain[0],
        sum_cross_query.T,
        sum_cross_key.T,
        sum_cross_value.T,
        sum_cross_out.T,
        sum_mlp_in,
        sum_mlp_out.T,
    )


def on_device_general(
    frames,
    text,
    timesteps,
    frame_lengths,
    text_mask,
    cotangent,
    w_time_in,
    w_time_out,
    w_adaln,
    w_query,
    w_key,
    w_value,
    w_attn_out,
    cross_gain,
    w_cross_query,
    w_cross_key,
    w_cross_value,
    w_cross_out,
    w_mlp_in,
    w_mlp_out,
):
    clips = frames.shape[0]
    rows = frames.shape[1]
    width = frames.shape[2]
    tokens = clips * rows
    text_count = text.shape[1]
    seq_place = lax.axis_index("seq")
    seq_count = lax.axis_size("seq")
    offset = seq_place * rows
    inputs = frames.astype(jnp.float32)
    own_valid = (offset + jnp.arange(rows))[None, :] < frame_lengths[:, None]
    row_valid = own_valid[:, :, None]
    text_valid = text_mask != 0

    def flatten(values):
        return values.reshape(tokens, values.shape[-1])

    def unflatten(values):
        return values.reshape(clips, rows, values.shape[-1])

    time_vector = narrow(time_embed(timesteps, w_time_in.shape[0]))
    time_first = product(time_vector, w_time_in)
    time_hidden = narrow(jax.nn.silu(time_first))
    time_out = product(time_hidden, w_time_out)
    condition = narrow(jax.nn.silu(time_out))
    modulation = product(condition, w_adaln)
    shift_attn, scale_attn, gate_attn, shift_mlp, scale_mlp, gate_mlp = [
        piece[:, None, :] for piece in jnp.split(modulation, 6, axis=1)
    ]
    normed_attn, scaling_attn = layer_norm(inputs)
    attn_in = narrow(normed_attn * (1.0 + scale_attn) + shift_attn)
    attn_flat = flatten(attn_in)
    query_flat = narrow(product(attn_flat, w_query))
    queries = split_heads(unflatten(query_flat))
    kv_local = unflatten(
        jnp.concatenate(
            [narrow(product(attn_flat, w_key)), narrow(product(attn_flat, w_value))], axis=1
        )
    )
    start_state = (
        jnp.full((clips, rows, H), -1e30, jnp.float32),
        jnp.zeros((clips, rows, H), jnp.float32),
        jnp.zeros((clips, rows, H, HD), jnp.float32),
    )
    row_max, row_sum, weighted = forward_piece(
        start_state,
        lax.all_gather(kv_local, "seq", axis=1, tiled=True),
        jnp.int32(0),
        queries,
        frame_lengths,
    )
    attended = weighted / row_sum[..., None]
    log_total = row_max + jnp.log(row_sum)
    attn_low = narrow(attended.reshape(clips, rows, width))
    attn_proj = unflatten(product(flatten(attn_low), w_attn_out))
    middle = inputs + gate_attn * attn_proj
    normed_cross, scaling_cross = layer_norm(middle)
    gain_values = cross_gain.astype(jnp.float32)
    cross_in = narrow(normed_cross * gain_values)
    cross_queries = split_heads(unflatten(narrow(product(flatten(cross_in), w_cross_query))))
    text_flat = text.reshape(clips * text_count, width)
    cross_keys = split_heads(
        narrow(product(text_flat, w_cross_key)).reshape(clips, text_count, width)
    )
    cross_values = split_heads(
        narrow(product(text_flat, w_cross_value)).reshape(clips, text_count, width)
    )
    cross_scores = masked_scores(cross_queries, cross_keys, text_valid)
    cross_max = jnp.max(cross_scores, axis=-1, keepdims=True)
    cross_total = cross_max + jnp.log(
        jnp.sum(jnp.exp(cross_scores - cross_max), axis=-1, keepdims=True)
    )
    cross_probs = jnp.exp(cross_scores - cross_total)
    cross_probs_low = narrow(cross_probs)
    cross_attended = jnp.einsum(
        "cqhk,ckhd->cqhd", cross_probs_low, cross_values, preferred_element_type=jnp.float32
    )
    cross_low = narrow(cross_attended.reshape(clips, rows, width))
    after_cross = middle + unflatten(product(flatten(cross_low), w_cross_out))
    normed_mlp, scaling_mlp = layer_norm(after_cross)
    mlp_in = narrow(normed_mlp * (1.0 + scale_mlp) + shift_mlp)
    pre_act = product(flatten(mlp_in), w_mlp_in)
    activation = narrow(jax.nn.gelu(pre_act, approximate=True))
    mlp_out = unflatten(product(activation, w_mlp_out))
    result = after_cross + gate_mlp * mlp_out
    block_out = jnp.where(row_valid, result, inputs).astype(jnp.bfloat16)
    grad_out = cotangent.astype(jnp.float32)
    grad_res = jnp.where(row_valid, grad_out, 0.0)
    grad_mlp = flatten(narrow(gate_mlp * grad_res))
    grad_w_mlp_out = transposed_left(activation, grad_mlp)
    grad_act = transposed_right(grad_mlp, w_mlp_out)
    gelu_pull = jax.vjp(lambda values: jax.nn.gelu(values, approximate=True), pre_act)[1]
    grad_pre = narrow(gelu_pull(grad_act)[0])
    grad_w_mlp_in = transposed_left(flatten(mlp_in), grad_pre)
    grad_mlp_in = unflatten(transposed_right(grad_pre, w_mlp_in))
    grad_after = grad_res + norm_back(normed_mlp, scaling_mlp, grad_mlp_in * (1.0 + scale_mlp))
    grad_cross_out = flatten(narrow(grad_after))
    grad_w_cross_out = transposed_left(flatten(cross_low), grad_cross_out)
    grad_cross_attn = split_heads(unflatten(narrow(transposed_right(grad_cross_out, w_cross_out))))
    cross_delta = jnp.sum(grad_cross_attn.astype(jnp.float32) * cross_attended, axis=-1)
    cross_grad_probs = jnp.einsum(
        "cqhd,ckhd->cqhk", grad_cross_attn, cross_values, preferred_element_type=jnp.float32
    )
    cross_grad_scores = narrow(cross_probs * (cross_grad_probs - cross_delta[..., None]))
    grad_cross_query = narrow(
        jnp.einsum(
            "cqhk,ckhd->cqhd", cross_grad_scores, cross_keys, preferred_element_type=jnp.float32
        )
        * 0.125
    ).reshape(tokens, width)
    cross_key_part = (
        jnp.einsum(
            "cqhk,cqhd->ckhd", cross_grad_scores, cross_queries, preferred_element_type=jnp.float32
        )
        * 0.125
    )
    cross_value_part = jnp.einsum(
        "cqhk,cqhd->ckhd", cross_probs_low, grad_cross_attn, preferred_element_type=jnp.float32
    )
    cross_kv_part = jnp.concatenate(
        [
            cross_key_part.reshape(clips, text_count, width),
            cross_value_part.reshape(clips, text_count, width),
        ],
        axis=2,
    )
    text_total = lax.psum_scatter(cross_kv_part, "seq", scatter_dimension=1, tiled=True)
    text_share = text_total.shape[1]
    grad_cross_key = narrow(text_total[:, :, :width]).reshape(clips * text_share, width)
    grad_cross_value = narrow(text_total[:, :, width:]).reshape(clips * text_share, width)
    text_own = lax.dynamic_slice_in_dim(text, seq_place * text_share, text_share, 1).reshape(
        clips * text_share, width
    )
    grad_text = (
        transposed_right(grad_cross_key, w_cross_key)
        + transposed_right(grad_cross_value, w_cross_value)
    ).reshape(clips, text_share, width)
    grad_w_cross_key = transposed_left(text_own, grad_cross_key)
    grad_w_cross_value = transposed_left(text_own, grad_cross_value)
    grad_w_cross_query = transposed_left(flatten(cross_in), grad_cross_query)
    grad_cross_in = unflatten(transposed_right(grad_cross_query, w_cross_query))
    grad_gain_part = jnp.sum(grad_cross_in * normed_cross, axis=(0, 1))
    grad_mid = grad_after + norm_back(normed_cross, scaling_cross, grad_cross_in * gain_values)
    grad_attn_proj = flatten(narrow(gate_attn * grad_mid))
    grad_w_attn_out = transposed_left(flatten(attn_low), grad_attn_proj)
    grad_attn_flat = narrow(transposed_right(grad_attn_proj, w_attn_out))
    grad_heads = split_heads(unflatten(grad_attn_flat))
    row_delta = jnp.sum(grad_heads.astype(jnp.float32) * attended, axis=-1)
    zero_heads = jnp.zeros((clips, rows, H, HD), jnp.float32)
    gathered = lax.all_gather(kv_local, "seq", axis=1, tiled=True)
    query_grad = query_piece(
        zero_heads, gathered, 0, queries, grad_heads, log_total, row_delta, frame_lengths
    )
    anchor = jnp.int32(0)
    block_size = math.gcd(rows * lax.axis_size("seq"), key_block)

    def key_one_block(counter):
        rows_in = lax.dynamic_slice_in_dim(gathered, counter * block_size, block_size, 1)
        key_valid = block_valid(anchor, counter * block_size, block_size, frame_lengths)
        scores = masked_scores(queries, split_heads(rows_in[:, :, :width]), key_valid)
        attn_probs = jnp.exp(scores - log_total[..., None])
        grad_probs = jnp.einsum(
            "cqhd,ckhd->cqhk",
            grad_heads,
            split_heads(rows_in[:, :, width:]),
            preferred_element_type=jnp.float32,
        )
        grad_scores = narrow(attn_probs * (grad_probs - row_delta[..., None]))
        grad_keys = (
            jnp.einsum("cqhk,cqhd->ckhd", grad_scores, queries, preferred_element_type=jnp.float32)
            * 0.125
        )
        grad_values = jnp.einsum(
            "cqhk,cqhd->ckhd", narrow(attn_probs), grad_heads, preferred_element_type=jnp.float32
        )
        joined = jnp.concatenate(
            [
                grad_keys.reshape(clips, block_size, width),
                grad_values.reshape(clips, block_size, width),
            ],
            axis=2,
        )
        return jnp.transpose(joined, (1, 0, 2))

    blocks = lax.map(key_one_block, jnp.arange(rows * lax.axis_size("seq") // block_size))
    kv_term = lax.psum_scatter(
        blocks.reshape(rows * lax.axis_size("seq"), clips, 2 * width),
        "seq",
        scatter_dimension=0,
        tiled=True,
    )
    kv_grad = jnp.transpose(kv_term, (1, 0, 2))
    grad_query = narrow(query_grad.reshape(tokens, width))
    grad_key = flatten(narrow(kv_grad[:, :, :width]))
    grad_value = flatten(narrow(kv_grad[:, :, width:]))
    grad_w_query = transposed_left(attn_flat, grad_query)
    grad_w_key = transposed_left(attn_flat, grad_key)
    grad_w_value = transposed_left(attn_flat, grad_value)
    grad_attn_in = unflatten(
        transposed_right(grad_query, w_query)
        + transposed_right(grad_key, w_key)
        + transposed_right(grad_value, w_value)
    )
    grad_inputs = grad_mid + norm_back(normed_attn, scaling_attn, grad_attn_in * (1.0 + scale_attn))
    grad_frames = jnp.where(row_valid, grad_inputs, grad_out).astype(jnp.bfloat16)
    modulation_part = jnp.concatenate(
        [
            jnp.sum(grad_attn_in, axis=1),
            jnp.sum(grad_attn_in * normed_attn, axis=1),
            jnp.sum(grad_mid * attn_proj, axis=1),
            jnp.sum(grad_mlp_in, axis=1),
            jnp.sum(grad_mlp_in * normed_mlp, axis=1),
            jnp.sum(grad_res * mlp_out, axis=1),
        ],
        axis=1,
    )
    modulation_total = lax.psum(modulation_part, "seq")
    grad_modulation = narrow(modulation_total)
    grad_w_adaln = transposed_left(condition, grad_modulation)
    grad_condition = transposed_right(grad_modulation, w_adaln)
    grad_time_out = narrow(jax.vjp(jax.nn.silu, time_out)[1](grad_condition)[0])
    grad_w_time_out = transposed_left(time_hidden, grad_time_out)
    grad_time_hidden = transposed_right(grad_time_out, w_time_out)
    grad_time_first = jax.vjp(jax.nn.silu, time_first)[1](grad_time_hidden)[0]
    grad_w_time_in = lax.dot_general(
        time_vector.astype(jnp.float32),
        grad_time_first,
        (((0,), (0,)), ((), ())),
        precision=lax.Precision.HIGHEST,
    )
    shared = (
        lax.psum_scatter(grad_w_query, "seq", scatter_dimension=1, tiled=True),
        lax.psum_scatter(grad_w_key, "seq", scatter_dimension=1, tiled=True),
        lax.psum_scatter(grad_w_value, "seq", scatter_dimension=1, tiled=True),
        lax.psum_scatter(grad_w_attn_out, "seq", scatter_dimension=1, tiled=True),
        lax.psum_scatter(grad_gain_part, "seq", scatter_dimension=0, tiled=True),
        lax.psum_scatter(grad_w_cross_query, "seq", scatter_dimension=1, tiled=True),
        lax.psum_scatter(grad_w_cross_key, "seq", scatter_dimension=1, tiled=True),
        lax.psum_scatter(grad_w_cross_value, "seq", scatter_dimension=1, tiled=True),
        lax.psum_scatter(grad_w_cross_out, "seq", scatter_dimension=1, tiled=True),
        lax.psum_scatter(grad_w_mlp_in, "seq", scatter_dimension=1, tiled=True),
        lax.psum_scatter(grad_w_mlp_out, "seq", scatter_dimension=1, tiled=True),
    )
    replicated = (
        own_columns(grad_w_time_in, seq_place, seq_count),
        own_columns(grad_w_time_out, seq_place, seq_count),
        own_columns(grad_w_adaln, seq_place, seq_count),
    )
    summed = jax.tree.map(
        lambda part: part.astype(jnp.float32), lax.psum(for_sending(shared + replicated), "band")
    )
    (
        sum_query,
        sum_key,
        sum_value,
        sum_attn_out,
        sum_gain,
        sum_cross_query,
        sum_cross_key,
        sum_cross_value,
        sum_cross_out,
        sum_mlp_in,
        sum_mlp_out,
        sum_time_in,
        sum_time_out,
        sum_adaln,
    ) = summed
    return (
        block_out,
        grad_frames,
        grad_text,
        sum_time_in,
        sum_time_out,
        sum_adaln,
        sum_query,
        sum_key,
        sum_value,
        sum_attn_out,
        sum_gain,
        sum_cross_query,
        sum_cross_key,
        sum_cross_value,
        sum_cross_out,
        sum_mlp_in,
        sum_mlp_out,
    )


def solution(mesh):
    placed = (
        P("band", "seq", None),
        P("band", None, None),
        P("band"),
        P("band"),
        P("band", None),
        P("band", "seq", None),
        P(),
        P(),
        P(),
        P(),
        P(),
        P(),
        P(),
        P(),
        P(),
        P(),
        P(),
        P(),
        P(),
        P(),
    )
    paired = mesh.shape["band"] == 4 and mesh.shape["seq"] == 8
    return jax.shard_map(
        on_device if paired else on_device_general,
        mesh=mesh,
        in_specs=placed,
        out_specs=(
            P("band", "seq", None),
            P("band", "seq", None),
            P("band", "seq", None),
            P(None, "seq"),
            P(None, "seq"),
            P(None, "seq"),
            P(None, "seq"),
            P(None, "seq"),
            P(None, "seq"),
            P(None, "seq"),
            P("seq"),
            P(None, "seq"),
            P(None, "seq"),
            P(None, "seq"),
            P(None, "seq"),
            P(None, "seq"),
            P(None, "seq"),
        ),
        check_vma=False,
    )
```

```python
import math
import types

import jax
import jax.numpy as jnp
from jax import lax
from jax.experimental import pallas as pl
from jax.experimental.pallas import tpu as pltpu
from jax.sharding import PartitionSpec as P

H = 12
HD = 64


epsilon = 1e-06
masked_value = -1000000000.0
key_block = 512


def for_sending(value):
    return jax.tree.map(lambda a: a.astype(jnp.bfloat16) if a.dtype == jnp.float32 else a, value)


def narrow(values):
    return values.astype(jnp.bfloat16)


def product(left, right):
    return jnp.dot(left, right, preferred_element_type=jnp.float32)


def transposed_left(left, right):
    return lax.dot_general(
        left, right, (((0,), (0,)), ((), ())), preferred_element_type=jnp.float32
    )


def transposed_right(left, right):
    return lax.dot_general(
        left, right, (((1,), (1,)), ((), ())), preferred_element_type=jnp.float32
    )


def layer_norm(inputs):
    center = inputs - jnp.mean(inputs, axis=-1, keepdims=True)
    scaling = lax.rsqrt(jnp.mean(center * center, axis=-1, keepdims=True) + epsilon)
    return (center * scaling, scaling)


def norm_back(normed, scaling, gradient):
    mean_grad = jnp.mean(gradient, axis=-1, keepdims=True)
    mean_prod = jnp.mean(gradient * normed, axis=-1, keepdims=True)
    return scaling * (gradient - mean_grad - normed * mean_prod)


def time_embed(timesteps, width):
    half_width = width // 2
    frequency = jnp.exp(-math.log(10000.0) * jnp.arange(half_width, dtype=jnp.float32) / half_width)
    angles = timesteps.astype(jnp.float32)[:, None] * frequency[None, :]
    return jnp.concatenate([jnp.cos(angles), jnp.sin(angles)], axis=1)


def split_heads(rows_in):
    return rows_in.reshape(rows_in.shape[0], rows_in.shape[1], H, HD)


def masked_scores(queries, key_rows, key_valid):
    scores = (
        jnp.einsum("cqhd,ckhd->cqhk", queries, key_rows, preferred_element_type=jnp.float32) * 0.125
    )
    return jnp.where(key_valid[:, None, None, :], scores, masked_value)


def block_valid(anchor, start_row, block_size, lengths):
    return (anchor + start_row + jnp.arange(block_size))[None, :] < lengths[:, None]


def forward_piece(running, segment, anchor, queries, lengths):
    row_count = segment.shape[1]
    block_size = math.gcd(row_count, key_block)
    width = queries.shape[2] * queries.shape[3]

    def forward_one_block(running, counter):
        rows_in = lax.dynamic_slice_in_dim(segment, counter * block_size, block_size, 1)
        key_valid = block_valid(anchor, counter * block_size, block_size, lengths)
        scores = masked_scores(queries, split_heads(rows_in[:, :, :width]), key_valid)
        row_max, row_sum, weighted = running
        new_max = jnp.maximum(row_max, jnp.max(scores, axis=-1))
        factor = jnp.exp(row_max - new_max)
        expanded = jnp.exp(scores - new_max[..., None])
        row_sum = row_sum * factor + jnp.sum(expanded, axis=-1)
        weighted = weighted * factor[..., None] + jnp.einsum(
            "cqhk,ckhd->cqhd",
            narrow(expanded),
            split_heads(rows_in[:, :, width:]),
            preferred_element_type=jnp.float32,
        )
        return ((new_max, row_sum, weighted), None)

    running, unused = lax.scan(forward_one_block, running, jnp.arange(row_count // block_size))
    return running


def query_piece(gradient, segment, anchor, queries, grad_heads, log_total, row_delta, lengths):
    row_count = segment.shape[1]
    block_size = math.gcd(row_count, key_block)
    width = queries.shape[2] * queries.shape[3]

    def query_one_block(gradient, counter):
        rows_in = lax.dynamic_slice_in_dim(segment, counter * block_size, block_size, 1)
        key_valid = block_valid(anchor, counter * block_size, block_size, lengths)
        key_rows = split_heads(rows_in[:, :, :width])
        scores = masked_scores(queries, key_rows, key_valid)
        attn_probs = jnp.exp(scores - log_total[..., None])
        grad_probs = jnp.einsum(
            "cqhd,ckhd->cqhk",
            grad_heads,
            split_heads(rows_in[:, :, width:]),
            preferred_element_type=jnp.float32,
        )
        grad_scores = narrow(attn_probs * (grad_probs - row_delta[..., None]))
        gradient = (
            gradient
            + jnp.einsum(
                "cqhk,ckhd->cqhd", grad_scores, key_rows, preferred_element_type=jnp.float32
            )
            * 0.125
        )
        return (gradient, None)

    gradient, unused = lax.scan(query_one_block, gradient, jnp.arange(row_count // block_size))
    return gradient


def own_columns(values, place, count):
    share = values.shape[1] // count
    return lax.dynamic_slice_in_dim(values, place * share, share, 1)


MESH = pl.DeviceIdType.MESH
D = 768
PART = 48
VMEM_BYTES = 66500 * 1000


def places():
    band, seq = lax.axis_index("band"), lax.axis_index("seq")
    return lax.div(band, 2), lax.rem(band, 2), lax.div(seq, 2), lax.rem(seq, 2)


def device(y, core, z, x):
    return (y * 2 + core, z * 2 + x)


def remote(src, dst, send, recv, target):
    return pltpu.make_async_remote_copy(
        src_ref=src, dst_ref=dst, send_sem=send, recv_sem=recv, device_id=target, device_id_type=MESH
    )


def greet(partners):
    barrier = pltpu.get_barrier_semaphore()
    for partner in partners:
        pl.semaphore_signal(barrier, inc=1, device_id=partner, device_id_type=MESH)
    pl.semaphore_wait(barrier, len(partners))


class Spread:
    def __init__(self, chunks, recv, up, down, across):
        self.chunks, self.recv, self.up, self.down, self.across = chunks, recv, up, down, across
        self.y, self.core, self.z, self.x = places()

    def copies(self, chunk, slot, sems, at, target):
        first = sum(len(pieces) for pieces in self.chunks[:chunk])
        return [
            remote(
                piece(slot),
                piece(slot),
                sems.at[first + i, at],
                self.recv.at[first + i, slot],
                target,
            )
            for i, piece in enumerate(self.chunks[chunk])
        ]

    def to_up(self, chunk, k):
        slot = (self.z - k) * 2 + self.x
        target = device(self.y, self.core, self.z + 1, self.x)
        return self.copies(chunk, slot, self.up, k, target)

    def to_down(self, chunk, k):
        slot = (self.z + k) * 2 + self.x
        target = device(self.y, self.core, self.z - 1, self.x)
        return self.copies(chunk, slot, self.down, k, target)

    def to_across(self, chunk, row):
        target = device(self.y, self.core, self.z, 1 - self.x)
        return self.copies(chunk, row * 2 + self.x, self.across, row, target)

    def arrived(self, chunk, slot):
        target = device(self.y, self.core, self.z, 1 - self.x)
        for copy in self.copies(chunk, slot, self.across, 0, target):
            copy.wait_recv()

    def all_arrived(self, slot):
        for chunk in range(len(self.chunks)):
            self.arrived(chunk, slot)

    def start(self):
        z = self.z
        for chunk in range(len(self.chunks)):

            @pl.when(z < 3)
            def _():
                for copy in self.to_up(chunk, 0):
                    copy.start()

            @pl.when(z > 0)
            def _():
                for copy in self.to_down(chunk, 0):
                    copy.start()

            for copy in self.to_across(chunk, z):
                copy.start()

    def relay(self, k, chunk):
        z = self.z

        @pl.when(z >= k)
        def _():
            self.arrived(chunk, (z - k) * 2 + self.x)

            @pl.when(z < 3)
            def _():
                for copy in self.to_up(chunk, k):
                    copy.start()

            for copy in self.to_across(chunk, z - k):
                copy.start()

        @pl.when(z + k <= 3)
        def _():
            self.arrived(chunk, (z + k) * 2 + self.x)

            @pl.when(z > 0)
            def _():
                for copy in self.to_down(chunk, k):
                    copy.start()

            for copy in self.to_across(chunk, z + k):
                copy.start()

    def finish(self):
        z = self.z
        for chunk in range(len(self.chunks)):
            for k in range(4):

                @pl.when((z >= k) & (z < 3))
                def _():
                    for copy in self.to_up(chunk, k):
                        copy.wait_send()

                @pl.when((z + k <= 3) & (z > 0))
                def _():
                    for copy in self.to_down(chunk, k):
                        copy.wait_send()

                for copy in self.to_across(chunk, k):
                    copy.wait_send()


def silu(values):
    return values / (1.0 + jnp.exp(-values))


def head_mask(half):
    lane = lax.broadcasted_iota(jnp.int32, (1, 128), 1)
    return (lane < 64) if half == 0 else (lane >= 64)


def keep_head(tile, half):
    return jnp.where(head_mask(half), tile, jnp.zeros_like(tile))


def vmem(*shape, dtype=jnp.bfloat16):
    return pltpu.VMEM(shape, dtype)

PRODUCTS = (
    [(1, 4), (0, 0), (2, 4), (0, 1), (0, 2), (3, 4), (0, 3), (4, 4)]
    + [(5, 5), (6, 6), (9, 8), (9, 9), (7, 7)]
    + [(8, 10), (8, 11), (8, 12)]
)
LEFTS = 8
RIGHTS = 13
TEXT_UNIT = 9
SLOTS = 4
LATER = (0, 1, 3, 7, 9, 10)
IN_VMEM = [
    "mask",
    "frames",
    "cotangent",
    "text",
    "gain",
    "vector",
]
IN_PLACE = [
    "hbm_out",
    "hbm_cross_query",
    "hbm_cross_key",
    "hbm_cross_value",
    "hbm_cross_out",
    "hbm_mlp_in",
    "hbm_mlp_out",
    "hbm_query",
    "hbm_key",
    "hbm_value",
    "hbm_adaln",
    "hbm_time_out",
    "hbm_time_in",
]
OUT_VMEM = [
    "block_out",
    "grad_frames",
    "grad_text",
    "gain_sum",
    "conditions",
    "hiddens",
    "vectors",
    "grad_mods",
    "grad_time_outs",
    "grad_time_firsts",
]
OUT_PLACE = ["pieces"]


def block_scratch():
    n = len(PRODUCTS)
    sem = lambda *shape: pltpu.SemaphoreType.DMA(shape)
    f32 = jnp.float32
    return dict(
        mod=vmem(8, 6 * D, dtype=f32),
        time=vmem(8, 2 * D, dtype=f32),
        qkv=vmem(3, 8, 128, D),
        attended=vmem(128, D, dtype=f32),
        pair=vmem(2, 128, D),
        stats=vmem(128, 128, dtype=f32),
        gathered=vmem(8, 128, D),
        time_in=vmem(256, D),
        fr_recv=sem(2, 8),
        fr_up=sem(2, 4),
        fr_down=sem(2, 4),
        fr_across=sem(2, 4),
        square=vmem(9, D, D),
        mlp_in=vmem(D, 4 * D),
        mlp_out=vmem(4 * D, D),
        adaln_high=vmem(D, 2 * D),
        load_sems=sem(16),
        lefts=vmem(LEFTS, 128, D),
        gt=vmem(RIGHTS, 2, 2, 192, 128),
        grecv=vmem(RIGHTS, 2, 192, 128),
        lrecv=vmem(LEFTS, 128, D),
        pbuf=vmem(SLOTS, 2, 192, D),
        precv=vmem(n, 192, D),
        qbuf=vmem(SLOTS, 2, 192, 384),
        qrecv=vmem(n, 192, 384),
        rbuf=vmem(SLOTS, 4, PART, 384),
        rrecv=vmem(n, 4, PART, 384),
        final=vmem(n, 2, 2, PART, 384),
        ls=sem(LEFTS),
        lr=sem(LEFTS),
        gs=sem(RIGHTS),
        gr=sem(RIGHTS),
        ps=sem(n),
        pr=sem(n),
        qs=sem(n),
        qr=sem(n),
        rs=sem(n, 4),
        rr=sem(n, 4),
        fs=sem(n, 2),
        fr=sem(n, 2),
        out_sems=sem(n),
        heads=vmem(8, 128, D),
        rowstats=vmem(8, 32, 128, dtype=f32),
        sp_recv=sem(3, 8),
        sp_up=sem(3, 4),
        sp_down=sem(3, 4),
        sp_across=sem(3, 4),
        times=vmem(4, 8, 2 * D, dtype=f32),
        vecs=vmem(4, 16, 256),
        ts=sem(2, 4),
        tr=sem(2, 4),
        text_part=vmem(8, 16, D, dtype=f32),
        text_send=vmem(8, 16, D),
        text_recv=vmem(8, 16, D),
        xs=sem(8),
        xr=sem(8),
        sums=vmem(8, D, dtype=f32),
        sums_recv=vmem(8, 8, D, dtype=f32),
        ss=sem(8),
        sr=sem(8),
        clip_sums=vmem(4, 8, D, dtype=f32),
        cs=sem(4),
        cr=sem(4),
        proj=vmem(128, D, dtype=f32),
        middle=vmem(128, D, dtype=f32),
        normed_cross=vmem(128, D, dtype=f32),
        normed_mlp=vmem(128, D, dtype=f32),
        after=vmem(128, D, dtype=f32),
        pre=vmem(4, 128, D, dtype=f32),
        acc=vmem(128, D, dtype=f32),
        grad_mlp=vmem(128, D),
        cross_probs=vmem(12, 128, 128, dtype=f32),
        grad_q=vmem(128, D),
        grad_k=vmem(128, D),
        grad_v=vmem(128, D),
    )


def gelu(v):
    inner = jnp.tanh(0.7978845608028654 * (v + 0.044715 * v * v * v))
    return 0.5 * v * (1.0 + inner)


def gelu_slope(v):
    inner = jnp.tanh(0.7978845608028654 * (v + 0.044715 * v * v * v))
    return 0.5 * (1.0 + inner) + 0.5 * v * (1.0 - inner * inner) * 0.7978845608028654 * (
        1.0 + 3 * 0.044715 * v * v
    )


def silu_slope(v):
    gate = 1.0 / (1.0 + jnp.exp(-v))
    return gate * (1.0 + v * (1.0 - gate))


class Sums:
    def __init__(self, r):
        self.r = r
        self.y, self.core, self.z, self.x = y, core, z, x = places()
        self.across = device(y, core, z, 1 - x)
        self.high, self.low = lax.div(z, 2), lax.rem(z, 2)
        self.along = device(y, core, 2 * self.high + 1 - self.low, x)
        self.clips = [
            None,
            device(y, 1 - core, z, x),
            device(1 - y, core, z, x),
            device(1 - y, 1 - core, z, x),
        ]
        self.done = 0

    def left_copy(self, u):
        r = self.r
        to = self.along if 1 <= u <= 4 else self.across
        return remote(r.lefts.at[u], r.lrecv.at[u], r.ls.at[u], r.lr.at[u], to)

    def right_copy(self, u):
        r = self.r
        if u == 4:
            half, to = 1 - self.low, self.along
        else:
            half, to = 1 - self.x, self.across
        return remote(r.gt.at[u, half], r.grecv.at[u], r.gs.at[u], r.gr.at[u], to)

    def core_copy(self, i):
        r = self.r
        mine = r.pbuf.at[i % SLOTS, 1 - self.core]
        return remote(mine, r.precv.at[i], r.ps.at[i], r.pr.at[i], self.clips[1])

    def y_copy(self, i):
        r = self.r
        mine = r.qbuf.at[i % SLOTS, 1 - self.y]
        return remote(mine, r.qrecv.at[i], r.qs.at[i], r.qr.at[i], self.clips[2])

    def spot(self, i):
        return self.high * 2 + self.x if 1 <= PRODUCTS[i][0] <= 4 else self.z

    def z_copy(self, i, k):
        r = self.r
        to = lax.rem(self.spot(i) + k, 4)
        if 1 <= PRODUCTS[i][0] <= 4:
            target = device(self.y, self.core, 2 * lax.div(to, 2) + self.low, lax.rem(to, 2))
        else:
            target = device(self.y, self.core, to, self.x)
        return remote(
            r.rbuf.at[i % SLOTS, to], r.rrecv.at[i, k], r.rs.at[i, k], r.rr.at[i, k], target
        )

    def last_y_copy(self, i):
        r = self.r
        piece = r.final.at[i, self.core, self.y]
        return remote(piece, piece, r.fs.at[i, 0], r.fr.at[i, 0], self.clips[2])

    def last_core_copy(self, i):
        r = self.r
        piece = r.final.at[i, self.core]
        return remote(piece, piece, r.fs.at[i, 1], r.fr.at[i, 1], self.clips[1])

    def out_copy(self, i):
        r = self.r
        return pltpu.make_async_copy(r.final.at[i], r.pieces.at[i], r.out_sems.at[i])

    def post_left(self, u, values):
        self.r.lefts[u] = values
        self.left_copy(u).start()

    def post_right(self, u, values):
        turned = narrow(jnp.transpose(values.astype(jnp.float32)))
        for s in range(8):
            for c in range(2):
                at = s * 96 + c * PART
                half, block = (s // 2 % 2, s // 4 * 2 + s % 2) if u == 4 else (s % 2, s // 2)
                self.r.gt[u, half, c, pl.ds(block * PART, PART), :] = turned[at : at + PART]
        self.right_copy(u).start()

    def multiply(self, i):
        r = self.r
        left, right = PRODUCTS[i]
        if left < LEFTS and left not in [l for l, unused in PRODUCTS[:i]]:
            self.left_copy(left).wait_recv()
        if right not in [r for unused, r in PRODUCTS[:i]]:
            self.right_copy(right).wait_recv()
        if i >= SLOTS:
            self.core_copy(i - SLOTS).wait_send()
        for c in range(2):
            mine, theirs = r.gt[right, self.low if right == 4 else self.x, c], r.grecv[right, c]
            if left == TEXT_UNIT:
                both = narrow(mine.astype(jnp.float32) + theirs.astype(jnp.float32))
                part = product(both, r.text[...])
            else:
                both = (r.pair[0], r.pair[1]) if left == 8 else (r.lefts[left], r.lrecv[left])
                part = product(
                    jnp.concatenate([mine, theirs], axis=1), jnp.concatenate(both, axis=0)
                )
            r.pbuf[i % SLOTS, c] = narrow(part)
        self.core_copy(i).start()

    def add_core(self, i):
        r = self.r
        self.core_copy(i).wait_recv()
        if i >= SLOTS:
            self.y_copy(i - SLOTS).wait_send()
        total = narrow(
            r.pbuf[i % SLOTS, self.core].astype(jnp.float32) + r.precv[i].astype(jnp.float32)
        )
        r.qbuf[i % SLOTS, 0] = total[:, :384]
        r.qbuf[i % SLOTS, 1] = total[:, 384:]
        self.y_copy(i).start()

    def add_y(self, i):
        r = self.r
        self.y_copy(i).wait_recv()
        if i >= SLOTS:
            for k in (1, 2, 3):
                self.z_copy(i - SLOTS, k).wait_send()
        total = narrow(
            r.qbuf[i % SLOTS, self.y].astype(jnp.float32) + r.qrecv[i].astype(jnp.float32)
        )
        for k in range(4):
            r.rbuf[i % SLOTS, k] = total[k * PART : (k + 1) * PART]
        for k in (1, 2, 3):
            self.z_copy(i, k).start()

    def add_z(self, i):
        r = self.r
        for k in (1, 2, 3):
            self.z_copy(i, k).wait_recv()
        total = r.rbuf[i % SLOTS, self.spot(i)].astype(jnp.float32)
        for k in (1, 2, 3):
            total = total + r.rrecv[i, k].astype(jnp.float32)
        r.final[i, self.core, self.y] = narrow(total)
        self.last_y_copy(i).start()

    def pass_on(self, i):
        self.last_y_copy(i).wait_recv()
        self.last_core_copy(i).start()

    def output(self, i):
        self.last_core_copy(i).wait_recv()
        self.out_copy(i).start()

    def step(self, times=1):
        n = len(PRODUCTS)
        stages = (
            self.multiply,
            self.add_core,
            self.add_y,
            self.add_z,
            self.pass_on,
            self.output,
        )
        for unused in range(times):
            for later, stage in reversed(list(zip(LATER, stages))):
                if 0 <= self.done - later < n:
                    stage(self.done - later)
            self.done += 1

    def finish(self):
        n = len(PRODUCTS)
        while self.done < n + LATER[-1]:
            self.step()
        for u in range(LEFTS):
            self.left_copy(u).wait_send()
        for u in range(RIGHTS):
            self.right_copy(u).wait_send()
        for i in range(n):
            if i >= n - SLOTS:
                self.core_copy(i).wait_send()
                self.y_copy(i).wait_send()
                for k in (1, 2, 3):
                    self.z_copy(i, k).wait_send()
            self.last_y_copy(i).wait_send()
            self.last_core_copy(i).wait_send()
            self.out_copy(i).wait()


def block_kernel(length_ref, *refs):
    names = IN_VMEM + IN_PLACE + OUT_VMEM + OUT_PLACE + list(block_scratch())
    r = types.SimpleNamespace(**dict(zip(names, refs, strict=True)))
    y, core, z, x = places()
    me, band = z * 2 + x, y * 2 + core
    peers = [device(y, core, lax.div(s, 2), lax.rem(s, 2)) for s in [lax.rem(me + k, 8) for k in range(8)]]
    r.cross_q, r.cross_k, r.cross_v, r.grad_heads = [r.gathered.at[i] for i in range(4, 8)]
    sums = Sums(r)

    def load(i, src, dst):
        return pltpu.make_async_copy(src, dst, r.load_sems.at[i])

    squares = (
        r.hbm_out,
        r.hbm_cross_query,
        r.hbm_cross_key,
        r.hbm_cross_value,
        r.hbm_cross_out,
        r.hbm_query,
        r.hbm_key,
        r.hbm_value,
        r.hbm_time_out,
    )
    OUT, CQ, CK, CV, CO, WQ, WK, WV, TIME = range(9)
    loads = [load(i, ref, r.square.at[i]) for i, ref in enumerate(squares)]
    loads.append(load(9, r.hbm_mlp_in, r.mlp_in))
    loads.append(load(10, r.hbm_mlp_out, r.mlp_out))
    loads.append(load(11, r.hbm_adaln.at[:, pl.ds(3072, 1536)], r.adaln_high))
    adaln_low = load(12, r.hbm_adaln.at[:, pl.ds(0, 3072)], r.mlp_in)
    load_time_in = load(13, r.hbm_time_in, r.time_in)
    own_frames = load(14, r.frames, r.gathered.at[me])
    own_frames.start()
    load_time_in.start()
    loads[TIME].start()
    adaln_low.start()
    for i in (11, WQ, WK, WV, OUT, CK, CV, CQ, CO, 10):
        loads[i].start()
    greet(peers[1:] + sums.clips[1:])
    own_frames.wait()

    def half(ref, i):
        return lambda slot: ref.at[slot, i * 64 : (i + 1) * 64]

    chunks = [[half(r.gathered, i)] for i in range(2)]
    neighbours = Spread(chunks, r.fr_recv, r.fr_up, r.fr_down, r.fr_across)
    neighbours.start()

    def clip_copy(refs, sems, recvs, j):
        return [
            remote(ref.at[band], ref.at[band], sems.at[i, j], recvs.at[i, j], sums.clips[j])
            for i, ref in enumerate(refs)
        ]

    length = length_ref[0]

    def row_valid():
        return lax.broadcasted_iota(jnp.int32, (128, 1), 0) + me * 128 < length

    def modulation(i):
        return r.mod[0:1, i * D : (i + 1) * D]

    def over_rows(values):
        return jnp.sum(values, axis=0, keepdims=True)

    lane = lax.broadcasted_iota(jnp.int32, (1, 128), 1)
    text_valid = r.mask[...] != 0
    gain = r.gain[...].astype(jnp.float32)

    def tile_at(tile):
        return pl.ds(pl.multiple_of(tile * 128, 128), 128)

    load_time_in.wait()
    first = product(r.vector[...], r.time_in[...])
    hidden = narrow(silu(first))
    loads[TIME].wait()
    second = product(hidden, r.square[TIME])
    condition = narrow(silu(second))
    r.time[:, 0:D] = first[0:8]
    r.time[:, D : 2 * D] = second[0:8]
    r.times[band] = r.time[...]
    r.vecs[band] = r.vector[...]
    for j in (1, 2, 3):
        for copy in clip_copy((r.times, r.vecs), r.ts, r.tr, j):
            copy.start()

    adaln_low.wait()
    r.mod[:, 0:1536] = product(condition, r.mlp_in[:, 0:1536])[0:8]
    neighbours.relay(1, 0)
    r.mod[:, 1536:3072] = product(condition, r.mlp_in[:, 1536:3072])[0:8]
    loads[9].start()
    neighbours.relay(1, 1)
    loads[11].wait()
    r.mod[:, 3072:4608] = product(condition, r.adaln_high[...])[0:8]
    for i in (WQ, WK, WV):
        loads[i].wait()
    def project(row, column):
        normed, unused = layer_norm(r.gathered[row * 2 + column].astype(jnp.float32))
        low = narrow(normed * (1.0 + modulation(1)) + modulation(0))
        for i in range(3):
            r.qkv[i, row * 2 + column] = narrow(product(low, r.square[WQ + i]))
        return low

    def own_column(row, unused):
        low = project(row, x)

        @pl.when(row == z)
        def _():
            r.pair[0] = low

        return unused

    def other_column(row, unused):
        neighbours.all_arrived(row * 2 + 1 - x)
        low = project(row, 1 - x)

        @pl.when(row == z)
        def _():
            r.pair[1] = low

        return unused

    for k in (2, 3):
        for chunk in range(2):
            neighbours.relay(k, chunk)
    lax.fori_loop(0, 4, own_column, 0)
    lax.fori_loop(0, 4, other_column, 0)
    key_valid = lax.broadcasted_iota(jnp.int32, (1, 1024), 1) < length

    def attend_pair(tile, stats):
        at = tile_at(tile)
        query = r.qkv[0, me, :, at]
        keys = r.qkv[1, :, :, at].reshape(1024, 128)
        values = r.qkv[2, :, :, at].reshape(1024, 128)
        outs = []
        for half in range(2):
            scores = transposed_right(keep_head(query, half), keys) * 0.125
            scores = jnp.where(key_valid, scores, masked_value)
            row_max = jnp.max(scores, axis=1, keepdims=True)
            expanded = jnp.exp(scores - row_max)
            row_sum = jnp.sum(expanded, axis=1, keepdims=True)
            outs.append(product(narrow(expanded), values) / row_sum)
            stats = jnp.where(lane == tile * 2 + half, row_max + jnp.log(row_sum), stats)
        r.attended[:, at] = jnp.where(head_mask(0), outs[0], outs[1])
        return stats

    r.stats[...] = lax.fori_loop(0, 6, attend_pair, jnp.zeros((128, 128), jnp.float32))
    neighbours.finish()
    sums.post_left(7, narrow(r.attended[...]))
    r.grad_mlp[...] = narrow(
        modulation(5) * jnp.where(row_valid(), r.cotangent[...].astype(jnp.float32), 0.0)
    )
    sums.post_right(4, r.grad_mlp[...])
    loads[OUT].wait()
    r.proj[...] = product(r.lefts[7], r.square[OUT])
    r.middle[...] = r.frames[...].astype(jnp.float32) + modulation(2) * r.proj[...]
    normed, scaling_cross = layer_norm(r.middle[...])
    r.normed_cross[...] = normed
    sums.post_left(6, narrow(normed * gain))
    loads[CK].wait()
    r.cross_k[...] = narrow(product(r.text[...], r.square[CK]))
    loads[CV].wait()
    r.cross_v[...] = narrow(product(r.text[...], r.square[CV]))
    loads[CQ].wait()
    r.cross_q[...] = narrow(product(r.lefts[6], r.square[CQ]))

    def cross_pair(tile, unused):
        at = tile_at(tile)
        query, keys, values = r.cross_q[:, at], r.cross_k[:, at], r.cross_v[:, at]
        outs = []
        for half in range(2):
            scores = transposed_right(keep_head(query, half), keys) * 0.125
            scores = jnp.where(text_valid, scores, masked_value)
            row_max = jnp.max(scores, axis=1, keepdims=True)
            total = row_max + jnp.log(jnp.sum(jnp.exp(scores - row_max), axis=1, keepdims=True))
            probs = jnp.exp(scores - total)
            r.cross_probs[tile * 2 + half] = probs
            outs.append(product(narrow(probs), values))
        r.lefts[5, :, at] = narrow(jnp.where(head_mask(0), outs[0], outs[1]))
        return unused

    lax.fori_loop(0, 6, cross_pair, 0)
    sums.left_copy(5).start()
    loads[CO].wait()
    r.after[...] = r.middle[...] + product(r.lefts[5], r.square[CO])
    normed, scaling_mlp = layer_norm(r.after[...])
    r.normed_mlp[...] = normed
    sums.post_left(0, narrow(normed * (1.0 + modulation(4)) + modulation(3)))
    loads[9].wait()
    loads[10].wait()
    for j in range(4):
        pre = product(r.lefts[0], r.mlp_in[:, j * D : (j + 1) * D])
        r.pre[j] = pre
        sums.post_left(1 + j, narrow(gelu(pre)))
        part = product(r.lefts[1 + j], r.mlp_out[j * D : (j + 1) * D, :])
        r.acc[...] = part if j == 0 else r.acc[...] + part
    frames = r.frames[...].astype(jnp.float32)
    r.block_out[...] = narrow(
        jnp.where(row_valid(), r.after[...] + modulation(5) * r.acc[...], frames)
    )
    grad_res = jnp.where(row_valid(), r.cotangent[...].astype(jnp.float32), 0.0)
    r.sums[5:6, :] = over_rows(grad_res * r.acc[...])
    for j in range(4):
        slope = gelu_slope(r.pre[j])
        grad = narrow(slope * transposed_right(r.grad_mlp[...], r.mlp_out[j * D : (j + 1) * D, :]))
        r.gathered[j] = grad
        for part in range(2):
            s = j * 2 + part
            turned = narrow(
                jnp.transpose(grad[:, part * 384 : (part + 1) * 384].astype(jnp.float32))
            )
            for u in range(4):
                for c in range(2):
                    at = u * 96 + c * PART
                    r.gt[u, s % 2, c, pl.ds((s // 2) * PART, PART), :] = turned[at : at + PART]
    for u in range(4):
        sums.right_copy(u).start()
    for j in range(4):
        part = transposed_right(r.gathered[j], r.mlp_in[:, j * D : (j + 1) * D])
        r.acc[...] = part if j == 0 else r.acc[...] + part
    adaln_low.start()
    sums.step(1)
    r.sums[3:4, :] = over_rows(r.acc[...])
    r.sums[4:5, :] = over_rows(r.acc[...] * r.normed_mlp[...])
    grad_res = jnp.where(row_valid(), r.cotangent[...].astype(jnp.float32), 0.0)
    r.after[...] = grad_res + norm_back(
        r.normed_mlp[...], scaling_mlp, r.acc[...] * (1.0 + modulation(4))
    )
    low = narrow(r.after[...])
    sums.post_right(5, low)
    r.grad_heads[...] = narrow(transposed_right(low, r.square[CO]))

    def cross_pair_back(tile, unused):
        at = tile_at(tile)
        query, keys, values = r.cross_q[:, at], r.cross_k[:, at], r.cross_v[:, at]
        grad = r.grad_heads[:, at]
        outs = []
        for half in range(2):
            probs = r.cross_probs[tile * 2 + half]
            grad_probs = transposed_right(keep_head(grad, half), values)
            inner = jnp.sum(probs * grad_probs, axis=1, keepdims=True)
            scores = narrow(probs * (grad_probs - inner)).astype(jnp.float32)
            outs.append(
                (
                    product(narrow(scores), keys),
                    product(narrow(jnp.transpose(scores)), query),
                    product(narrow(jnp.transpose(probs)), grad),
                )
            )
        grad_q, grad_k, grad_v = [jnp.where(head_mask(0), a, b) for a, b in zip(*outs)]
        r.grad_q[:, at] = narrow(grad_q * 0.125)
        r.grad_k[:, at] = narrow(grad_k * 0.125)
        r.grad_v[:, at] = narrow(grad_v)
        return unused

    lax.fori_loop(0, 6, cross_pair_back, 0)
    sums.post_right(6, r.grad_q[...])
    sums.step(1)
    grad_cross_in = transposed_right(r.grad_q[...], r.square[CQ])
    r.sums[6:7, :] = over_rows(grad_cross_in * r.normed_cross[...])
    r.sums[7:8, :] = jnp.zeros((1, D), jnp.float32)
    r.middle[...] = r.after[...] + norm_back(
        r.normed_cross[...], scaling_cross, grad_cross_in * gain
    )
    low = narrow(modulation(2) * r.middle[...])
    grad_heads = narrow(transposed_right(low, r.square[OUT]))
    r.heads[me] = grad_heads
    products = grad_heads.astype(jnp.float32) * r.attended[...]
    delta = jnp.zeros((128, 128), jnp.float32)
    for h in range(12):
        tile = products[:, (h // 2) * 128 : (h // 2 + 1) * 128]
        inner = jnp.sum(jnp.where(head_mask(h % 2), tile, 0.0), axis=1, keepdims=True)
        delta = jnp.where(lane == h, inner, delta)
    r.rowstats[me] = jnp.concatenate(
        [jnp.transpose(r.stats[...])[:16], jnp.transpose(delta)[:16]], axis=0
    )
    chunks = [[half(r.heads, 0), lambda slot: r.rowstats.at[slot]], [half(r.heads, 1)]]
    spread = Spread(chunks, r.sp_recv, r.sp_up, r.sp_down, r.sp_across)
    spread.start()
    sums.post_right(7, low)
    r.sums[2:3, :] = over_rows(r.middle[...] * r.proj[...])
    sums.post_right(8, r.grad_k[...])
    sums.post_right(9, r.grad_v[...])
    text_grad = transposed_right(r.grad_k[...], r.square[CK]) + transposed_right(
        r.grad_v[...], r.square[CV]
    )
    for s in range(8):
        r.text_part[s] = text_grad[s * 16 : (s + 1) * 16]
        r.text_send[s] = narrow(text_grad[s * 16 : (s + 1) * 16])

    def text_copy(k):
        return remote(
            r.text_send.at[lax.rem(me + k, 8)], r.text_recv.at[k], r.xs.at[k], r.xr.at[k], peers[k]
        )

    for k in range(1, 8):
        text_copy(k).start()
    sums.step(2)
    spread.relay(1, 0)
    key_valid = lax.broadcasted_iota(jnp.int32, (1, 1024), 1) < length

    def query_pair(tile, unused):
        at = tile_at(tile)
        query, grad = r.qkv[0, me, :, at], r.heads[me, :, at]
        keys = r.qkv[1, :, :, at].reshape(1024, 128)
        values = r.qkv[2, :, :, at].reshape(1024, 128)
        tile_product = grad.astype(jnp.float32) * r.attended[:, at]
        outs = []
        for half in range(2):
            scores = transposed_right(keep_head(query, half), keys) * 0.125
            scores = jnp.where(key_valid, scores, masked_value)
            total = jnp.sum(
                jnp.where(lane == tile * 2 + half, r.stats[...], 0.0), axis=1, keepdims=True
            )
            inner = jnp.sum(jnp.where(head_mask(half), tile_product, 0.0), axis=1, keepdims=True)
            grad_probs = transposed_right(keep_head(grad, half), values)
            outs.append(product(narrow(jnp.exp(scores - total) * (grad_probs - inner)), keys))
        r.grad_q[:, at] = narrow(jnp.where(head_mask(0), outs[0], outs[1]) * 0.125)
        return unused

    lax.fori_loop(0, 1, query_pair, 0)
    spread.relay(1, 1)
    lax.fori_loop(1, 3, query_pair, 0)
    sums.step(2)
    spread.relay(2, 0)
    lax.fori_loop(3, 4, query_pair, 0)
    spread.relay(2, 1)
    lax.fori_loop(4, 6, query_pair, 0)
    sums.step(3)
    spread.relay(3, 0)
    spread.relay(3, 1)
    sums.post_right(10, r.grad_q[...])
    sums.step(4)
    for row in range(4):
        spread.all_arrived(row * 2 + 1 - x)

    def key_pair(tile, unused):
        at = tile_at(tile)
        key, value = r.qkv[1, me, :, at], r.qkv[2, me, :, at]
        queries = r.qkv[0, :, :, at].reshape(1024, 128)
        grads = r.heads[:, :, at].reshape(1024, 128)
        outs = []
        for half in range(2):
            h = tile * 2 + half
            total = jnp.concatenate([r.rowstats[s, pl.ds(h, 1), :] for s in range(8)], axis=1)
            inner = jnp.concatenate([r.rowstats[s, pl.ds(16 + h, 1), :] for s in range(8)], axis=1)
            scores = transposed_right(keep_head(key, half), queries) * 0.125
            scores = jnp.where(row_valid(), scores, masked_value)
            probs = jnp.exp(scores - total)
            grad_probs = transposed_right(keep_head(value, half), grads)
            grad_scores = narrow(probs * (grad_probs - inner))
            outs.append((product(grad_scores, queries), product(narrow(probs), grads)))
        grad_k, grad_v = [jnp.where(head_mask(0), a, b) for a, b in zip(*outs)]
        r.grad_k[:, at] = narrow(grad_k * 0.125)
        r.grad_v[:, at] = narrow(grad_v)
        return unused

    lax.fori_loop(0, 6, key_pair, 0)
    sums.post_right(11, r.grad_k[...])
    sums.post_right(12, r.grad_v[...])
    sums.step(1)
    grad_in = (
        transposed_right(r.grad_q[...], r.square[WQ])
        + transposed_right(r.grad_k[...], r.square[WK])
        + transposed_right(r.grad_v[...], r.square[WV])
    )
    r.acc[...] = grad_in
    normed, scaling = layer_norm(r.frames[...].astype(jnp.float32))
    r.sums[0:1, :] = over_rows(r.acc[...])
    r.sums[1:2, :] = over_rows(r.acc[...] * normed)

    def sums_copy(k):
        return remote(r.sums, r.sums_recv.at[k], r.ss.at[k], r.sr.at[k], peers[k])

    for k in range(1, 8):
        sums_copy(k).start()
    sums.step(3)
    grads = r.middle[...] + norm_back(normed, scaling, r.acc[...] * (1.0 + modulation(1)))
    r.grad_frames[...] = narrow(
        jnp.where(row_valid(), grads, r.cotangent[...].astype(jnp.float32))
    )
    total = r.sums[...]
    for k in range(1, 8):
        sums_copy(k).wait_recv()
        total = total + r.sums_recv[k]
    r.clip_sums[band] = total

    def total_copy(j):
        return remote(
            r.clip_sums.at[band], r.clip_sums.at[band], r.cs.at[j], r.cr.at[j], sums.clips[j]
        )

    for j in (1, 2, 3):
        total_copy(j).start()
    sums.step(2)
    for j in (1, 2, 3):
        total_copy(j).wait_recv()
        for copy in clip_copy((r.times, r.vecs), r.ts, r.tr, j):
            copy.wait_recv()
    r.gain_sum[0:1, :] = (r.clip_sums[0, 6:7] + r.clip_sums[1, 6:7]) + (
        r.clip_sums[2, 6:7] + r.clip_sums[3, 6:7]
    )
    r.gain_sum[1:8, :] = jnp.zeros((7, D), jnp.float32)

    def by_clip(pieces):
        return jnp.concatenate(pieces + [jnp.zeros((12, pieces[0].shape[1]), jnp.float32)], axis=0)

    for i in range(6):
        r.grad_mods[:, i * D : (i + 1) * D] = narrow(
            by_clip([r.clip_sums[b, i : i + 1] for b in range(4)])
        )
    firsts = by_clip([r.times[b, 0:1, 0:D] for b in range(4)])
    seconds = by_clip([r.times[b, 0:1, D : 2 * D] for b in range(4)])
    r.hiddens[...] = narrow(silu(firsts))
    r.conditions[...] = narrow(silu(seconds))
    for b in range(4):
        r.vectors[b] = r.vecs[b]
    adaln_low.wait()
    grad_condition = transposed_right(r.grad_mods[:, :3072], r.mlp_in[...]) + transposed_right(
        r.grad_mods[:, 3072:], r.adaln_high[...]
    )
    low = narrow(silu_slope(seconds) * grad_condition)
    r.grad_time_outs[...] = low
    r.grad_time_firsts[...] = silu_slope(firsts) * transposed_right(low, r.square[TIME])
    total = r.text_part[me]
    for k in range(1, 8):
        text_copy(k).wait_recv()
        total = total + r.text_recv[k].astype(jnp.float32)
    r.grad_text[...] = total
    sums.finish()
    spread.finish()
    for k in range(1, 8):
        text_copy(k).wait_send()
        sums_copy(k).wait_send()
    for j in (1, 2, 3):
        total_copy(j).wait_send()
        for copy in clip_copy((r.times, r.vecs), r.ts, r.tr, j):
            copy.wait_send()


def block(length, vmem_args, place_args):
    in_vmem = pl.BlockSpec(memory_space=pltpu.VMEM)
    in_place = pl.BlockSpec(memory_space=pl.ANY)
    shape = jax.ShapeDtypeStruct
    f32, bf16 = jnp.float32, jnp.bfloat16
    return pl.pallas_call(
        block_kernel,
        out_shape=(
            shape((128, D), bf16),
            shape((128, D), bf16),
            shape((16, D), f32),
            shape((8, D), f32),
            shape((16, D), bf16),
            shape((16, D), bf16),
            shape((4, 16, 256), bf16),
            shape((16, 6 * D), bf16),
            shape((16, D), bf16),
            shape((16, D), f32),
            shape((len(PRODUCTS), 2, 2, PART, 384), bf16),
        ),
        in_specs=[pl.BlockSpec(memory_space=pltpu.SMEM)]
        + [in_vmem] * len(IN_VMEM)
        + [in_place] * len(IN_PLACE),
        out_specs=(in_vmem,) * len(OUT_VMEM) + (in_place,) * len(OUT_PLACE),
        scratch_shapes=list(block_scratch().values()),
        compiler_params=pltpu.CompilerParams(
            collective_id=0, has_side_effects=True, vmem_limit_bytes=VMEM_BYTES
        ),
    )(length, *vmem_args, *place_args)


SQUARES = (8, 9, 12, 10, 11, 13, 14, 15)
FINAL_IN = [
    "pieces",
    "block_out",
    "grad_frames",
    "grad_text",
    "gain_sum",
    "conditions",
    "hiddens",
    "vectors",
    "grad_mods",
    "grad_time_outs",
    "grad_time_firsts",
]
FINAL_SHAPES = (
    [((128, D), jnp.bfloat16), ((128, D), jnp.bfloat16), ((16, D), jnp.float32)]
    + [((96, 256), jnp.float32), ((96, D), jnp.float32), ((576, D), jnp.float32)]
    + [((1, 96), jnp.float32), ((D, 384), jnp.float32), ((96, 4 * D), jnp.float32)]
    + [((96, D), jnp.float32)] * 8
)


def final_kernel(*refs):
    r = types.SimpleNamespace(**dict(zip(FINAL_IN, refs)))
    count = len(FINAL_SHAPES)
    rest = refs[len(FINAL_IN) :]
    outs, staged, (turned_mods, turned_small, sems) = rest[:count], rest[count : 2 * count], rest[2 * count :]
    seq = lax.axis_index("seq")

    def put(i, values):
        staged[i][...] = values
        copy(i).start()

    def copy(i):
        return pltpu.make_async_copy(staged[i], outs[i], sems.at[i])

    def whole(p):
        return jnp.concatenate(
            [jnp.concatenate([r.pieces[p, c, h] for h in range(2)], axis=1) for c in range(2)],
            axis=0,
        ).astype(jnp.float32)

    put(7, jnp.transpose(jnp.concatenate([whole(PRODUCTS.index((0, j))) for j in range(4)], axis=0)))
    for j in range(4):
        staged[8][:, j * D : (j + 1) * D] = whole(PRODUCTS.index((1 + j, 4)))
    copy(8).start()
    for j, p in enumerate(SQUARES):
        put(9 + j, whole(p))
    put(0, r.block_out[...])
    put(1, r.grad_frames[...])
    put(2, r.grad_text[...])
    turned_mods[...] = jnp.transpose(r.grad_mods[...].astype(jnp.float32))
    put(
        5,
        product(
            narrow(turned_mods[pl.ds(pl.multiple_of(seq * 576, 64), 576), :]), r.conditions[...]
        ),
    )
    own = pl.ds(pl.multiple_of(seq * 96, 32), 96)
    turned_small[0] = jnp.transpose(r.grad_time_outs[...].astype(jnp.float32))
    put(4, product(narrow(turned_small[0, own, :]), r.hiddens[...]))
    turned_small[1] = jnp.transpose(r.grad_time_firsts[...])
    rows = [r.vectors[b, 0:1].astype(jnp.float32) for b in range(4)]
    vectors = jnp.concatenate(rows + [jnp.zeros((12, 256), jnp.float32)], axis=0)
    put(
        3,
        jnp.dot(
            turned_small[1, own, :],
            vectors,
            precision=lax.Precision.HIGHEST,
            preferred_element_type=jnp.float32,
        ),
    )
    gains = jnp.concatenate([r.gain_sum[...], jnp.zeros((8, D), jnp.float32)], axis=0)
    turned_small[2] = jnp.transpose(gains)
    put(6, jnp.transpose(turned_small[2, own, :])[0:1])
    for i in range(count):
        copy(i).wait()


def finish(values):
    in_vmem = pl.BlockSpec(memory_space=pltpu.VMEM)
    in_place = pl.BlockSpec(memory_space=pl.ANY)
    return pl.pallas_call(
        final_kernel,
        out_shape=tuple(jax.ShapeDtypeStruct(*shape) for shape in FINAL_SHAPES),
        in_specs=[in_vmem] * len(FINAL_IN),
        out_specs=(in_place,) * len(FINAL_SHAPES),
        scratch_shapes=[pltpu.VMEM(*shape) for shape in FINAL_SHAPES]
        + [
            vmem(6 * D, 16, dtype=jnp.float32),
            vmem(3, D, 16, dtype=jnp.float32),
            pltpu.SemaphoreType.DMA((len(FINAL_SHAPES),)),
        ],
        compiler_params=pltpu.CompilerParams(vmem_limit_bytes=VMEM_BYTES),
    )(*values)


def on_device(
    frames,
    text,
    timesteps,
    frame_lengths,
    text_mask,
    cotangent,
    w_time_in,
    w_time_out,
    w_adaln,
    w_query,
    w_key,
    w_value,
    w_attn_out,
    cross_gain,
    w_cross_query,
    w_cross_key,
    w_cross_value,
    w_cross_out,
    w_mlp_in,
    w_mlp_out,
):
    vector = jnp.broadcast_to(narrow(time_embed(timesteps, w_time_in.shape[0])), (16, 256))
    (
        block_out,
        grad_frames,
        grad_text,
        gain_sum,
        conditions,
        hiddens,
        vectors,
        grad_mods,
        grad_time_outs,
        grad_time_firsts,
        pieces,
    ) = block(
        frame_lengths,
        (
            text_mask,
            frames[0],
            cotangent[0],
            text[0],
            cross_gain[None],
            vector,
        ),
        (
            w_attn_out,
            w_cross_query,
            w_cross_key,
            w_cross_value,
            w_cross_out,
            w_mlp_in,
            w_mlp_out,
            w_query,
            w_key,
            w_value,
            w_adaln,
            w_time_out,
            w_time_in,
        ),
    )
    (
        block_out,
        grad_frames,
        grad_text,
        sum_time_in,
        sum_time_out,
        sum_adaln,
        sum_gain,
        sum_mlp_in,
        sum_mlp_out,
        sum_cross_out,
        sum_cross_query,
        sum_attn_out,
        sum_cross_key,
        sum_cross_value,
        sum_query,
        sum_key,
        sum_value,
    ) = finish(
        (
            pieces,
            block_out,
            grad_frames,
            grad_text,
            gain_sum,
            conditions,
            hiddens,
            vectors,
            grad_mods,
            grad_time_outs,
            grad_time_firsts,
        )
    )
    return (
        block_out[None],
        grad_frames[None],
        grad_text[None],
        sum_time_in.T,
        sum_time_out.T,
        sum_adaln.T,
        sum_query.T,
        sum_key.T,
        sum_value.T,
        sum_attn_out.T,
        sum_gain[0],
        sum_cross_query.T,
        sum_cross_key.T,
        sum_cross_value.T,
        sum_cross_out.T,
        sum_mlp_in,
        sum_mlp_out.T,
    )


def on_device_general(
    frames,
    text,
    timesteps,
    frame_lengths,
    text_mask,
    cotangent,
    w_time_in,
    w_time_out,
    w_adaln,
    w_query,
    w_key,
    w_value,
    w_attn_out,
    cross_gain,
    w_cross_query,
    w_cross_key,
    w_cross_value,
    w_cross_out,
    w_mlp_in,
    w_mlp_out,
):
    clips = frames.shape[0]
    rows = frames.shape[1]
    width = frames.shape[2]
    tokens = clips * rows
    text_count = text.shape[1]
    seq_place = lax.axis_index("seq")
    seq_count = lax.axis_size("seq")
    offset = seq_place * rows
    inputs = frames.astype(jnp.float32)
    own_valid = (offset + jnp.arange(rows))[None, :] < frame_lengths[:, None]
    row_valid = own_valid[:, :, None]
    text_valid = text_mask != 0

    def flatten(values):
        return values.reshape(tokens, values.shape[-1])

    def unflatten(values):
        return values.reshape(clips, rows, values.shape[-1])

    time_vector = narrow(time_embed(timesteps, w_time_in.shape[0]))
    time_first = product(time_vector, w_time_in)
    time_hidden = narrow(jax.nn.silu(time_first))
    time_out = product(time_hidden, w_time_out)
    condition = narrow(jax.nn.silu(time_out))
    modulation = product(condition, w_adaln)
    shift_attn, scale_attn, gate_attn, shift_mlp, scale_mlp, gate_mlp = [
        piece[:, None, :] for piece in jnp.split(modulation, 6, axis=1)
    ]
    normed_attn, scaling_attn = layer_norm(inputs)
    attn_in = narrow(normed_attn * (1.0 + scale_attn) + shift_attn)
    attn_flat = flatten(attn_in)
    query_flat = narrow(product(attn_flat, w_query))
    queries = split_heads(unflatten(query_flat))
    kv_local = unflatten(
        jnp.concatenate(
            [narrow(product(attn_flat, w_key)), narrow(product(attn_flat, w_value))], axis=1
        )
    )
    start_state = (
        jnp.full((clips, rows, H), -1e30, jnp.float32),
        jnp.zeros((clips, rows, H), jnp.float32),
        jnp.zeros((clips, rows, H, HD), jnp.float32),
    )
    row_max, row_sum, weighted = forward_piece(
        start_state,
        lax.all_gather(kv_local, "seq", axis=1, tiled=True),
        jnp.int32(0),
        queries,
        frame_lengths,
    )
    attended = weighted / row_sum[..., None]
    log_total = row_max + jnp.log(row_sum)
    attn_low = narrow(attended.reshape(clips, rows, width))
    attn_proj = unflatten(product(flatten(attn_low), w_attn_out))
    middle = inputs + gate_attn * attn_proj
    normed_cross, scaling_cross = layer_norm(middle)
    gain_values = cross_gain.astype(jnp.float32)
    cross_in = narrow(normed_cross * gain_values)
    cross_queries = split_heads(unflatten(narrow(product(flatten(cross_in), w_cross_query))))
    text_flat = text.reshape(clips * text_count, width)
    cross_keys = split_heads(
        narrow(product(text_flat, w_cross_key)).reshape(clips, text_count, width)
    )
    cross_values = split_heads(
        narrow(product(text_flat, w_cross_value)).reshape(clips, text_count, width)
    )
    cross_scores = masked_scores(cross_queries, cross_keys, text_valid)
    cross_max = jnp.max(cross_scores, axis=-1, keepdims=True)
    cross_total = cross_max + jnp.log(
        jnp.sum(jnp.exp(cross_scores - cross_max), axis=-1, keepdims=True)
    )
    cross_probs = jnp.exp(cross_scores - cross_total)
    cross_probs_low = narrow(cross_probs)
    cross_attended = jnp.einsum(
        "cqhk,ckhd->cqhd", cross_probs_low, cross_values, preferred_element_type=jnp.float32
    )
    cross_low = narrow(cross_attended.reshape(clips, rows, width))
    after_cross = middle + unflatten(product(flatten(cross_low), w_cross_out))
    normed_mlp, scaling_mlp = layer_norm(after_cross)
    mlp_in = narrow(normed_mlp * (1.0 + scale_mlp) + shift_mlp)
    pre_act = product(flatten(mlp_in), w_mlp_in)
    activation = narrow(jax.nn.gelu(pre_act, approximate=True))
    mlp_out = unflatten(product(activation, w_mlp_out))
    result = after_cross + gate_mlp * mlp_out
    block_out = jnp.where(row_valid, result, inputs).astype(jnp.bfloat16)
    grad_out = cotangent.astype(jnp.float32)
    grad_res = jnp.where(row_valid, grad_out, 0.0)
    grad_mlp = flatten(narrow(gate_mlp * grad_res))
    grad_w_mlp_out = transposed_left(activation, grad_mlp)
    grad_act = transposed_right(grad_mlp, w_mlp_out)
    gelu_pull = jax.vjp(lambda values: jax.nn.gelu(values, approximate=True), pre_act)[1]
    grad_pre = narrow(gelu_pull(grad_act)[0])
    grad_w_mlp_in = transposed_left(flatten(mlp_in), grad_pre)
    grad_mlp_in = unflatten(transposed_right(grad_pre, w_mlp_in))
    grad_after = grad_res + norm_back(normed_mlp, scaling_mlp, grad_mlp_in * (1.0 + scale_mlp))
    grad_cross_out = flatten(narrow(grad_after))
    grad_w_cross_out = transposed_left(flatten(cross_low), grad_cross_out)
    grad_cross_attn = split_heads(unflatten(narrow(transposed_right(grad_cross_out, w_cross_out))))
    cross_delta = jnp.sum(grad_cross_attn.astype(jnp.float32) * cross_attended, axis=-1)
    cross_grad_probs = jnp.einsum(
        "cqhd,ckhd->cqhk", grad_cross_attn, cross_values, preferred_element_type=jnp.float32
    )
    cross_grad_scores = narrow(cross_probs * (cross_grad_probs - cross_delta[..., None]))
    grad_cross_query = narrow(
        jnp.einsum(
            "cqhk,ckhd->cqhd", cross_grad_scores, cross_keys, preferred_element_type=jnp.float32
        )
        * 0.125
    ).reshape(tokens, width)
    cross_key_part = (
        jnp.einsum(
            "cqhk,cqhd->ckhd", cross_grad_scores, cross_queries, preferred_element_type=jnp.float32
        )
        * 0.125
    )
    cross_value_part = jnp.einsum(
        "cqhk,cqhd->ckhd", cross_probs_low, grad_cross_attn, preferred_element_type=jnp.float32
    )
    cross_kv_part = jnp.concatenate(
        [
            cross_key_part.reshape(clips, text_count, width),
            cross_value_part.reshape(clips, text_count, width),
        ],
        axis=2,
    )
    text_total = lax.psum_scatter(cross_kv_part, "seq", scatter_dimension=1, tiled=True)
    text_share = text_total.shape[1]
    grad_cross_key = narrow(text_total[:, :, :width]).reshape(clips * text_share, width)
    grad_cross_value = narrow(text_total[:, :, width:]).reshape(clips * text_share, width)
    text_own = lax.dynamic_slice_in_dim(text, seq_place * text_share, text_share, 1).reshape(
        clips * text_share, width
    )
    grad_text = (
        transposed_right(grad_cross_key, w_cross_key)
        + transposed_right(grad_cross_value, w_cross_value)
    ).reshape(clips, text_share, width)
    grad_w_cross_key = transposed_left(text_own, grad_cross_key)
    grad_w_cross_value = transposed_left(text_own, grad_cross_value)
    grad_w_cross_query = transposed_left(flatten(cross_in), grad_cross_query)
    grad_cross_in = unflatten(transposed_right(grad_cross_query, w_cross_query))
    grad_gain_part = jnp.sum(grad_cross_in * normed_cross, axis=(0, 1))
    grad_mid = grad_after + norm_back(normed_cross, scaling_cross, grad_cross_in * gain_values)
    grad_attn_proj = flatten(narrow(gate_attn * grad_mid))
    grad_w_attn_out = transposed_left(flatten(attn_low), grad_attn_proj)
    grad_attn_flat = narrow(transposed_right(grad_attn_proj, w_attn_out))
    grad_heads = split_heads(unflatten(grad_attn_flat))
    row_delta = jnp.sum(grad_heads.astype(jnp.float32) * attended, axis=-1)
    zero_heads = jnp.zeros((clips, rows, H, HD), jnp.float32)
    gathered = lax.all_gather(kv_local, "seq", axis=1, tiled=True)
    query_grad = query_piece(
        zero_heads, gathered, 0, queries, grad_heads, log_total, row_delta, frame_lengths
    )
    anchor = jnp.int32(0)
    block_size = math.gcd(rows * lax.axis_size("seq"), key_block)

    def key_one_block(counter):
        rows_in = lax.dynamic_slice_in_dim(gathered, counter * block_size, block_size, 1)
        key_valid = block_valid(anchor, counter * block_size, block_size, frame_lengths)
        scores = masked_scores(queries, split_heads(rows_in[:, :, :width]), key_valid)
        attn_probs = jnp.exp(scores - log_total[..., None])
        grad_probs = jnp.einsum(
            "cqhd,ckhd->cqhk",
            grad_heads,
            split_heads(rows_in[:, :, width:]),
            preferred_element_type=jnp.float32,
        )
        grad_scores = narrow(attn_probs * (grad_probs - row_delta[..., None]))
        grad_keys = (
            jnp.einsum("cqhk,cqhd->ckhd", grad_scores, queries, preferred_element_type=jnp.float32)
            * 0.125
        )
        grad_values = jnp.einsum(
            "cqhk,cqhd->ckhd", narrow(attn_probs), grad_heads, preferred_element_type=jnp.float32
        )
        joined = jnp.concatenate(
            [
                grad_keys.reshape(clips, block_size, width),
                grad_values.reshape(clips, block_size, width),
            ],
            axis=2,
        )
        return jnp.transpose(joined, (1, 0, 2))

    blocks = lax.map(key_one_block, jnp.arange(rows * lax.axis_size("seq") // block_size))
    kv_term = lax.psum_scatter(
        blocks.reshape(rows * lax.axis_size("seq"), clips, 2 * width),
        "seq",
        scatter_dimension=0,
        tiled=True,
    )
    kv_grad = jnp.transpose(kv_term, (1, 0, 2))
    grad_query = narrow(query_grad.reshape(tokens, width))
    grad_key = flatten(narrow(kv_grad[:, :, :width]))
    grad_value = flatten(narrow(kv_grad[:, :, width:]))
    grad_w_query = transposed_left(attn_flat, grad_query)
    grad_w_key = transposed_left(attn_flat, grad_key)
    grad_w_value = transposed_left(attn_flat, grad_value)
    grad_attn_in = unflatten(
        transposed_right(grad_query, w_query)
        + transposed_right(grad_key, w_key)
        + transposed_right(grad_value, w_value)
    )
    grad_inputs = grad_mid + norm_back(normed_attn, scaling_attn, grad_attn_in * (1.0 + scale_attn))
    grad_frames = jnp.where(row_valid, grad_inputs, grad_out).astype(jnp.bfloat16)
    modulation_part = jnp.concatenate(
        [
            jnp.sum(grad_attn_in, axis=1),
            jnp.sum(grad_attn_in * normed_attn, axis=1),
            jnp.sum(grad_mid * attn_proj, axis=1),
            jnp.sum(grad_mlp_in, axis=1),
            jnp.sum(grad_mlp_in * normed_mlp, axis=1),
            jnp.sum(grad_res * mlp_out, axis=1),
        ],
        axis=1,
    )
    modulation_total = lax.psum(modulation_part, "seq")
    grad_modulation = narrow(modulation_total)
    grad_w_adaln = transposed_left(condition, grad_modulation)
    grad_condition = transposed_right(grad_modulation, w_adaln)
    grad_time_out = narrow(jax.vjp(jax.nn.silu, time_out)[1](grad_condition)[0])
    grad_w_time_out = transposed_left(time_hidden, grad_time_out)
    grad_time_hidden = transposed_right(grad_time_out, w_time_out)
    grad_time_first = jax.vjp(jax.nn.silu, time_first)[1](grad_time_hidden)[0]
    grad_w_time_in = lax.dot_general(
        time_vector.astype(jnp.float32),
        grad_time_first,
        (((0,), (0,)), ((), ())),
        precision=lax.Precision.HIGHEST,
    )
    shared = (
        lax.psum_scatter(grad_w_query, "seq", scatter_dimension=1, tiled=True),
        lax.psum_scatter(grad_w_key, "seq", scatter_dimension=1, tiled=True),
        lax.psum_scatter(grad_w_value, "seq", scatter_dimension=1, tiled=True),
        lax.psum_scatter(grad_w_attn_out, "seq", scatter_dimension=1, tiled=True),
        lax.psum_scatter(grad_gain_part, "seq", scatter_dimension=0, tiled=True),
        lax.psum_scatter(grad_w_cross_query, "seq", scatter_dimension=1, tiled=True),
        lax.psum_scatter(grad_w_cross_key, "seq", scatter_dimension=1, tiled=True),
        lax.psum_scatter(grad_w_cross_value, "seq", scatter_dimension=1, tiled=True),
        lax.psum_scatter(grad_w_cross_out, "seq", scatter_dimension=1, tiled=True),
        lax.psum_scatter(grad_w_mlp_in, "seq", scatter_dimension=1, tiled=True),
        lax.psum_scatter(grad_w_mlp_out, "seq", scatter_dimension=1, tiled=True),
    )
    replicated = (
        own_columns(grad_w_time_in, seq_place, seq_count),
        own_columns(grad_w_time_out, seq_place, seq_count),
        own_columns(grad_w_adaln, seq_place, seq_count),
    )
    summed = jax.tree.map(
        lambda part: part.astype(jnp.float32), lax.psum(for_sending(shared + replicated), "band")
    )
    (
        sum_query,
        sum_key,
        sum_value,
        sum_attn_out,
        sum_gain,
        sum_cross_query,
        sum_cross_key,
        sum_cross_value,
        sum_cross_out,
        sum_mlp_in,
        sum_mlp_out,
        sum_time_in,
        sum_time_out,
        sum_adaln,
    ) = summed
    return (
        block_out,
        grad_frames,
        grad_text,
        sum_time_in,
        sum_time_out,
        sum_adaln,
        sum_query,
        sum_key,
        sum_value,
        sum_attn_out,
        sum_gain,
        sum_cross_query,
        sum_cross_key,
        sum_cross_value,
        sum_cross_out,
        sum_mlp_in,
        sum_mlp_out,
    )


def solution(mesh):
    placed = (
        P("band", "seq", None),
        P("band", None, None),
        P("band"),
        P("band"),
        P("band", None),
        P("band", "seq", None),
        P(),
        P(),
        P(),
        P(),
        P(),
        P(),
        P(),
        P(),
        P(),
        P(),
        P(),
        P(),
        P(),
        P(),
    )
    paired = mesh.shape["band"] == 4 and mesh.shape["seq"] == 8
    return jax.shard_map(
        on_device if paired else on_device_general,
        mesh=mesh,
        in_specs=placed,
        out_specs=(
            P("band", "seq", None),
            P("band", "seq", None),
            P("band", "seq", None),
            P(None, "seq"),
            P(None, "seq"),
            P(None, "seq"),
            P(None, "seq"),
            P(None, "seq"),
            P(None, "seq"),
            P(None, "seq"),
            P("seq"),
            P(None, "seq"),
            P(None, "seq"),
            P(None, "seq"),
            P(None, "seq"),
            P(None, "seq"),
            P(None, "seq"),
        ),
        check_vma=False,
    )
```

```python
import math
import types

import jax
import jax.numpy as jnp
from jax import lax
from jax.experimental import pallas as pl
from jax.experimental.pallas import tpu as pltpu
from jax.sharding import PartitionSpec as P

H = 12
HD = 64


epsilon = 1e-06
masked_value = -1000000000.0
key_block = 512


def for_sending(value):
    return jax.tree.map(lambda a: a.astype(jnp.bfloat16) if a.dtype == jnp.float32 else a, value)


def narrow(values):
    return values.astype(jnp.bfloat16)


def product(left, right):
    return jnp.dot(left, right, preferred_element_type=jnp.float32)


def transposed_left(left, right):
    return lax.dot_general(
        left, right, (((0,), (0,)), ((), ())), preferred_element_type=jnp.float32
    )


def transposed_right(left, right):
    return lax.dot_general(
        left, right, (((1,), (1,)), ((), ())), preferred_element_type=jnp.float32
    )


def layer_norm(inputs):
    center = inputs - jnp.mean(inputs, axis=-1, keepdims=True)
    scaling = lax.rsqrt(jnp.mean(center * center, axis=-1, keepdims=True) + epsilon)
    return (center * scaling, scaling)


def norm_back(normed, scaling, gradient):
    mean_grad = jnp.mean(gradient, axis=-1, keepdims=True)
    mean_prod = jnp.mean(gradient * normed, axis=-1, keepdims=True)
    return scaling * (gradient - mean_grad - normed * mean_prod)


def time_embed(timesteps, width):
    half_width = width // 2
    frequency = jnp.exp(-math.log(10000.0) * jnp.arange(half_width, dtype=jnp.float32) / half_width)
    angles = timesteps.astype(jnp.float32)[:, None] * frequency[None, :]
    return jnp.concatenate([jnp.cos(angles), jnp.sin(angles)], axis=1)


def split_heads(rows_in):
    return rows_in.reshape(rows_in.shape[0], rows_in.shape[1], H, HD)


def masked_scores(queries, key_rows, key_valid):
    scores = (
        jnp.einsum("cqhd,ckhd->cqhk", queries, key_rows, preferred_element_type=jnp.float32) * 0.125
    )
    return jnp.where(key_valid[:, None, None, :], scores, masked_value)


def block_valid(anchor, start_row, block_size, lengths):
    return (anchor + start_row + jnp.arange(block_size))[None, :] < lengths[:, None]


def forward_piece(running, segment, anchor, queries, lengths):
    row_count = segment.shape[1]
    block_size = math.gcd(row_count, key_block)
    width = queries.shape[2] * queries.shape[3]

    def forward_one_block(running, counter):
        rows_in = lax.dynamic_slice_in_dim(segment, counter * block_size, block_size, 1)
        key_valid = block_valid(anchor, counter * block_size, block_size, lengths)
        scores = masked_scores(queries, split_heads(rows_in[:, :, :width]), key_valid)
        row_max, row_sum, weighted = running
        new_max = jnp.maximum(row_max, jnp.max(scores, axis=-1))
        factor = jnp.exp(row_max - new_max)
        expanded = jnp.exp(scores - new_max[..., None])
        row_sum = row_sum * factor + jnp.sum(expanded, axis=-1)
        weighted = weighted * factor[..., None] + jnp.einsum(
            "cqhk,ckhd->cqhd",
            narrow(expanded),
            split_heads(rows_in[:, :, width:]),
            preferred_element_type=jnp.float32,
        )
        return ((new_max, row_sum, weighted), None)

    running, unused = lax.scan(forward_one_block, running, jnp.arange(row_count // block_size))
    return running


def query_piece(gradient, segment, anchor, queries, grad_heads, log_total, row_delta, lengths):
    row_count = segment.shape[1]
    block_size = math.gcd(row_count, key_block)
    width = queries.shape[2] * queries.shape[3]

    def query_one_block(gradient, counter):
        rows_in = lax.dynamic_slice_in_dim(segment, counter * block_size, block_size, 1)
        key_valid = block_valid(anchor, counter * block_size, block_size, lengths)
        key_rows = split_heads(rows_in[:, :, :width])
        scores = masked_scores(queries, key_rows, key_valid)
        attn_probs = jnp.exp(scores - log_total[..., None])
        grad_probs = jnp.einsum(
            "cqhd,ckhd->cqhk",
            grad_heads,
            split_heads(rows_in[:, :, width:]),
            preferred_element_type=jnp.float32,
        )
        grad_scores = narrow(attn_probs * (grad_probs - row_delta[..., None]))
        gradient = (
            gradient
            + jnp.einsum(
                "cqhk,ckhd->cqhd", grad_scores, key_rows, preferred_element_type=jnp.float32
            )
            * 0.125
        )
        return (gradient, None)

    gradient, unused = lax.scan(query_one_block, gradient, jnp.arange(row_count // block_size))
    return gradient


def own_columns(values, place, count):
    share = values.shape[1] // count
    return lax.dynamic_slice_in_dim(values, place * share, share, 1)


MESH = pl.DeviceIdType.MESH
D = 768
PART = 48
VMEM_BYTES = 66500 * 1000


def places():
    band, seq = lax.axis_index("band"), lax.axis_index("seq")
    return lax.div(band, 2), lax.rem(band, 2), lax.div(seq, 2), lax.rem(seq, 2)


def device(y, core, z, x):
    return (y * 2 + core, z * 2 + x)


def remote(src, dst, send, recv, target):
    return pltpu.make_async_remote_copy(
        src_ref=src, dst_ref=dst, send_sem=send, recv_sem=recv, device_id=target, device_id_type=MESH
    )


def greet(partners):
    barrier = pltpu.get_barrier_semaphore()
    for partner in partners:
        pl.semaphore_signal(barrier, inc=1, device_id=partner, device_id_type=MESH)
    pl.semaphore_wait(barrier, len(partners))


class Spread:
    def __init__(self, chunks, recv, up, down, across):
        self.chunks, self.recv, self.up, self.down, self.across = chunks, recv, up, down, across
        self.y, self.core, self.z, self.x = places()

    def copies(self, chunk, slot, sems, at, target):
        first = sum(len(pieces) for pieces in self.chunks[:chunk])
        return [
            remote(
                piece(slot),
                piece(slot),
                sems.at[first + i, at],
                self.recv.at[first + i, slot],
                target,
            )
            for i, piece in enumerate(self.chunks[chunk])
        ]

    def to_up(self, chunk, k):
        slot = (self.z - k) * 2 + self.x
        target = device(self.y, self.core, self.z + 1, self.x)
        return self.copies(chunk, slot, self.up, k, target)

    def to_down(self, chunk, k):
        slot = (self.z + k) * 2 + self.x
        target = device(self.y, self.core, self.z - 1, self.x)
        return self.copies(chunk, slot, self.down, k, target)

    def to_across(self, chunk, row):
        target = device(self.y, self.core, self.z, 1 - self.x)
        return self.copies(chunk, row * 2 + self.x, self.across, row, target)

    def arrived(self, chunk, slot):
        target = device(self.y, self.core, self.z, 1 - self.x)
        for copy in self.copies(chunk, slot, self.across, 0, target):
            copy.wait_recv()

    def all_arrived(self, slot):
        for chunk in range(len(self.chunks)):
            self.arrived(chunk, slot)

    def start(self):
        z = self.z
        for chunk in range(len(self.chunks)):

            @pl.when(z < 3)
            def _():
                for copy in self.to_up(chunk, 0):
                    copy.start()

            @pl.when(z > 0)
            def _():
                for copy in self.to_down(chunk, 0):
                    copy.start()

            for copy in self.to_across(chunk, z):
                copy.start()

    def relay(self, k, chunk):
        z = self.z

        @pl.when(z >= k)
        def _():
            self.arrived(chunk, (z - k) * 2 + self.x)

            @pl.when(z < 3)
            def _():
                for copy in self.to_up(chunk, k):
                    copy.start()

            for copy in self.to_across(chunk, z - k):
                copy.start()

        @pl.when(z + k <= 3)
        def _():
            self.arrived(chunk, (z + k) * 2 + self.x)

            @pl.when(z > 0)
            def _():
                for copy in self.to_down(chunk, k):
                    copy.start()

            for copy in self.to_across(chunk, z + k):
                copy.start()

    def finish(self):
        z = self.z
        for chunk in range(len(self.chunks)):
            for k in range(4):

                @pl.when((z >= k) & (z < 3))
                def _():
                    for copy in self.to_up(chunk, k):
                        copy.wait_send()

                @pl.when((z + k <= 3) & (z > 0))
                def _():
                    for copy in self.to_down(chunk, k):
                        copy.wait_send()

                for copy in self.to_across(chunk, k):
                    copy.wait_send()


def silu(values):
    return values / (1.0 + jnp.exp(-values))


def head_mask(half):
    lane = lax.broadcasted_iota(jnp.int32, (1, 128), 1)
    return (lane < 64) if half == 0 else (lane >= 64)


def keep_head(tile, half):
    return jnp.where(head_mask(half), tile, jnp.zeros_like(tile))


def vmem(*shape, dtype=jnp.bfloat16):
    return pltpu.VMEM(shape, dtype)

PRODUCTS = (
    [(1, 4), (0, 0), (2, 4), (0, 1), (0, 2), (3, 4), (0, 3), (4, 4)]
    + [(5, 5), (6, 6), (9, 8), (9, 9), (7, 7)]
    + [(8, 10), (8, 11), (8, 12)]
)
LEFTS = 8
RIGHTS = 13
TEXT_UNIT = 9
SLOTS = 4
LATER = (0, 1, 3, 7, 10, 12)
IN_VMEM = [
    "mask",
    "frames",
    "cotangent",
    "text",
    "gain",
    "vector",
]
IN_PLACE = [
    "hbm_out",
    "hbm_cross_query",
    "hbm_cross_key",
    "hbm_cross_value",
    "hbm_cross_out",
    "hbm_mlp_in",
    "hbm_mlp_out",
    "hbm_query",
    "hbm_key",
    "hbm_value",
    "hbm_adaln",
    "hbm_time_out",
    "hbm_time_in",
]
OUT_VMEM = [
    "block_out",
    "grad_frames",
    "grad_text",
    "gain_sum",
    "conditions",
    "hiddens",
    "vectors",
    "grad_mods",
    "grad_time_outs",
    "grad_time_firsts",
]
OUT_PLACE = ["pieces"]


def block_scratch():
    n = len(PRODUCTS)
    sem = lambda *shape: pltpu.SemaphoreType.DMA(shape)
    f32 = jnp.float32
    return dict(
        mod=vmem(8, 6 * D, dtype=f32),
        time=vmem(8, 2 * D, dtype=f32),
        qkv=vmem(3, 8, 128, D),
        attended=vmem(128, D, dtype=f32),
        pair=vmem(2, 128, D),
        stats=vmem(128, 128, dtype=f32),
        gathered=vmem(8, 128, D),
        time_in=vmem(256, D),
        fr_recv=sem(2, 8),
        fr_up=sem(2, 4),
        fr_down=sem(2, 4),
        fr_across=sem(2, 4),
        square=vmem(9, D, D),
        mlp_in=vmem(D, 4 * D),
        mlp_out=vmem(4 * D, D),
        adaln_high=vmem(D, 2 * D),
        load_sems=sem(16),
        lefts=vmem(LEFTS, 128, D),
        gt=vmem(RIGHTS, 2, 2, 192, 128),
        grecv=vmem(RIGHTS, 2, 192, 128),
        lrecv=vmem(LEFTS, 128, D),
        pbuf=vmem(SLOTS, 2, 192, D),
        precv=vmem(n, 192, D),
        qbuf=vmem(SLOTS, 2, 192, 384),
        qrecv=vmem(n, 192, 384),
        rbuf=vmem(SLOTS, 4, PART, 384),
        rrecv=vmem(n, 4, PART, 384),
        final=vmem(n, 2, 2, PART, 384),
        ls=sem(LEFTS),
        lr=sem(LEFTS),
        gs=sem(RIGHTS),
        gr=sem(RIGHTS),
        ps=sem(n),
        pr=sem(n),
        qs=sem(n),
        qr=sem(n),
        rs=sem(n, 4),
        rr=sem(n, 4),
        fs=sem(n, 2),
        fr=sem(n, 2),
        out_sems=sem(n),
        heads=vmem(8, 128, D),
        rowstats=vmem(8, 32, 128, dtype=f32),
        sp_recv=sem(3, 8),
        sp_up=sem(3, 4),
        sp_down=sem(3, 4),
        sp_across=sem(3, 4),
        times=vmem(4, 8, 2 * D, dtype=f32),
        vecs=vmem(4, 16, 256),
        ts=sem(2, 4),
        tr=sem(2, 4),
        text_part=vmem(8, 16, D, dtype=f32),
        text_send=vmem(8, 16, D),
        text_recv=vmem(8, 16, D),
        xs=sem(8),
        xr=sem(8),
        sums=vmem(8, D, dtype=f32),
        sums_recv=vmem(8, 8, D, dtype=f32),
        ss=sem(8),
        sr=sem(8),
        clip_sums=vmem(4, 8, D, dtype=f32),
        cs=sem(4),
        cr=sem(4),
        proj=vmem(128, D, dtype=f32),
        middle=vmem(128, D, dtype=f32),
        normed_cross=vmem(128, D, dtype=f32),
        normed_mlp=vmem(128, D, dtype=f32),
        after=vmem(128, D, dtype=f32),
        pre=vmem(4, 128, D, dtype=f32),
        acc=vmem(128, D, dtype=f32),
        grad_mlp=vmem(128, D),
        cross_probs=vmem(12, 128, 128, dtype=f32),
        grad_q=vmem(128, D),
        grad_k=vmem(128, D),
        grad_v=vmem(128, D),
    )


def gelu(v):
    inner = jnp.tanh(0.7978845608028654 * (v + 0.044715 * v * v * v))
    return 0.5 * v * (1.0 + inner)


def gelu_slope(v):
    inner = jnp.tanh(0.7978845608028654 * (v + 0.044715 * v * v * v))
    return 0.5 * (1.0 + inner) + 0.5 * v * (1.0 - inner * inner) * 0.7978845608028654 * (
        1.0 + 3 * 0.044715 * v * v
    )


def silu_slope(v):
    gate = 1.0 / (1.0 + jnp.exp(-v))
    return gate * (1.0 + v * (1.0 - gate))


class Sums:
    def __init__(self, r):
        self.r = r
        self.y, self.core, self.z, self.x = y, core, z, x = places()
        self.across = device(y, core, z, 1 - x)
        self.high, self.low = lax.div(z, 2), lax.rem(z, 2)
        self.along = device(y, core, 2 * self.high + 1 - self.low, x)
        self.clips = [
            None,
            device(y, 1 - core, z, x),
            device(1 - y, core, z, x),
            device(1 - y, 1 - core, z, x),
        ]
        self.done = 0

    def left_copy(self, u):
        r = self.r
        to = self.along if 1 <= u <= 4 else self.across
        return remote(r.lefts.at[u], r.lrecv.at[u], r.ls.at[u], r.lr.at[u], to)

    def right_copy(self, u):
        r = self.r
        if u == 4:
            half, to = 1 - self.low, self.along
        else:
            half, to = 1 - self.x, self.across
        return remote(r.gt.at[u, half], r.grecv.at[u], r.gs.at[u], r.gr.at[u], to)

    def core_copy(self, i):
        r = self.r
        mine = r.pbuf.at[i % SLOTS, 1 - self.core]
        return remote(mine, r.precv.at[i], r.ps.at[i], r.pr.at[i], self.clips[1])

    def y_copy(self, i):
        r = self.r
        mine = r.qbuf.at[i % SLOTS, 1 - self.y]
        return remote(mine, r.qrecv.at[i], r.qs.at[i], r.qr.at[i], self.clips[2])

    def spot(self, i):
        return self.high * 2 + self.x if 1 <= PRODUCTS[i][0] <= 4 else self.z

    def z_copy(self, i, k):
        r = self.r
        to = lax.rem(self.spot(i) + k, 4)
        if 1 <= PRODUCTS[i][0] <= 4:
            target = device(self.y, self.core, 2 * lax.div(to, 2) + self.low, lax.rem(to, 2))
        else:
            target = device(self.y, self.core, to, self.x)
        return remote(
            r.rbuf.at[i % SLOTS, to], r.rrecv.at[i, k], r.rs.at[i, k], r.rr.at[i, k], target
        )

    def last_y_copy(self, i):
        r = self.r
        piece = r.final.at[i, self.core, self.y]
        return remote(piece, piece, r.fs.at[i, 0], r.fr.at[i, 0], self.clips[2])

    def last_core_copy(self, i):
        r = self.r
        piece = r.final.at[i, self.core]
        return remote(piece, piece, r.fs.at[i, 1], r.fr.at[i, 1], self.clips[1])

    def out_copy(self, i):
        r = self.r
        return pltpu.make_async_copy(r.final.at[i], r.pieces.at[i], r.out_sems.at[i])

    def post_left(self, u, values):
        self.r.lefts[u] = values
        self.left_copy(u).start()

    def post_right(self, u, values):
        turned = narrow(jnp.transpose(values.astype(jnp.float32)))
        for s in range(8):
            for c in range(2):
                at = s * 96 + c * PART
                half, block = (s // 2 % 2, s // 4 * 2 + s % 2) if u == 4 else (s % 2, s // 2)
                self.r.gt[u, half, c, pl.ds(block * PART, PART), :] = turned[at : at + PART]
        self.right_copy(u).start()

    def multiply(self, i):
        r = self.r
        left, right = PRODUCTS[i]
        if left < LEFTS and left not in [l for l, unused in PRODUCTS[:i]]:
            self.left_copy(left).wait_recv()
        if right not in [r for unused, r in PRODUCTS[:i]]:
            self.right_copy(right).wait_recv()
        if i >= SLOTS:
            self.core_copy(i - SLOTS).wait_send()
        for c in range(2):
            mine, theirs = r.gt[right, self.low if right == 4 else self.x, c], r.grecv[right, c]
            if left == TEXT_UNIT:
                both = narrow(mine.astype(jnp.float32) + theirs.astype(jnp.float32))
                part = product(both, r.text[...])
            else:
                both = (r.pair[0], r.pair[1]) if left == 8 else (r.lefts[left], r.lrecv[left])
                part = product(
                    jnp.concatenate([mine, theirs], axis=1), jnp.concatenate(both, axis=0)
                )
            r.pbuf[i % SLOTS, c] = narrow(part)
        self.core_copy(i).start()

    def add_core(self, i):
        r = self.r
        self.core_copy(i).wait_recv()
        if i >= SLOTS:
            self.y_copy(i - SLOTS).wait_send()
        total = narrow(
            r.pbuf[i % SLOTS, self.core].astype(jnp.float32) + r.precv[i].astype(jnp.float32)
        )
        r.qbuf[i % SLOTS, 0] = total[:, :384]
        r.qbuf[i % SLOTS, 1] = total[:, 384:]
        self.y_copy(i).start()

    def add_y(self, i):
        r = self.r
        self.y_copy(i).wait_recv()
        if i >= SLOTS:
            for k in (1, 2, 3):
                self.z_copy(i - SLOTS, k).wait_send()
        total = narrow(
            r.qbuf[i % SLOTS, self.y].astype(jnp.float32) + r.qrecv[i].astype(jnp.float32)
        )
        for k in range(4):
            r.rbuf[i % SLOTS, k] = total[k * PART : (k + 1) * PART]
        for k in (1, 2, 3):
            self.z_copy(i, k).start()

    def add_z(self, i):
        r = self.r
        for k in (1, 2, 3):
            self.z_copy(i, k).wait_recv()
        total = r.rbuf[i % SLOTS, self.spot(i)].astype(jnp.float32)
        for k in (1, 2, 3):
            total = total + r.rrecv[i, k].astype(jnp.float32)
        r.final[i, self.core, self.y] = narrow(total)
        self.last_y_copy(i).start()

    def pass_on(self, i):
        self.last_y_copy(i).wait_recv()
        self.last_core_copy(i).start()

    def output(self, i):
        self.last_core_copy(i).wait_recv()
        self.out_copy(i).start()

    def step(self, times=1):
        n = len(PRODUCTS)
        stages = (
            self.multiply,
            self.add_core,
            self.add_y,
            self.add_z,
            self.pass_on,
            self.output,
        )
        for unused in range(times):
            for later, stage in reversed(list(zip(LATER, stages))):
                if 0 <= self.done - later < n:
                    stage(self.done - later)
            self.done += 1

    def finish(self):
        n = len(PRODUCTS)
        while self.done < n + LATER[-1]:
            self.step()
        for u in range(LEFTS):
            self.left_copy(u).wait_send()
        for u in range(RIGHTS):
            self.right_copy(u).wait_send()
        for i in range(n):
            if i >= n - SLOTS:
                self.core_copy(i).wait_send()
                self.y_copy(i).wait_send()
                for k in (1, 2, 3):
                    self.z_copy(i, k).wait_send()
            self.last_y_copy(i).wait_send()
            self.last_core_copy(i).wait_send()
            self.out_copy(i).wait()


def block_kernel(length_ref, *refs):
    names = IN_VMEM + IN_PLACE + OUT_VMEM + OUT_PLACE + list(block_scratch())
    r = types.SimpleNamespace(**dict(zip(names, refs, strict=True)))
    y, core, z, x = places()
    me, band = z * 2 + x, y * 2 + core
    peers = [device(y, core, lax.div(s, 2), lax.rem(s, 2)) for s in [lax.rem(me + k, 8) for k in range(8)]]
    r.cross_q, r.cross_k, r.cross_v, r.grad_heads = [r.gathered.at[i] for i in range(4, 8)]
    sums = Sums(r)

    def load(i, src, dst):
        return pltpu.make_async_copy(src, dst, r.load_sems.at[i])

    squares = (
        r.hbm_out,
        r.hbm_cross_query,
        r.hbm_cross_key,
        r.hbm_cross_value,
        r.hbm_cross_out,
        r.hbm_query,
        r.hbm_key,
        r.hbm_value,
        r.hbm_time_out,
    )
    OUT, CQ, CK, CV, CO, WQ, WK, WV, TIME = range(9)
    loads = [load(i, ref, r.square.at[i]) for i, ref in enumerate(squares)]
    loads.append(load(9, r.hbm_mlp_in, r.mlp_in))
    loads.append(load(10, r.hbm_mlp_out, r.mlp_out))
    loads.append(load(11, r.hbm_adaln.at[:, pl.ds(3072, 1536)], r.adaln_high))
    adaln_low = load(12, r.hbm_adaln.at[:, pl.ds(0, 3072)], r.mlp_in)
    load_time_in = load(13, r.hbm_time_in, r.time_in)
    own_frames = load(14, r.frames, r.gathered.at[me])
    own_frames.start()
    load_time_in.start()
    loads[TIME].start()
    adaln_low.start()
    for i in (11, WQ, WK, WV, OUT, CK, CV, CQ, CO, 10):
        loads[i].start()
    greet(peers[1:] + sums.clips[1:])
    own_frames.wait()

    def half(ref, i):
        return lambda slot: ref.at[slot, i * 64 : (i + 1) * 64]

    chunks = [[half(r.gathered, i)] for i in range(2)]
    neighbours = Spread(chunks, r.fr_recv, r.fr_up, r.fr_down, r.fr_across)
    neighbours.start()

    def clip_copy(refs, sems, recvs, j):
        return [
            remote(ref.at[band], ref.at[band], sems.at[i, j], recvs.at[i, j], sums.clips[j])
            for i, ref in enumerate(refs)
        ]

    length = length_ref[0]

    def row_valid():
        return lax.broadcasted_iota(jnp.int32, (128, 1), 0) + me * 128 < length

    def modulation(i):
        return r.mod[0:1, i * D : (i + 1) * D]

    def over_rows(values):
        return jnp.sum(values, axis=0, keepdims=True)

    lane = lax.broadcasted_iota(jnp.int32, (1, 128), 1)
    text_valid = r.mask[...] != 0
    gain = r.gain[...].astype(jnp.float32)

    def tile_at(tile):
        return pl.ds(pl.multiple_of(tile * 128, 128), 128)

    load_time_in.wait()
    first = product(r.vector[...], r.time_in[...])
    hidden = narrow(silu(first))
    loads[TIME].wait()
    second = product(hidden, r.square[TIME])
    condition = narrow(silu(second))
    r.time[:, 0:D] = first[0:8]
    r.time[:, D : 2 * D] = second[0:8]
    r.times[band] = r.time[...]
    r.vecs[band] = r.vector[...]
    for j in (1, 2, 3):
        for copy in clip_copy((r.times, r.vecs), r.ts, r.tr, j):
            copy.start()

    adaln_low.wait()
    r.mod[:, 0:1536] = product(condition, r.mlp_in[:, 0:1536])[0:8]
    neighbours.relay(1, 0)
    r.mod[:, 1536:3072] = product(condition, r.mlp_in[:, 1536:3072])[0:8]
    loads[9].start()
    neighbours.relay(1, 1)
    loads[11].wait()
    r.mod[:, 3072:4608] = product(condition, r.adaln_high[...])[0:8]
    for i in (WQ, WK, WV):
        loads[i].wait()
    def project(row, column):
        normed, unused = layer_norm(r.gathered[row * 2 + column].astype(jnp.float32))
        low = narrow(normed * (1.0 + modulation(1)) + modulation(0))
        for i in range(3):
            r.qkv[i, row * 2 + column] = narrow(product(low, r.square[WQ + i]))
        return low

    def own_column(row, unused):
        low = project(row, x)

        @pl.when(row == z)
        def _():
            r.pair[0] = low

        return unused

    def other_column(row, unused):
        neighbours.all_arrived(row * 2 + 1 - x)
        low = project(row, 1 - x)

        @pl.when(row == z)
        def _():
            r.pair[1] = low

        return unused

    for k in (2, 3):
        for chunk in range(2):
            neighbours.relay(k, chunk)
    lax.fori_loop(0, 4, own_column, 0)
    lax.fori_loop(0, 4, other_column, 0)
    key_valid = lax.broadcasted_iota(jnp.int32, (1, 1024), 1) < length

    def attend_pair(tile, stats):
        at = tile_at(tile)
        query = r.qkv[0, me, :, at]
        keys = r.qkv[1, :, :, at].reshape(1024, 128)
        values = r.qkv[2, :, :, at].reshape(1024, 128)
        outs = []
        for half in range(2):
            scores = transposed_right(keep_head(query, half), keys) * 0.125
            scores = jnp.where(key_valid, scores, masked_value)
            row_max = jnp.max(scores, axis=1, keepdims=True)
            expanded = jnp.exp(scores - row_max)
            row_sum = jnp.sum(expanded, axis=1, keepdims=True)
            outs.append(product(narrow(expanded), values) / row_sum)
            stats = jnp.where(lane == tile * 2 + half, row_max + jnp.log(row_sum), stats)
        r.attended[:, at] = jnp.where(head_mask(0), outs[0], outs[1])
        return stats

    r.stats[...] = lax.fori_loop(0, 6, attend_pair, jnp.zeros((128, 128), jnp.float32))
    neighbours.finish()
    sums.post_left(7, narrow(r.attended[...]))
    r.grad_mlp[...] = narrow(
        modulation(5) * jnp.where(row_valid(), r.cotangent[...].astype(jnp.float32), 0.0)
    )
    sums.post_right(4, r.grad_mlp[...])
    loads[OUT].wait()
    r.proj[...] = product(r.lefts[7], r.square[OUT])
    r.middle[...] = r.frames[...].astype(jnp.float32) + modulation(2) * r.proj[...]
    normed, scaling_cross = layer_norm(r.middle[...])
    r.normed_cross[...] = normed
    sums.post_left(6, narrow(normed * gain))
    loads[CK].wait()
    r.cross_k[...] = narrow(product(r.text[...], r.square[CK]))
    loads[CV].wait()
    r.cross_v[...] = narrow(product(r.text[...], r.square[CV]))
    loads[CQ].wait()
    r.cross_q[...] = narrow(product(r.lefts[6], r.square[CQ]))

    def cross_pair(tile, unused):
        at = tile_at(tile)
        query, keys, values = r.cross_q[:, at], r.cross_k[:, at], r.cross_v[:, at]
        outs = []
        for half in range(2):
            scores = transposed_right(keep_head(query, half), keys) * 0.125
            scores = jnp.where(text_valid, scores, masked_value)
            row_max = jnp.max(scores, axis=1, keepdims=True)
            total = row_max + jnp.log(jnp.sum(jnp.exp(scores - row_max), axis=1, keepdims=True))
            probs = jnp.exp(scores - total)
            r.cross_probs[tile * 2 + half] = probs
            outs.append(product(narrow(probs), values))
        r.lefts[5, :, at] = narrow(jnp.where(head_mask(0), outs[0], outs[1]))
        return unused

    lax.fori_loop(0, 6, cross_pair, 0)
    sums.left_copy(5).start()
    loads[CO].wait()
    r.after[...] = r.middle[...] + product(r.lefts[5], r.square[CO])
    normed, scaling_mlp = layer_norm(r.after[...])
    r.normed_mlp[...] = normed
    sums.post_left(0, narrow(normed * (1.0 + modulation(4)) + modulation(3)))
    loads[9].wait()
    loads[10].wait()
    for j in range(4):
        pre = product(r.lefts[0], r.mlp_in[:, j * D : (j + 1) * D])
        r.pre[j] = pre
        sums.post_left(1 + j, narrow(gelu(pre)))
        part = product(r.lefts[1 + j], r.mlp_out[j * D : (j + 1) * D, :])
        r.acc[...] = part if j == 0 else r.acc[...] + part
    frames = r.frames[...].astype(jnp.float32)
    r.block_out[...] = narrow(
        jnp.where(row_valid(), r.after[...] + modulation(5) * r.acc[...], frames)
    )
    grad_res = jnp.where(row_valid(), r.cotangent[...].astype(jnp.float32), 0.0)
    r.sums[5:6, :] = over_rows(grad_res * r.acc[...])
    for j in range(4):
        slope = gelu_slope(r.pre[j])
        grad = narrow(slope * transposed_right(r.grad_mlp[...], r.mlp_out[j * D : (j + 1) * D, :]))
        r.gathered[j] = grad
        for part in range(2):
            s = j * 2 + part
            turned = narrow(
                jnp.transpose(grad[:, part * 384 : (part + 1) * 384].astype(jnp.float32))
            )
            for u in range(4):
                for c in range(2):
                    at = u * 96 + c * PART
                    r.gt[u, s % 2, c, pl.ds((s // 2) * PART, PART), :] = turned[at : at + PART]
    for u in range(4):
        sums.right_copy(u).start()
    for j in range(4):
        part = transposed_right(r.gathered[j], r.mlp_in[:, j * D : (j + 1) * D])
        r.acc[...] = part if j == 0 else r.acc[...] + part
    adaln_low.start()
    sums.step(1)
    r.sums[3:4, :] = over_rows(r.acc[...])
    r.sums[4:5, :] = over_rows(r.acc[...] * r.normed_mlp[...])
    grad_res = jnp.where(row_valid(), r.cotangent[...].astype(jnp.float32), 0.0)
    r.after[...] = grad_res + norm_back(
        r.normed_mlp[...], scaling_mlp, r.acc[...] * (1.0 + modulation(4))
    )
    low = narrow(r.after[...])
    sums.post_right(5, low)
    r.grad_heads[...] = narrow(transposed_right(low, r.square[CO]))

    def cross_pair_back(tile, unused):
        at = tile_at(tile)
        query, keys, values = r.cross_q[:, at], r.cross_k[:, at], r.cross_v[:, at]
        grad = r.grad_heads[:, at]
        outs = []
        for half in range(2):
            probs = r.cross_probs[tile * 2 + half]
            grad_probs = transposed_right(keep_head(grad, half), values)
            inner = jnp.sum(probs * grad_probs, axis=1, keepdims=True)
            scores = narrow(probs * (grad_probs - inner)).astype(jnp.float32)
            outs.append(
                (
                    product(narrow(scores), keys),
                    product(narrow(jnp.transpose(scores)), query),
                    product(narrow(jnp.transpose(probs)), grad),
                )
            )
        grad_q, grad_k, grad_v = [jnp.where(head_mask(0), a, b) for a, b in zip(*outs)]
        r.grad_q[:, at] = narrow(grad_q * 0.125)
        r.grad_k[:, at] = narrow(grad_k * 0.125)
        r.grad_v[:, at] = narrow(grad_v)
        return unused

    lax.fori_loop(0, 6, cross_pair_back, 0)
    sums.post_right(6, r.grad_q[...])
    sums.step(1)
    grad_cross_in = transposed_right(r.grad_q[...], r.square[CQ])
    r.sums[6:7, :] = over_rows(grad_cross_in * r.normed_cross[...])
    r.sums[7:8, :] = jnp.zeros((1, D), jnp.float32)
    r.middle[...] = r.after[...] + norm_back(
        r.normed_cross[...], scaling_cross, grad_cross_in * gain
    )
    low = narrow(modulation(2) * r.middle[...])
    grad_heads = narrow(transposed_right(low, r.square[OUT]))
    r.heads[me] = grad_heads
    products = grad_heads.astype(jnp.float32) * r.attended[...]
    delta = jnp.zeros((128, 128), jnp.float32)
    for h in range(12):
        tile = products[:, (h // 2) * 128 : (h // 2 + 1) * 128]
        inner = jnp.sum(jnp.where(head_mask(h % 2), tile, 0.0), axis=1, keepdims=True)
        delta = jnp.where(lane == h, inner, delta)
    r.rowstats[me] = jnp.concatenate(
        [jnp.transpose(r.stats[...])[:16], jnp.transpose(delta)[:16]], axis=0
    )
    chunks = [[half(r.heads, 0), lambda slot: r.rowstats.at[slot]], [half(r.heads, 1)]]
    spread = Spread(chunks, r.sp_recv, r.sp_up, r.sp_down, r.sp_across)
    spread.start()
    sums.post_right(7, low)
    r.sums[2:3, :] = over_rows(r.middle[...] * r.proj[...])
    sums.post_right(8, r.grad_k[...])
    sums.post_right(9, r.grad_v[...])
    text_grad = transposed_right(r.grad_k[...], r.square[CK]) + transposed_right(
        r.grad_v[...], r.square[CV]
    )
    for s in range(8):
        r.text_part[s] = text_grad[s * 16 : (s + 1) * 16]
        r.text_send[s] = narrow(text_grad[s * 16 : (s + 1) * 16])

    def text_copy(k):
        return remote(
            r.text_send.at[lax.rem(me + k, 8)], r.text_recv.at[k], r.xs.at[k], r.xr.at[k], peers[k]
        )

    for k in range(1, 8):
        text_copy(k).start()
    sums.step(2)
    spread.relay(1, 0)
    key_valid = lax.broadcasted_iota(jnp.int32, (1, 1024), 1) < length

    def query_pair(tile, unused):
        at = tile_at(tile)
        query, grad = r.qkv[0, me, :, at], r.heads[me, :, at]
        keys = r.qkv[1, :, :, at].reshape(1024, 128)
        values = r.qkv[2, :, :, at].reshape(1024, 128)
        tile_product = grad.astype(jnp.float32) * r.attended[:, at]
        outs = []
        for half in range(2):
            scores = transposed_right(keep_head(query, half), keys) * 0.125
            scores = jnp.where(key_valid, scores, masked_value)
            total = jnp.sum(
                jnp.where(lane == tile * 2 + half, r.stats[...], 0.0), axis=1, keepdims=True
            )
            inner = jnp.sum(jnp.where(head_mask(half), tile_product, 0.0), axis=1, keepdims=True)
            grad_probs = transposed_right(keep_head(grad, half), values)
            outs.append(product(narrow(jnp.exp(scores - total) * (grad_probs - inner)), keys))
        r.grad_q[:, at] = narrow(jnp.where(head_mask(0), outs[0], outs[1]) * 0.125)
        return unused

    lax.fori_loop(0, 1, query_pair, 0)
    spread.relay(1, 1)
    lax.fori_loop(1, 3, query_pair, 0)
    sums.step(2)
    spread.relay(2, 0)
    lax.fori_loop(3, 4, query_pair, 0)
    spread.relay(2, 1)
    lax.fori_loop(4, 6, query_pair, 0)
    sums.step(3)
    spread.relay(3, 0)
    spread.relay(3, 1)
    sums.post_right(10, r.grad_q[...])
    sums.step(4)
    for row in range(4):
        spread.all_arrived(row * 2 + 1 - x)

    def key_pair(tile, unused):
        at = tile_at(tile)
        key, value = r.qkv[1, me, :, at], r.qkv[2, me, :, at]
        queries = r.qkv[0, :, :, at].reshape(1024, 128)
        grads = r.heads[:, :, at].reshape(1024, 128)
        outs = []
        for half in range(2):
            h = tile * 2 + half
            total = jnp.concatenate([r.rowstats[s, pl.ds(h, 1), :] for s in range(8)], axis=1)
            inner = jnp.concatenate([r.rowstats[s, pl.ds(16 + h, 1), :] for s in range(8)], axis=1)
            scores = transposed_right(keep_head(key, half), queries) * 0.125
            scores = jnp.where(row_valid(), scores, masked_value)
            probs = jnp.exp(scores - total)
            grad_probs = transposed_right(keep_head(value, half), grads)
            grad_scores = narrow(probs * (grad_probs - inner))
            outs.append((product(grad_scores, queries), product(narrow(probs), grads)))
        grad_k, grad_v = [jnp.where(head_mask(0), a, b) for a, b in zip(*outs)]
        r.grad_k[:, at] = narrow(grad_k * 0.125)
        r.grad_v[:, at] = narrow(grad_v)
        return unused

    lax.fori_loop(0, 6, key_pair, 0)
    sums.post_right(11, r.grad_k[...])
    sums.post_right(12, r.grad_v[...])
    sums.step(1)
    grad_in = (
        transposed_right(r.grad_q[...], r.square[WQ])
        + transposed_right(r.grad_k[...], r.square[WK])
        + transposed_right(r.grad_v[...], r.square[WV])
    )
    r.acc[...] = grad_in
    normed, scaling = layer_norm(r.frames[...].astype(jnp.float32))
    r.sums[0:1, :] = over_rows(r.acc[...])
    r.sums[1:2, :] = over_rows(r.acc[...] * normed)

    def sums_copy(k):
        return remote(r.sums, r.sums_recv.at[k], r.ss.at[k], r.sr.at[k], peers[k])

    for k in range(1, 8):
        sums_copy(k).start()
    sums.step(3)
    grads = r.middle[...] + norm_back(normed, scaling, r.acc[...] * (1.0 + modulation(1)))
    r.grad_frames[...] = narrow(
        jnp.where(row_valid(), grads, r.cotangent[...].astype(jnp.float32))
    )
    total = r.sums[...]
    for k in range(1, 8):
        sums_copy(k).wait_recv()
        total = total + r.sums_recv[k]
    r.clip_sums[band] = total

    def total_copy(j):
        return remote(
            r.clip_sums.at[band], r.clip_sums.at[band], r.cs.at[j], r.cr.at[j], sums.clips[j]
        )

    for j in (1, 2, 3):
        total_copy(j).start()
    sums.step(2)
    for j in (1, 2, 3):
        total_copy(j).wait_recv()
        for copy in clip_copy((r.times, r.vecs), r.ts, r.tr, j):
            copy.wait_recv()
    r.gain_sum[0:1, :] = (r.clip_sums[0, 6:7] + r.clip_sums[1, 6:7]) + (
        r.clip_sums[2, 6:7] + r.clip_sums[3, 6:7]
    )
    r.gain_sum[1:8, :] = jnp.zeros((7, D), jnp.float32)

    def by_clip(pieces):
        return jnp.concatenate(pieces + [jnp.zeros((12, pieces[0].shape[1]), jnp.float32)], axis=0)

    for i in range(6):
        r.grad_mods[:, i * D : (i + 1) * D] = narrow(
            by_clip([r.clip_sums[b, i : i + 1] for b in range(4)])
        )
    firsts = by_clip([r.times[b, 0:1, 0:D] for b in range(4)])
    seconds = by_clip([r.times[b, 0:1, D : 2 * D] for b in range(4)])
    r.hiddens[...] = narrow(silu(firsts))
    r.conditions[...] = narrow(silu(seconds))
    for b in range(4):
        r.vectors[b] = r.vecs[b]
    adaln_low.wait()
    grad_condition = transposed_right(r.grad_mods[:, :3072], r.mlp_in[...]) + transposed_right(
        r.grad_mods[:, 3072:], r.adaln_high[...]
    )
    low = narrow(silu_slope(seconds) * grad_condition)
    r.grad_time_outs[...] = low
    r.grad_time_firsts[...] = silu_slope(firsts) * transposed_right(low, r.square[TIME])
    total = r.text_part[me]
    for k in range(1, 8):
        text_copy(k).wait_recv()
        total = total + r.text_recv[k].astype(jnp.float32)
    r.grad_text[...] = total
    sums.finish()
    spread.finish()
    for k in range(1, 8):
        text_copy(k).wait_send()
        sums_copy(k).wait_send()
    for j in (1, 2, 3):
        total_copy(j).wait_send()
        for copy in clip_copy((r.times, r.vecs), r.ts, r.tr, j):
            copy.wait_send()


def block(length, vmem_args, place_args):
    in_vmem = pl.BlockSpec(memory_space=pltpu.VMEM)
    in_place = pl.BlockSpec(memory_space=pl.ANY)
    shape = jax.ShapeDtypeStruct
    f32, bf16 = jnp.float32, jnp.bfloat16
    return pl.pallas_call(
        block_kernel,
        out_shape=(
            shape((128, D), bf16),
            shape((128, D), bf16),
            shape((16, D), f32),
            shape((8, D), f32),
            shape((16, D), bf16),
            shape((16, D), bf16),
            shape((4, 16, 256), bf16),
            shape((16, 6 * D), bf16),
            shape((16, D), bf16),
            shape((16, D), f32),
            shape((len(PRODUCTS), 2, 2, PART, 384), bf16),
        ),
        in_specs=[pl.BlockSpec(memory_space=pltpu.SMEM)]
        + [in_vmem] * len(IN_VMEM)
        + [in_place] * len(IN_PLACE),
        out_specs=(in_vmem,) * len(OUT_VMEM) + (in_place,) * len(OUT_PLACE),
        scratch_shapes=list(block_scratch().values()),
        compiler_params=pltpu.CompilerParams(
            collective_id=0, has_side_effects=True, vmem_limit_bytes=VMEM_BYTES
        ),
    )(length, *vmem_args, *place_args)


SQUARES = (8, 9, 12, 10, 11, 13, 14, 15)
FINAL_IN = [
    "pieces",
    "block_out",
    "grad_frames",
    "grad_text",
    "gain_sum",
    "conditions",
    "hiddens",
    "vectors",
    "grad_mods",
    "grad_time_outs",
    "grad_time_firsts",
]
FINAL_SHAPES = (
    [((128, D), jnp.bfloat16), ((128, D), jnp.bfloat16), ((16, D), jnp.float32)]
    + [((96, 256), jnp.float32), ((96, D), jnp.float32), ((576, D), jnp.float32)]
    + [((1, 96), jnp.float32), ((D, 384), jnp.float32), ((96, 4 * D), jnp.float32)]
    + [((96, D), jnp.float32)] * 8
)


def final_kernel(*refs):
    r = types.SimpleNamespace(**dict(zip(FINAL_IN, refs)))
    count = len(FINAL_SHAPES)
    rest = refs[len(FINAL_IN) :]
    outs, staged, (turned_mods, turned_small, sems) = rest[:count], rest[count : 2 * count], rest[2 * count :]
    seq = lax.axis_index("seq")

    def put(i, values):
        staged[i][...] = values
        copy(i).start()

    def copy(i):
        return pltpu.make_async_copy(staged[i], outs[i], sems.at[i])

    def whole(p):
        return jnp.concatenate(
            [jnp.concatenate([r.pieces[p, c, h] for h in range(2)], axis=1) for c in range(2)],
            axis=0,
        ).astype(jnp.float32)

    put(7, jnp.transpose(jnp.concatenate([whole(PRODUCTS.index((0, j))) for j in range(4)], axis=0)))
    for j in range(4):
        staged[8][:, j * D : (j + 1) * D] = whole(PRODUCTS.index((1 + j, 4)))
    copy(8).start()
    for j, p in enumerate(SQUARES):
        put(9 + j, whole(p))
    put(0, r.block_out[...])
    put(1, r.grad_frames[...])
    put(2, r.grad_text[...])
    turned_mods[...] = jnp.transpose(r.grad_mods[...].astype(jnp.float32))
    put(
        5,
        product(
            narrow(turned_mods[pl.ds(pl.multiple_of(seq * 576, 64), 576), :]), r.conditions[...]
        ),
    )
    own = pl.ds(pl.multiple_of(seq * 96, 32), 96)
    turned_small[0] = jnp.transpose(r.grad_time_outs[...].astype(jnp.float32))
    put(4, product(narrow(turned_small[0, own, :]), r.hiddens[...]))
    turned_small[1] = jnp.transpose(r.grad_time_firsts[...])
    rows = [r.vectors[b, 0:1].astype(jnp.float32) for b in range(4)]
    vectors = jnp.concatenate(rows + [jnp.zeros((12, 256), jnp.float32)], axis=0)
    put(
        3,
        jnp.dot(
            turned_small[1, own, :],
            vectors,
            precision=lax.Precision.HIGHEST,
            preferred_element_type=jnp.float32,
        ),
    )
    gains = jnp.concatenate([r.gain_sum[...], jnp.zeros((8, D), jnp.float32)], axis=0)
    turned_small[2] = jnp.transpose(gains)
    put(6, jnp.transpose(turned_small[2, own, :])[0:1])
    for i in range(count):
        copy(i).wait()


def finish(values):
    in_vmem = pl.BlockSpec(memory_space=pltpu.VMEM)
    in_place = pl.BlockSpec(memory_space=pl.ANY)
    return pl.pallas_call(
        final_kernel,
        out_shape=tuple(jax.ShapeDtypeStruct(*shape) for shape in FINAL_SHAPES),
        in_specs=[in_vmem] * len(FINAL_IN),
        out_specs=(in_place,) * len(FINAL_SHAPES),
        scratch_shapes=[pltpu.VMEM(*shape) for shape in FINAL_SHAPES]
        + [
            vmem(6 * D, 16, dtype=jnp.float32),
            vmem(3, D, 16, dtype=jnp.float32),
            pltpu.SemaphoreType.DMA((len(FINAL_SHAPES),)),
        ],
        compiler_params=pltpu.CompilerParams(vmem_limit_bytes=VMEM_BYTES),
    )(*values)


def on_device(
    frames,
    text,
    timesteps,
    frame_lengths,
    text_mask,
    cotangent,
    w_time_in,
    w_time_out,
    w_adaln,
    w_query,
    w_key,
    w_value,
    w_attn_out,
    cross_gain,
    w_cross_query,
    w_cross_key,
    w_cross_value,
    w_cross_out,
    w_mlp_in,
    w_mlp_out,
):
    vector = jnp.broadcast_to(narrow(time_embed(timesteps, w_time_in.shape[0])), (16, 256))
    (
        block_out,
        grad_frames,
        grad_text,
        gain_sum,
        conditions,
        hiddens,
        vectors,
        grad_mods,
        grad_time_outs,
        grad_time_firsts,
        pieces,
    ) = block(
        frame_lengths,
        (
            text_mask,
            frames[0],
            cotangent[0],
            text[0],
            cross_gain[None],
            vector,
        ),
        (
            w_attn_out,
            w_cross_query,
            w_cross_key,
            w_cross_value,
            w_cross_out,
            w_mlp_in,
            w_mlp_out,
            w_query,
            w_key,
            w_value,
            w_adaln,
            w_time_out,
            w_time_in,
        ),
    )
    (
        block_out,
        grad_frames,
        grad_text,
        sum_time_in,
        sum_time_out,
        sum_adaln,
        sum_gain,
        sum_mlp_in,
        sum_mlp_out,
        sum_cross_out,
        sum_cross_query,
        sum_attn_out,
        sum_cross_key,
        sum_cross_value,
        sum_query,
        sum_key,
        sum_value,
    ) = finish(
        (
            pieces,
            block_out,
            grad_frames,
            grad_text,
            gain_sum,
            conditions,
            hiddens,
            vectors,
            grad_mods,
            grad_time_outs,
            grad_time_firsts,
        )
    )
    return (
        block_out[None],
        grad_frames[None],
        grad_text[None],
        sum_time_in.T,
        sum_time_out.T,
        sum_adaln.T,
        sum_query.T,
        sum_key.T,
        sum_value.T,
        sum_attn_out.T,
        sum_gain[0],
        sum_cross_query.T,
        sum_cross_key.T,
        sum_cross_value.T,
        sum_cross_out.T,
        sum_mlp_in,
        sum_mlp_out.T,
    )


def on_device_general(
    frames,
    text,
    timesteps,
    frame_lengths,
    text_mask,
    cotangent,
    w_time_in,
    w_time_out,
    w_adaln,
    w_query,
    w_key,
    w_value,
    w_attn_out,
    cross_gain,
    w_cross_query,
    w_cross_key,
    w_cross_value,
    w_cross_out,
    w_mlp_in,
    w_mlp_out,
):
    clips = frames.shape[0]
    rows = frames.shape[1]
    width = frames.shape[2]
    tokens = clips * rows
    text_count = text.shape[1]
    seq_place = lax.axis_index("seq")
    seq_count = lax.axis_size("seq")
    offset = seq_place * rows
    inputs = frames.astype(jnp.float32)
    own_valid = (offset + jnp.arange(rows))[None, :] < frame_lengths[:, None]
    row_valid = own_valid[:, :, None]
    text_valid = text_mask != 0

    def flatten(values):
        return values.reshape(tokens, values.shape[-1])

    def unflatten(values):
        return values.reshape(clips, rows, values.shape[-1])

    time_vector = narrow(time_embed(timesteps, w_time_in.shape[0]))
    time_first = product(time_vector, w_time_in)
    time_hidden = narrow(jax.nn.silu(time_first))
    time_out = product(time_hidden, w_time_out)
    condition = narrow(jax.nn.silu(time_out))
    modulation = product(condition, w_adaln)
    shift_attn, scale_attn, gate_attn, shift_mlp, scale_mlp, gate_mlp = [
        piece[:, None, :] for piece in jnp.split(modulation, 6, axis=1)
    ]
    normed_attn, scaling_attn = layer_norm(inputs)
    attn_in = narrow(normed_attn * (1.0 + scale_attn) + shift_attn)
    attn_flat = flatten(attn_in)
    query_flat = narrow(product(attn_flat, w_query))
    queries = split_heads(unflatten(query_flat))
    kv_local = unflatten(
        jnp.concatenate(
            [narrow(product(attn_flat, w_key)), narrow(product(attn_flat, w_value))], axis=1
        )
    )
    start_state = (
        jnp.full((clips, rows, H), -1e30, jnp.float32),
        jnp.zeros((clips, rows, H), jnp.float32),
        jnp.zeros((clips, rows, H, HD), jnp.float32),
    )
    row_max, row_sum, weighted = forward_piece(
        start_state,
        lax.all_gather(kv_local, "seq", axis=1, tiled=True),
        jnp.int32(0),
        queries,
        frame_lengths,
    )
    attended = weighted / row_sum[..., None]
    log_total = row_max + jnp.log(row_sum)
    attn_low = narrow(attended.reshape(clips, rows, width))
    attn_proj = unflatten(product(flatten(attn_low), w_attn_out))
    middle = inputs + gate_attn * attn_proj
    normed_cross, scaling_cross = layer_norm(middle)
    gain_values = cross_gain.astype(jnp.float32)
    cross_in = narrow(normed_cross * gain_values)
    cross_queries = split_heads(unflatten(narrow(product(flatten(cross_in), w_cross_query))))
    text_flat = text.reshape(clips * text_count, width)
    cross_keys = split_heads(
        narrow(product(text_flat, w_cross_key)).reshape(clips, text_count, width)
    )
    cross_values = split_heads(
        narrow(product(text_flat, w_cross_value)).reshape(clips, text_count, width)
    )
    cross_scores = masked_scores(cross_queries, cross_keys, text_valid)
    cross_max = jnp.max(cross_scores, axis=-1, keepdims=True)
    cross_total = cross_max + jnp.log(
        jnp.sum(jnp.exp(cross_scores - cross_max), axis=-1, keepdims=True)
    )
    cross_probs = jnp.exp(cross_scores - cross_total)
    cross_probs_low = narrow(cross_probs)
    cross_attended = jnp.einsum(
        "cqhk,ckhd->cqhd", cross_probs_low, cross_values, preferred_element_type=jnp.float32
    )
    cross_low = narrow(cross_attended.reshape(clips, rows, width))
    after_cross = middle + unflatten(product(flatten(cross_low), w_cross_out))
    normed_mlp, scaling_mlp = layer_norm(after_cross)
    mlp_in = narrow(normed_mlp * (1.0 + scale_mlp) + shift_mlp)
    pre_act = product(flatten(mlp_in), w_mlp_in)
    activation = narrow(jax.nn.gelu(pre_act, approximate=True))
    mlp_out = unflatten(product(activation, w_mlp_out))
    result = after_cross + gate_mlp * mlp_out
    block_out = jnp.where(row_valid, result, inputs).astype(jnp.bfloat16)
    grad_out = cotangent.astype(jnp.float32)
    grad_res = jnp.where(row_valid, grad_out, 0.0)
    grad_mlp = flatten(narrow(gate_mlp * grad_res))
    grad_w_mlp_out = transposed_left(activation, grad_mlp)
    grad_act = transposed_right(grad_mlp, w_mlp_out)
    gelu_pull = jax.vjp(lambda values: jax.nn.gelu(values, approximate=True), pre_act)[1]
    grad_pre = narrow(gelu_pull(grad_act)[0])
    grad_w_mlp_in = transposed_left(flatten(mlp_in), grad_pre)
    grad_mlp_in = unflatten(transposed_right(grad_pre, w_mlp_in))
    grad_after = grad_res + norm_back(normed_mlp, scaling_mlp, grad_mlp_in * (1.0 + scale_mlp))
    grad_cross_out = flatten(narrow(grad_after))
    grad_w_cross_out = transposed_left(flatten(cross_low), grad_cross_out)
    grad_cross_attn = split_heads(unflatten(narrow(transposed_right(grad_cross_out, w_cross_out))))
    cross_delta = jnp.sum(grad_cross_attn.astype(jnp.float32) * cross_attended, axis=-1)
    cross_grad_probs = jnp.einsum(
        "cqhd,ckhd->cqhk", grad_cross_attn, cross_values, preferred_element_type=jnp.float32
    )
    cross_grad_scores = narrow(cross_probs * (cross_grad_probs - cross_delta[..., None]))
    grad_cross_query = narrow(
        jnp.einsum(
            "cqhk,ckhd->cqhd", cross_grad_scores, cross_keys, preferred_element_type=jnp.float32
        )
        * 0.125
    ).reshape(tokens, width)
    cross_key_part = (
        jnp.einsum(
            "cqhk,cqhd->ckhd", cross_grad_scores, cross_queries, preferred_element_type=jnp.float32
        )
        * 0.125
    )
    cross_value_part = jnp.einsum(
        "cqhk,cqhd->ckhd", cross_probs_low, grad_cross_attn, preferred_element_type=jnp.float32
    )
    cross_kv_part = jnp.concatenate(
        [
            cross_key_part.reshape(clips, text_count, width),
            cross_value_part.reshape(clips, text_count, width),
        ],
        axis=2,
    )
    text_total = lax.psum_scatter(cross_kv_part, "seq", scatter_dimension=1, tiled=True)
    text_share = text_total.shape[1]
    grad_cross_key = narrow(text_total[:, :, :width]).reshape(clips * text_share, width)
    grad_cross_value = narrow(text_total[:, :, width:]).reshape(clips * text_share, width)
    text_own = lax.dynamic_slice_in_dim(text, seq_place * text_share, text_share, 1).reshape(
        clips * text_share, width
    )
    grad_text = (
        transposed_right(grad_cross_key, w_cross_key)
        + transposed_right(grad_cross_value, w_cross_value)
    ).reshape(clips, text_share, width)
    grad_w_cross_key = transposed_left(text_own, grad_cross_key)
    grad_w_cross_value = transposed_left(text_own, grad_cross_value)
    grad_w_cross_query = transposed_left(flatten(cross_in), grad_cross_query)
    grad_cross_in = unflatten(transposed_right(grad_cross_query, w_cross_query))
    grad_gain_part = jnp.sum(grad_cross_in * normed_cross, axis=(0, 1))
    grad_mid = grad_after + norm_back(normed_cross, scaling_cross, grad_cross_in * gain_values)
    grad_attn_proj = flatten(narrow(gate_attn * grad_mid))
    grad_w_attn_out = transposed_left(flatten(attn_low), grad_attn_proj)
    grad_attn_flat = narrow(transposed_right(grad_attn_proj, w_attn_out))
    grad_heads = split_heads(unflatten(grad_attn_flat))
    row_delta = jnp.sum(grad_heads.astype(jnp.float32) * attended, axis=-1)
    zero_heads = jnp.zeros((clips, rows, H, HD), jnp.float32)
    gathered = lax.all_gather(kv_local, "seq", axis=1, tiled=True)
    query_grad = query_piece(
        zero_heads, gathered, 0, queries, grad_heads, log_total, row_delta, frame_lengths
    )
    anchor = jnp.int32(0)
    block_size = math.gcd(rows * lax.axis_size("seq"), key_block)

    def key_one_block(counter):
        rows_in = lax.dynamic_slice_in_dim(gathered, counter * block_size, block_size, 1)
        key_valid = block_valid(anchor, counter * block_size, block_size, frame_lengths)
        scores = masked_scores(queries, split_heads(rows_in[:, :, :width]), key_valid)
        attn_probs = jnp.exp(scores - log_total[..., None])
        grad_probs = jnp.einsum(
            "cqhd,ckhd->cqhk",
            grad_heads,
            split_heads(rows_in[:, :, width:]),
            preferred_element_type=jnp.float32,
        )
        grad_scores = narrow(attn_probs * (grad_probs - row_delta[..., None]))
        grad_keys = (
            jnp.einsum("cqhk,cqhd->ckhd", grad_scores, queries, preferred_element_type=jnp.float32)
            * 0.125
        )
        grad_values = jnp.einsum(
            "cqhk,cqhd->ckhd", narrow(attn_probs), grad_heads, preferred_element_type=jnp.float32
        )
        joined = jnp.concatenate(
            [
                grad_keys.reshape(clips, block_size, width),
                grad_values.reshape(clips, block_size, width),
            ],
            axis=2,
        )
        return jnp.transpose(joined, (1, 0, 2))

    blocks = lax.map(key_one_block, jnp.arange(rows * lax.axis_size("seq") // block_size))
    kv_term = lax.psum_scatter(
        blocks.reshape(rows * lax.axis_size("seq"), clips, 2 * width),
        "seq",
        scatter_dimension=0,
        tiled=True,
    )
    kv_grad = jnp.transpose(kv_term, (1, 0, 2))
    grad_query = narrow(query_grad.reshape(tokens, width))
    grad_key = flatten(narrow(kv_grad[:, :, :width]))
    grad_value = flatten(narrow(kv_grad[:, :, width:]))
    grad_w_query = transposed_left(attn_flat, grad_query)
    grad_w_key = transposed_left(attn_flat, grad_key)
    grad_w_value = transposed_left(attn_flat, grad_value)
    grad_attn_in = unflatten(
        transposed_right(grad_query, w_query)
        + transposed_right(grad_key, w_key)
        + transposed_right(grad_value, w_value)
    )
    grad_inputs = grad_mid + norm_back(normed_attn, scaling_attn, grad_attn_in * (1.0 + scale_attn))
    grad_frames = jnp.where(row_valid, grad_inputs, grad_out).astype(jnp.bfloat16)
    modulation_part = jnp.concatenate(
        [
            jnp.sum(grad_attn_in, axis=1),
            jnp.sum(grad_attn_in * normed_attn, axis=1),
            jnp.sum(grad_mid * attn_proj, axis=1),
            jnp.sum(grad_mlp_in, axis=1),
            jnp.sum(grad_mlp_in * normed_mlp, axis=1),
            jnp.sum(grad_res * mlp_out, axis=1),
        ],
        axis=1,
    )
    modulation_total = lax.psum(modulation_part, "seq")
    grad_modulation = narrow(modulation_total)
    grad_w_adaln = transposed_left(condition, grad_modulation)
    grad_condition = transposed_right(grad_modulation, w_adaln)
    grad_time_out = narrow(jax.vjp(jax.nn.silu, time_out)[1](grad_condition)[0])
    grad_w_time_out = transposed_left(time_hidden, grad_time_out)
    grad_time_hidden = transposed_right(grad_time_out, w_time_out)
    grad_time_first = jax.vjp(jax.nn.silu, time_first)[1](grad_time_hidden)[0]
    grad_w_time_in = lax.dot_general(
        time_vector.astype(jnp.float32),
        grad_time_first,
        (((0,), (0,)), ((), ())),
        precision=lax.Precision.HIGHEST,
    )
    shared = (
        lax.psum_scatter(grad_w_query, "seq", scatter_dimension=1, tiled=True),
        lax.psum_scatter(grad_w_key, "seq", scatter_dimension=1, tiled=True),
        lax.psum_scatter(grad_w_value, "seq", scatter_dimension=1, tiled=True),
        lax.psum_scatter(grad_w_attn_out, "seq", scatter_dimension=1, tiled=True),
        lax.psum_scatter(grad_gain_part, "seq", scatter_dimension=0, tiled=True),
        lax.psum_scatter(grad_w_cross_query, "seq", scatter_dimension=1, tiled=True),
        lax.psum_scatter(grad_w_cross_key, "seq", scatter_dimension=1, tiled=True),
        lax.psum_scatter(grad_w_cross_value, "seq", scatter_dimension=1, tiled=True),
        lax.psum_scatter(grad_w_cross_out, "seq", scatter_dimension=1, tiled=True),
        lax.psum_scatter(grad_w_mlp_in, "seq", scatter_dimension=1, tiled=True),
        lax.psum_scatter(grad_w_mlp_out, "seq", scatter_dimension=1, tiled=True),
    )
    replicated = (
        own_columns(grad_w_time_in, seq_place, seq_count),
        own_columns(grad_w_time_out, seq_place, seq_count),
        own_columns(grad_w_adaln, seq_place, seq_count),
    )
    summed = jax.tree.map(
        lambda part: part.astype(jnp.float32), lax.psum(for_sending(shared + replicated), "band")
    )
    (
        sum_query,
        sum_key,
        sum_value,
        sum_attn_out,
        sum_gain,
        sum_cross_query,
        sum_cross_key,
        sum_cross_value,
        sum_cross_out,
        sum_mlp_in,
        sum_mlp_out,
        sum_time_in,
        sum_time_out,
        sum_adaln,
    ) = summed
    return (
        block_out,
        grad_frames,
        grad_text,
        sum_time_in,
        sum_time_out,
        sum_adaln,
        sum_query,
        sum_key,
        sum_value,
        sum_attn_out,
        sum_gain,
        sum_cross_query,
        sum_cross_key,
        sum_cross_value,
        sum_cross_out,
        sum_mlp_in,
        sum_mlp_out,
    )


def solution(mesh):
    placed = (
        P("band", "seq", None),
        P("band", None, None),
        P("band"),
        P("band"),
        P("band", None),
        P("band", "seq", None),
        P(),
        P(),
        P(),
        P(),
        P(),
        P(),
        P(),
        P(),
        P(),
        P(),
        P(),
        P(),
        P(),
        P(),
    )
    paired = mesh.shape["band"] == 4 and mesh.shape["seq"] == 8
    return jax.shard_map(
        on_device if paired else on_device_general,
        mesh=mesh,
        in_specs=placed,
        out_specs=(
            P("band", "seq", None),
            P("band", "seq", None),
            P("band", "seq", None),
            P(None, "seq"),
            P(None, "seq"),
            P(None, "seq"),
            P(None, "seq"),
            P(None, "seq"),
            P(None, "seq"),
            P(None, "seq"),
            P("seq"),
            P(None, "seq"),
            P(None, "seq"),
            P(None, "seq"),
            P(None, "seq"),
            P(None, "seq"),
            P(None, "seq"),
        ),
        check_vma=False,
    )
```
